32 devices in a mesh: dp: 8 (over y, x, core), mp: 4 (over z).
Axes of the slice: x: 2, y: 2, z: 4, core: 2. Of those that a mesh axis runs over, the one named last changes fastest.
Arguments:
- target_ids: int32 [16, 1024], P('dp', 'mp'), may hold values from 0 to 131071
- tgt_lengths: int32 [16], P('dp'), may hold values from 1 to 1024, 12288 in all
- encoder_states: bfloat16 [16, 1024, 1024], P('dp', 'mp'), may hold values from -6 to 6
- src_lengths: int32 [16], P('dp'), may hold values from 1 to 1024, 12288 in all
- table: bfloat16 [1024, 131072], P(('dp', 'mp')), may hold values from -0.1875 to 0.1875
- pos_table: bfloat16 [1024, 1024], P('dp', 'mp'), may hold values from -3 to 3
- self_query_key_value_weight: bfloat16 [1024, 3, 1024], P('dp', None, 'mp'), may hold values from -0.1875 to 0.1875
- self_output_weight: bfloat16 [1024, 1024], P('dp', 'mp'), may hold values from -0.75 to 0.75
- cross_query_weight: bfloat16 [1024, 1024], P('dp', 'mp'), may hold values from -0.1875 to 0.1875
- cross_key_value_weight: bfloat16 [1024, 2, 1024], P('dp', None, 'mp'), may hold values from -0.1875 to 0.1875
- cross_output_weight: bfloat16 [1024, 1024], P('dp', 'mp'), may hold values from -0.75 to 0.75
- feedforward_input_weight: bfloat16 [1024, 4096], P('dp', 'mp'), may hold values from -0.1875 to 0.1875
- feedforward_output_weight: bfloat16 [1024, 4096], P('dp', 'mp'), may hold values from -0.09375 to 0.09375
- norm_gains: float32 [5, 1024], replicated, may hold values from 0.5 to 1.5
- norm_biases: float32 [5, 1024], replicated, may hold values from -1.25 to 1.25
- out_grad: float32 [16, 1024, 1024], P('dp', 'mp'), may hold values from -6 to 6
Outputs:
- hidden_out: float32 [16, 1024, 1024], P('dp', 'mp')
- table_grad: float32 [1024, 131072], P(('dp', 'mp'))
- pos_grad: float32 [1024, 1024], P('dp', 'mp')
- self_qkv_grad: float32 [1024, 3, 1024], P('dp', None, 'mp')
- self_out_grad: float32 [1024, 1024], P('dp', 'mp')
- cross_q_grad: float32 [1024, 1024], P('dp', 'mp')
- cross_kv_grad: float32 [1024, 2, 1024], P('dp', None, 'mp')
- cross_out_grad: float32 [1024, 1024], P('dp', 'mp')
- ffn_in_grad: float32 [1024, 4096], P('dp', 'mp')
- ffn_out_grad: float32 [1024, 4096], P('dp', 'mp')
- gains_grad: float32 [5, 1024], replicated
- biases_grad: float32 [5, 1024], replicated
- encoder_grad: float32 [16, 1024, 1024], P('dp', 'mp')
The draws below stay inside these ranges and needn't reach their ends.
Inputs may be any that keep to these rules, and one draw needn't show every extreme that they name: `tgt_lengths`: some target sequence has all 1024 tokens. `src_lengths`: some source sequence has all 1024 tokens.
All inputs are finite; a program needn't handle non-finite values. No bound on the sum of `tgt_lengths` or of `src_lengths` on one device may be relied on, other than what follows from the above.
Results may differ from the reference program's by a relative error of at most 0.02.
Values may be sent and summed in bfloat16 or wider, within the bound.
No kernel may reach another device: no remote copies, remote signals or barrier semaphores. Data moves between devices by JAX's collectives and lax.ppermute only.
A program may use at most 256 MiB of HBM per device.

```python
import math
from functools import partial
import jax
import jax.numpy as jnp
import numpy as np
from jax import lax

D = 1024
HEAD_DIM = 64
FF = 4096
VOCAB = 131072
LEN = 1024
SEQS = 16


def set_ends(drawn, stream_key, smallest, high):
    dims = drawn.shape
    spot = [jax.random.randint(jax.random.fold_in(stream_key, axis), (), 0, dims[axis]) for axis in range(len(dims))]
    drawn = drawn.at[tuple(spot)].set(smallest)
    longest = dims.index(max(dims))
    spot[longest] = (spot[longest] + 1) % dims[longest]
    return drawn.at[tuple(spot)].set(high)


def shard_levels(key, dims, cuts, low, top_value):
    gain, own = 1.0, jax.random.fold_in(key, 6)
    for position, parts in cuts:
        heights = jnp.exp(jax.random.uniform(jax.random.fold_in(own, position), (parts,), jnp.float32, low / len(cuts), top_value / len(cuts)))
        gain = gain * jnp.repeat(heights, dims[position] // parts).reshape([-1 if axis == position else 1 for axis in range(len(dims))])
    return gain


def skewed_wide(own_key, extent, count, lean):
    portions = [min(1 << octave, count + 1 - (1 << octave)) * (1 << 20) // math.isqrt((1 << octave) ** lean) + 1 for octave in range((count + 1).bit_length()) if 1 << octave <= count]
    spread = 1 + sum(portions) // (1 << 30)
    listing = np.cumsum(np.array([max(1, weight // spread) for weight in portions]))
    pick = jax.random.randint(jax.random.fold_in(own_key, 1), extent, 0, int(listing[len(portions) - 1]))
    start = jnp.left_shift(1, jnp.searchsorted(jnp.asarray(listing, jnp.int32), pick, side="right").astype(jnp.int32))
    rank = start - 1 + jax.random.randint(jax.random.fold_in(own_key, 4), extent, 0, 1 << 30) % jnp.minimum(start, count + 1 - start)
    return jax.random.permutation(jax.random.fold_in(own_key, 2), count)[rank].astype(jnp.int32)


def profile(count, total, reach, slope):
    loads = [(1 << 20) // math.isqrt(grade ** slope) + 1 for grade in range(2, count + 1)]
    rest, given = total - reach - (count - 1), [1] * (count - 1)
    while rest > 0:
        candidates = [i for i in range(count - 1) if given[i] < reach]
        whole, left = sum([loads[i] for i in candidates]), rest
        for i in candidates:
            more = min(reach - given[i], max(1, left * loads[i] // whole), rest)
            given[i] = given[i] + more
            rest = rest - more
    return np.array([reach] + given)


def uneven(rng, amount, total, limit, lean):
    if amount == 2:
        one = jax.random.randint(rng, (), max(1, total - limit), min(limit, total - 1) + 1)
        return jnp.stack([one, total - one])
    sizes = jnp.asarray(profile(amount, total, limit, lean), jnp.int32)
    twos = (amount - 1) // 2
    giver, receiver = sizes[1:1 + 2 * twos:2], sizes[2:2 + 2 * twos:2]
    margin = jnp.minimum(giver - 1, limit - receiver)
    passed = jax.random.randint(jax.random.fold_in(rng, 1), (twos,), 0, 1 << 20) % (margin + 1)
    sizes = sizes.at[1:1 + 2 * twos:2].set(giver - passed).at[2:2 + 2 * twos:2].set(receiver + passed)
    return sizes[jax.random.permutation(jax.random.fold_in(rng, 2), amount)]


def bell_draw(own_key, dims, deviation, bound, shards=(), held_as=jnp.bfloat16):
    level = shard_levels(own_key, dims, shards, -0.22, 0.18) if shards else 1.0
    array = jax.random.normal(own_key, dims, jnp.float32) * deviation * level
    return jnp.minimum(jnp.maximum(array, -bound), bound).astype(held_as)


def setup_inputs(seed: int = 0) -> dict:
    splits = jax.random.split(jax.random.key(seed), 17)
    target_ids = set_ends(skewed_wide(splits[0], (SEQS, LEN), VOCAB, 2), jax.random.fold_in(splits[0], 3), 0, VOCAB - 1).astype(jnp.int32)
    tgt_lengths = uneven(splits[1], SEQS, SEQS * LEN * 3 // 4, LEN, 0).astype(jnp.int32)
    encoder_states = bell_draw(splits[2], (SEQS, LEN, D), 1.0, 6.0, ((0, 8), (1, 4)))
    src_lengths = uneven(splits[3], SEQS, SEQS * LEN * 3 // 4, LEN, 0).astype(jnp.int32)
    table = bell_draw(splits[4], (D, VOCAB), 0.03125, 0.1875, ((0, 32),))
    pos_table = bell_draw(splits[5], (D, LEN), 0.5, 3.0, ((0, 8), (1, 4)))
    self_query_key_value_weight = bell_draw(splits[6], (D, 3, D), D ** -0.5, 0.1875, ((0, 8), (2, 4)))
    self_output_weight = bell_draw(splits[7], (D, D), (D // 16) ** -0.5, 0.75, ((0, 8), (1, 4)))
    cross_query_weight = bell_draw(splits[8], (D, D), D ** -0.5, 0.1875, ((0, 8), (1, 4)))
    cross_key_value_weight = bell_draw(splits[9], (D, 2, D), D ** -0.5, 0.1875, ((0, 8), (2, 4)))
    cross_output_weight = bell_draw(splits[10], (D, D), (D // 16) ** -0.5, 0.75, ((0, 8), (1, 4)))
    feedforward_input_weight = bell_draw(splits[11], (D, FF), D ** -0.5, 0.1875, ((0, 8), (1, 4)))
    feedforward_output_weight = bell_draw(splits[12], (D, FF), FF ** -0.5, 0.09375, ((0, 8), (1, 4)))
    norm_gains = jnp.clip(1.0 + 0.1 * jax.random.normal(splits[13], (5, D), jnp.float32), 0.5, 1.5)
    norm_biases = bell_draw(splits[14], (5, D), 0.2, 1.25, (), jnp.float32)
    out_grad = bell_draw(splits[15], (SEQS, LEN, D), 1.0, 6.0, ((0, 8), (1, 4)), jnp.float32)
    return {"target_ids": target_ids, "tgt_lengths": tgt_lengths, "encoder_states": encoder_states, "src_lengths": src_lengths, "table": table, "pos_table": pos_table, "self_query_key_value_weight": self_query_key_value_weight, "self_output_weight": self_output_weight, "cross_query_weight": cross_query_weight, "cross_key_value_weight": cross_key_value_weight, "cross_output_weight": cross_output_weight, "feedforward_input_weight": feedforward_input_weight, "feedforward_output_weight": feedforward_output_weight, "norm_gains": norm_gains, "norm_biases": norm_biases, "out_grad": out_grad}


MATMUL_ACCURACY = lax.Precision.HIGHEST
EPSILON = 1e-05
NEGATIVE = -1e+30

@jax.custom_vjp
def reduced_precision(v):
    return lax.optimization_barrier(v.astype(jnp.bfloat16)).astype(jnp.float32)

@jax.custom_vjp
def reduced_precision_reverse(v):
    return v

def low_keep(v):
    return (reduced_precision(v), None)

def low_pass(kept, grad):
    return (grad,)

def back_keep(v):
    return (v, None)

def back_low(kept, grad):
    return (reduced_precision(grad),)
reduced_precision.defvjp(low_keep, low_pass)
reduced_precision_reverse.defvjp(back_keep, back_low)

def layer_norm(values, gains, shifts):
    average = lax.optimization_barrier(jnp.mean(values, axis=-1, keepdims=True))
    centred = values - average
    variance = lax.optimization_barrier(jnp.mean(centred * centred, axis=-1, keepdims=True))
    return centred * lax.rsqrt(variance + EPSILON) * gains + shifts

def split_heads(values):
    return values.reshape(values.shape[:2] + (values.shape[2] // HEAD_DIM, HEAD_DIM))

def attend_seq(queries, keys, values, length, causal):
    scores = jnp.einsum('qhd,khd->hqk', queries, keys, precision=MATMUL_ACCURACY) * HEAD_DIM ** (-0.5)
    scores = reduced_precision_reverse(scores)
    key_pos = jnp.arange(keys.shape[0], dtype=jnp.int32)
    allowed = key_pos[None, None, :] < length
    if causal:
        query_pos = jnp.arange(queries.shape[0], dtype=jnp.int32)
        allowed = allowed & (key_pos[None, None, :] <= query_pos[None, :, None])
    probs = jax.nn.softmax(jnp.where(allowed, scores, NEGATIVE), axis=-1)
    return jnp.einsum('hqk,khd->qhd', reduced_precision(probs), values, precision=MATMUL_ACCURACY)

def self_seq(inputs):
    queries, keys, values, length = inputs
    return attend_seq(queries, keys, values, length, True)

def cross_seq(inputs):
    queries, keys, values, length = inputs
    return attend_seq(queries, keys, values, length, False)

def forward(target_ids, tgt_lengths, src_lengths, table, pos_table, self_query_key_value_weight, self_output_weight, cross_query_weight, cross_key_value_weight, cross_output_weight, feedforward_input_weight, feedforward_output_weight, norm_gains, norm_biases, encoder_states):
    seq_count = target_ids.shape[0]
    picked = jnp.moveaxis(jnp.take(table, target_ids, axis=1), 0, -1)
    state_zero = picked * 32.0 + pos_table.T[None]
    hidden_state_one = layer_norm(state_zero, norm_gains[0], norm_biases[0])
    self_normalized = reduced_precision(layer_norm(hidden_state_one, norm_gains[1], norm_biases[1]))
    projected_rows = reduced_precision_reverse(reduced_precision(jnp.einsum('uvb,bqn->uvqn', self_normalized, self_query_key_value_weight, precision=MATMUL_ACCURACY)))
    self_attended = lax.map(jax.checkpoint(self_seq), (split_heads(projected_rows[:, :, 0]), split_heads(projected_rows[:, :, 1]), split_heads(projected_rows[:, :, 2]), tgt_lengths))
    self_attended = reduced_precision_reverse(reduced_precision(self_attended.reshape(seq_count, LEN, D)))
    hidden_state_two = hidden_state_one + reduced_precision_reverse(jnp.einsum('zvr,nr->zvn', self_attended, self_output_weight, precision=MATMUL_ACCURACY))
    cross_normalized = reduced_precision(layer_norm(hidden_state_two, norm_gains[2], norm_biases[2]))
    cross_query_rows = reduced_precision_reverse(reduced_precision(jnp.einsum('hzc,cv->hzv', cross_normalized, cross_query_weight, precision=MATMUL_ACCURACY)))
    source_key_value = reduced_precision_reverse(reduced_precision(jnp.einsum('uvb,bqn->uvqn', encoder_states, cross_key_value_weight, precision=MATMUL_ACCURACY)))
    cross_attended = lax.map(jax.checkpoint(cross_seq), (split_heads(cross_query_rows), split_heads(source_key_value[:, :, 0]), split_heads(source_key_value[:, :, 1]), src_lengths))
    cross_attended = reduced_precision_reverse(reduced_precision(cross_attended.reshape(seq_count, LEN, D)))
    hidden_state_three = hidden_state_two + reduced_precision_reverse(jnp.einsum('zvr,nr->zvn', cross_attended, cross_output_weight, precision=MATMUL_ACCURACY))
    feedforward_normalized = reduced_precision(layer_norm(hidden_state_three, norm_gains[3], norm_biases[3]))
    preactivation = reduced_precision_reverse(jnp.einsum('rqo,og->rqg', feedforward_normalized, feedforward_input_weight, precision=MATMUL_ACCURACY))
    activation_rows = reduced_precision(jax.nn.gelu(preactivation, approximate=False))
    hidden_state_four = hidden_state_three + reduced_precision_reverse(jnp.einsum('hbc,nc->hbn', activation_rows, feedforward_output_weight, precision=MATMUL_ACCURACY))
    return layer_norm(hidden_state_four, norm_gains[4], norm_biases[4])

def reference(target_ids, tgt_lengths, encoder_states, src_lengths, table, pos_table, self_query_key_value_weight, self_output_weight, cross_query_weight, cross_key_value_weight, cross_output_weight, feedforward_input_weight, feedforward_output_weight, norm_gains, norm_biases, out_grad):
    floats = tuple((item.astype(jnp.float32) for item in (table, pos_table, self_query_key_value_weight, self_output_weight, cross_query_weight, cross_key_value_weight, cross_output_weight, feedforward_input_weight, feedforward_output_weight, norm_gains, norm_biases, encoder_states)))
    hidden_out, pullback = jax.vjp(partial(forward, target_ids, tgt_lengths, src_lengths), *floats)
    grads = pullback(out_grad.astype(jnp.float32))
    return (hidden_out, grads[0], grads[1], grads[2], grads[3], grads[4], grads[5], grads[6], grads[7], grads[8], grads[9], grads[10], grads[11])
```

```python
import functools

import jax
import jax.numpy as jnp
from jax import lax
from jax.experimental import pallas as pl
from jax.experimental.pallas import tpu as pltpu
from jax.sharding import Mesh
from jax.sharding import PartitionSpec as P

HEAD_DIM = 64
EPSILON = 1e-05
NEGATIVE = -1e30
LANES = 128
ALL = ("chip", "core", "mp")
LINE = ("core", "mp")
CORES = 2

f32 = jnp.float32
bf16 = jnp.bfloat16
i32 = jnp.int32

NT = (((1,), (1,)), ((), ()))
NN = (((1,), (0,)), ((), ()))
TN = (((0,), (0,)), ((), ()))


def dot(a, b, dims=NN):
    return lax.dot_general(a, b, dims, preferred_element_type=f32)


def params(mib=56):
    return pltpu.CompilerParams(vmem_limit_bytes=mib << 20)


def cost(flops, moved, trans=0):
    return pl.CostEstimate(flops=int(flops), bytes_accessed=int(moved), transcendentals=int(trans))


def normed(values):
    centred = values - jnp.mean(values, axis=-1, keepdims=True)
    inverse = lax.rsqrt(jnp.mean(centred * centred, axis=-1, keepdims=True) + EPSILON)
    return centred * inverse, inverse


def norm_back(values, gain, grad):
    hat, inverse = normed(values)
    scaled = grad * gain
    first = jnp.mean(scaled, axis=-1, keepdims=True)
    second = jnp.mean(scaled * hat, axis=-1, keepdims=True)
    back = inverse * (scaled - first - hat * second)
    gain_grad = jnp.sum(grad * hat, axis=0, keepdims=True)
    bias_grad = jnp.sum(grad, axis=0, keepdims=True)
    return back, gain_grad, bias_grad


def columns(w_ref, m):
    block = w_ref[:, pl.ds(m, 1)]
    return block.reshape(block.shape[0] * block.shape[3], block.shape[4])


def whole_weight(w_ref):
    parts = [columns(w_ref, m) for m in range(w_ref.shape[1])]
    return jnp.concatenate(parts, axis=1)


def project(x, w_ref, store):
    width = w_ref.shape[4]

    def step(m, carry):
        store(pl.multiple_of(m * width, width), dot(x, columns(w_ref, m)))
        return carry

    lax.fori_loop(0, w_ref.shape[1], step, 0)


def weight_spec(weights, index):
    shape = weights.shape
    return pl.BlockSpec(
        (shape[0], shape[1], 1, shape[3], shape[4]), lambda *a: (0, 0, index(a[0]), 0, 0)
    )


def full(shape):
    return pl.BlockSpec(shape, lambda *a: (0,) * len(shape))


def gather_kernel(groups, fill, rows_ref, group_ref, *refs):
    tables, out_ref, turned, picked = refs[:groups], refs[groups], refs[-2], refs[-1]
    step = pl.program_id(0)
    feats, width = tables[0].shape
    tokens = picked.shape[0]

    @pl.when(step < fill)
    def _():
        stacked = jnp.concatenate([t[...].astype(f32) for t in tables], axis=0).astype(bf16)
        row = lax.broadcasted_iota(i32, (256, 256), 0)
        eye = jnp.where(row == lax.broadcasted_iota(i32, (256, 256), 1), 1.0, 0.0).astype(bf16)
        for k in range(width // 256):
            at = pl.multiple_of(step * width + k * 256, 256)
            turned[pl.ds(at, 256), :] = dot(eye, stacked[:, k * 256 : (k + 1) * 256], NT)

    @pl.when(step >= fill)
    def _():
        base = (step - fill) * tokens

        def some(k, carry):
            for u in range(16):
                t = k * 16 + u
                picked[pl.ds(t, 1), :] = turned[pl.ds(rows_ref[base + t], 1), :]
            return carry

        lax.fori_loop(0, tokens // 16, some, 0)
        row = lax.broadcasted_iota(i32, (LANES, LANES), 0)
        eye = jnp.where(row == lax.broadcasted_iota(i32, (LANES, LANES), 1), 1.0, 0.0)
        across = dot(eye.astype(bf16), picked[...].astype(bf16), NT)
        own = lax.broadcasted_iota(i32, (LANES, tokens), 0) // feats == group_ref[0]
        kept = jnp.where(own, across, 0.0)
        total = kept[:feats]
        for g in range(1, groups):
            total = total + kept[g * feats : (g + 1) * feats]
        out_ref[0] = total.astype(out_ref.dtype)


def gather_tokens(table, rows, group):
    feats, vocab = table.shape
    groups = LANES // feats
    height = vocab // groups
    n, _, tokens = group.shape
    width = min(2048, height)
    fill = height // width

    def table_spec(g):
        return pl.BlockSpec(
            (feats, width), lambda s, r, g=g: (0, g * fill + jnp.minimum(s, fill - 1))
        )

    return pl.pallas_call(
        functools.partial(gather_kernel, groups, fill),
        out_shape=jax.ShapeDtypeStruct((n, feats, tokens), bf16),
        grid_spec=pltpu.PrefetchScalarGridSpec(
            num_scalar_prefetch=1,
            grid=(fill + n,),
            in_specs=[pl.BlockSpec((1, 1, tokens), lambda s, r: (jnp.maximum(s - fill, 0), 0, 0))]
            + [table_spec(g) for g in range(groups)],
            out_specs=pl.BlockSpec(
                (1, feats, tokens), lambda s, r: (jnp.maximum(s - fill, 0), 0, 0)
            ),
            scratch_shapes=[pltpu.VMEM((height, LANES), f32), pltpu.VMEM((tokens, LANES), f32)],
        ),
        compiler_params=params(),
        cost_estimate=cost(4 * vocab * LANES * 64, 2 * feats * vocab + 400 * n * tokens),
        name="gather_tokens",
    )(rows, group, *([table] * groups))


BATCH = 16


def scatter_kernel(
    groups, per_core, rows_ref, row_ref, group_ref, grad_ref, out_ref, pos_ref, acc, update, turned, sem
):
    step = pl.program_id(0)
    feats, tokens = grad_ref.shape[1:]
    height = acc.shape[0]
    width = turned.shape[2]

    @pl.when(step == 0)
    def _():
        def clear(k, carry):
            acc[pl.ds(pl.multiple_of(k * 256, 256), 256), :] = jnp.zeros((256, LANES), f32)
            return carry

        lax.fori_loop(0, height // 256, clear, 0)
        pos_ref[...] = jnp.zeros_like(pos_ref)

    grads = grad_ref[0].astype(f32)
    core = lax.rem(lax.div(step, per_core), CORES)
    pos_ref[core] += grads
    tall = jnp.concatenate([grads] * groups, axis=0)
    own = lax.broadcasted_iota(i32, (LANES, tokens), 0) // feats == group_ref[0]
    tall = jnp.where(own, tall, 0.0).astype(bf16)
    row = lax.broadcasted_iota(i32, (LANES, LANES), 0)
    col = lax.broadcasted_iota(i32, (LANES, LANES), 1)
    near = row // BATCH == col // BATCH
    for b in range(tokens // LANES):
        at = slice(b * LANES, (b + 1) * LANES)
        along = jnp.broadcast_to(row_ref[0][:, at].astype(f32), (LANES, LANES))
        same = jnp.where((along == along.T) & near, 1.0, 0.0).astype(bf16)
        update[at, :] = dot(same, tall[:, at], NT)
    base = step * tokens

    def some(k, carry):
        where = [rows_ref[base + k * BATCH + u] for u in range(BATCH)]
        fresh = [
            acc[pl.ds(where[u], 1), :] + update[pl.ds(k * BATCH + u, 1), :] for u in range(BATCH)
        ]
        for u in range(BATCH):
            acc[pl.ds(where[u], 1), :] = fresh[u]
        return carry

    lax.fori_loop(0, tokens // BATCH, some, 0)

    @pl.when(step == pl.num_programs(0) - 1)
    def _():
        def copy(i, slot, g):
            at = pl.multiple_of(g * height + i * width, width)
            return pltpu.make_async_copy(
                turned.at[slot, pl.ds(g * feats, feats)],
                out_ref.at[:, pl.ds(at, width)],
                sem.at[slot, g],
            )

        def turn(i, carry):
            slot = lax.rem(i, 2)

            @pl.when(i >= 2)
            def _():
                for g in range(groups):
                    copy(i - 2, slot, g).wait()

            at = pl.multiple_of(i * width, width)
            turned[slot] = (acc[pl.ds(at, width), :] * 32.0).T
            for g in range(groups):
                copy(i, slot, g).start()
            return carry

        count = height // width
        lax.fori_loop(0, count, turn, 0)
        for i in range(max(count - 2, 0), count):
            for g in range(groups):
                copy(i, i % 2, g).wait()


def scatter_tokens(grads, rows, row, group, vocab, per_core):
    n, feats, tokens = grads.shape
    groups = LANES // feats
    height = vocab // groups
    width = min(1024, height)
    token_spec = pl.BlockSpec((1, 1, tokens), lambda s, r: (s, 0, 0))
    return pl.pallas_call(
        functools.partial(scatter_kernel, groups, per_core),
        out_shape=(
            jax.ShapeDtypeStruct((feats, vocab), f32),
            jax.ShapeDtypeStruct((CORES, feats, tokens), f32),
        ),
        grid_spec=pltpu.PrefetchScalarGridSpec(
            num_scalar_prefetch=1,
            grid=(n,),
            in_specs=[
                token_spec,
                token_spec,
                pl.BlockSpec((1, feats, tokens), lambda s, r: (s, 0, 0)),
            ],
            out_specs=(
                pl.BlockSpec(memory_space=pl.ANY),
                full((CORES, feats, tokens)),
            ),
            scratch_shapes=[
                pltpu.VMEM((height, LANES), f32),
                pltpu.VMEM((tokens, LANES), f32),
                pltpu.VMEM((2, LANES, width), f32),
                pltpu.SemaphoreType.DMA((2, groups)),
            ],
        ),
        compiler_params=params(),
        cost_estimate=cost(n * tokens * LANES * 256, 4 * feats * vocab + 1000 * n * tokens),
        name="scatter_tokens",
    )(rows, row, group, grads)


def entry_kernel(
    info_ref, emb_ref, pos_a, pos_b, w_ref, gain_ref, bias_ref, x0_ref, x1_ref, a_ref, q_ref, kv_ref
):
    step = pl.program_id(0)
    half = x0_ref.shape[0] // 2

    @pl.when(step == 0)
    def _():
        for i, pos in enumerate((pos_a, pos_b)):
            at = slice(i * half, (i + 1) * half)
            places = pos[...].reshape(pos.shape[0] * pos.shape[3], pos.shape[4])
            x0 = (emb_ref[:, at].astype(f32) * 32.0 + places.astype(f32)).T
            x1 = normed(x0)[0] * gain_ref[0:1] + bias_ref[0:1]
            a = normed(x1)[0] * gain_ref[1:2] + bias_ref[1:2]
            x0_ref[at] = x0
            x1_ref[at] = x1
            a_ref[at] = a.astype(bf16)

    x = a_ref[...]

    @pl.when(step == 0)
    def _():
        def store(at, y):
            q_ref[0, :, pl.ds(at, w_ref.shape[4])] = (y * HEAD_DIM**-0.5).astype(bf16)

        project(x, w_ref, store)

    @pl.when(step > 0)
    def _():
        def store(at, y):
            kv_ref[0, :, pl.ds(at, w_ref.shape[4])] = y.astype(bf16)

        project(x, w_ref, store)


def entry(info, emb, first, gains, biases):
    width, tokens = emb.shape
    half = tokens // 2
    shape = first.shape

    def pos_spec(i):
        return pl.BlockSpec(
            (shape[0], 1, 1, shape[3], shape[4]), lambda s, info, i=i: (0, info[3 + i], 0, 0, 0)
        )

    rows = jax.ShapeDtypeStruct((tokens, width), f32)
    return pl.pallas_call(
        entry_kernel,
        out_shape=(
            rows,
            rows,
            jax.ShapeDtypeStruct((tokens, width), bf16),
            jax.ShapeDtypeStruct((1, tokens, width), bf16),
            jax.ShapeDtypeStruct((2, tokens, width), bf16),
        ),
        grid_spec=pltpu.PrefetchScalarGridSpec(
            num_scalar_prefetch=1,
            grid=(3,),
            in_specs=[
                full(emb.shape),
                pos_spec(0),
                pos_spec(1),
                weight_spec(first, lambda s: s + 1),
                full(gains.shape),
                full(biases.shape),
            ],
            out_specs=(
                full((tokens, width)),
                full((tokens, width)),
                full((tokens, width)),
                full((1, tokens, width)),
                pl.BlockSpec((1, tokens, width), lambda s, info: (jnp.maximum(s - 1, 0), 0, 0)),
            ),
        ),
        compiler_params=params(),
        cost_estimate=cost(6 * tokens * width * width, 20 * tokens * width + 6 * width * width),
        name="entry",
    )(info, emb, first, first, first, gains, biases)


def source_kernel(x_ref, w_ref, kv_ref):
    def store(at, y):
        kv_ref[0, :, pl.ds(at, w_ref.shape[4])] = y.astype(bf16)

    project(x_ref[...], w_ref, store)


def source_keys(states, second):
    tokens, width = states.shape
    return pl.pallas_call(
        source_kernel,
        out_shape=jax.ShapeDtypeStruct((2, tokens, width), bf16),
        grid=(2,),
        in_specs=[full(states.shape), weight_spec(second, lambda s: s + 2)],
        out_specs=pl.BlockSpec((1, tokens, width), lambda s: (s, 0, 0)),
        compiler_params=params(),
        cost_estimate=cost(4 * tokens * width * width, 6 * tokens * width + 4 * width * width),
        name="source_keys",
    )(states, second)


def attend_kernel(causal, info_ref, q_ref, own_ref, par_ref, o_ref, p_ref, hide):
    tokens = q_ref.shape[1]
    half = tokens // 2
    core = info_ref[0]

    @pl.when(pl.program_id(0) == 0)
    def _():
        length = info_ref[1] if causal else info_ref[2]
        key = lax.broadcasted_iota(i32, (tokens, tokens), 0)
        query = lax.broadcasted_iota(i32, (tokens, tokens), 1)
        upper = key >= half
        own = key + jnp.where(upper, info_ref[4] - 1, info_ref[3]) * half
        par = key + jnp.where(upper, info_ref[6] - 1, info_ref[5]) * half
        at = query + jnp.where(query >= half, info_ref[4] - 1, info_ref[3]) * half
        for i, place in enumerate((own, par)):
            seen = place < length
            if causal:
                seen = seen & (place <= at)
            hide[i] = jnp.where(seen, 0.0, NEGATIVE)

    outs = []
    for h in range(LANES // HEAD_DIM):
        lanes = slice(h * HEAD_DIM, (h + 1) * HEAD_DIM)
        q = q_ref[0][:, lanes]
        s_own = dot(own_ref[0][:, lanes], q, NT) + hide[0]
        s_par = dot(par_ref[0][:, lanes], q, NT) + hide[1]
        top = jnp.maximum(
            jnp.max(s_own, axis=0, keepdims=True), jnp.max(s_par, axis=0, keepdims=True)
        )
        e_own = jnp.exp(s_own - top)
        e_par = jnp.exp(s_par - top)
        total = jnp.sum(e_own, axis=0, keepdims=True) + jnp.sum(e_par, axis=0, keepdims=True)
        scale = 1.0 / total
        p_own = (e_own * scale).astype(bf16)
        p_par = (e_par * scale).astype(bf16)
        p_ref[h, 0] = p_own
        p_ref[h, 1] = p_par
        outs.append(dot(own_ref[1][:, lanes], p_own, TN) + dot(par_ref[1][:, lanes], p_par, TN))
    o_ref[0] = jnp.concatenate(outs, axis=0).T.astype(bf16)


def attend(info, q, own, par, causal):
    _, tokens, width = q.shape
    heads = width // HEAD_DIM
    pair = LANES // HEAD_DIM
    one = pl.BlockSpec((1, tokens, LANES), lambda s, info: (0, 0, s))
    two = pl.BlockSpec((2, tokens, LANES), lambda s, info: (0, 0, s))
    return pl.pallas_call(
        functools.partial(attend_kernel, causal),
        out_shape=(
            jax.ShapeDtypeStruct((1, tokens, width), bf16),
            jax.ShapeDtypeStruct((heads, 2, tokens, tokens), bf16),
        ),
        grid_spec=pltpu.PrefetchScalarGridSpec(
            num_scalar_prefetch=1,
            grid=(heads // pair,),
            in_specs=[one, two, two],
            out_specs=(
                one,
                pl.BlockSpec((pair, 2, tokens, tokens), lambda s, info: (s, 0, 0, 0)),
            ),
            scratch_shapes=[pltpu.VMEM((2, tokens, tokens), f32)],
        ),
        compiler_params=params(),
        cost_estimate=cost(
            32 * tokens * tokens * width, 4 * heads * tokens * tokens, 2 * heads * tokens * tokens
        ),
        name="attend",
    )(info, q, own, par)


def middle_kernel(o_ref, w_ref, x_ref, wq_ref, gain_ref, bias_ref, x2_ref, c_ref, q_ref):
    x2 = x_ref[...] + dot(o_ref[0], whole_weight(w_ref), NT)
    x2_ref[...] = x2
    c = (normed(x2)[0] * gain_ref[2:3] + bias_ref[2:3]).astype(bf16)
    c_ref[...] = c

    def store(at, y):
        q_ref[0, :, pl.ds(at, wq_ref.shape[4])] = (y * HEAD_DIM**-0.5).astype(bf16)

    project(c, wq_ref, store)


def middle(o, second, x1, gains, biases):
    _, tokens, width = o.shape
    return pl.pallas_call(
        middle_kernel,
        out_shape=(
            jax.ShapeDtypeStruct((tokens, width), f32),
            jax.ShapeDtypeStruct((tokens, width), bf16),
            jax.ShapeDtypeStruct((1, tokens, width), bf16),
        ),
        grid=(1,),
        in_specs=[
            full(o.shape),
            weight_spec(second, lambda s: 0),
            full(x1.shape),
            weight_spec(second, lambda s: 1),
            full(gains.shape),
            full(biases.shape),
        ],
        out_specs=(full((tokens, width)), full((tokens, width)), full((1, tokens, width))),
        compiler_params=params(),
        cost_estimate=cost(4 * tokens * width * width, 14 * tokens * width + 4 * width * width),
        name="middle",
    )(o, second, x1, second, gains, biases)


def feed_kernel(
    o_ref,
    wo_ref,
    x_ref,
    w1_ref,
    w2_ref,
    og_ref,
    gain_ref,
    bias_ref,
    x3_ref,
    f_ref,
    g_ref,
    slope_ref,
    hid_ref,
    g4_ref,
    g4b_ref,
    sums_ref,
    total,
):
    step = pl.program_id(0)

    @pl.when(step == 0)
    def _():
        x3 = x_ref[...] + dot(o_ref[0], whole_weight(wo_ref), NT)
        x3_ref[...] = x3
        f_ref[...] = (normed(x3)[0] * gain_ref[3:4] + bias_ref[3:4]).astype(bf16)
        total[...] = x3

    def store(at, u):
        bell = 0.5 + 0.5 * lax.erf(u * 0.7071067811865476)
        lanes = pl.ds(at, w1_ref.shape[4])
        g_ref[0, :, lanes] = (u * bell).astype(bf16)
        slope = bell + u * (0.3989422804014327 * jnp.exp(-0.5 * u * u))
        slope_ref[0, :, lanes] = slope.astype(bf16)

    project(f_ref[...], w1_ref, store)
    total[...] += dot(g_ref[0], whole_weight(w2_ref), NT)

    @pl.when(step == pl.num_programs(0) - 1)
    def _():
        x4 = total[...]
        grad = og_ref[...].astype(f32)
        hid_ref[...] = (normed(x4)[0] * gain_ref[4:5] + bias_ref[4:5]).astype(hid_ref.dtype)
        g4, gain_grad, bias_grad = norm_back(x4, gain_ref[4:5], grad)
        g4_ref[...] = g4
        g4b_ref[...] = g4.astype(bf16)
        sums_ref[0:1] = gain_grad
        sums_ref[1:2] = bias_grad


def feed(o, second, x2, third, og, gains, biases):
    _, tokens, width = o.shape
    blocks = third.shape[2] // 2
    row = full((tokens, width))
    part = pl.BlockSpec((1, tokens, width), lambda s: (s, 0, 0))
    wide = jax.ShapeDtypeStruct((tokens, width), f32)
    slim = jax.ShapeDtypeStruct((tokens, width), bf16)
    many = jax.ShapeDtypeStruct((blocks, tokens, width), bf16)
    return pl.pallas_call(
        feed_kernel,
        out_shape=(wide, slim, many, many, slim, wide, slim, jax.ShapeDtypeStruct((2, width), f32)),
        grid=(blocks,),
        in_specs=[
            full(o.shape),
            weight_spec(second, lambda s: 4),
            row,
            weight_spec(third, lambda s: s),
            weight_spec(third, lambda s: s + blocks),
            row,
            full(gains.shape),
            full(biases.shape),
        ],
        out_specs=(row, row, part, part, row, row, row, full((2, width))),
        scratch_shapes=[pltpu.VMEM((tokens, width), f32)],
        compiler_params=params(60),
        cost_estimate=cost(
            (4 * blocks + 2) * tokens * width * width,
            (22 + 4 * blocks) * tokens * width + (2 + 4 * blocks) * width * width,
            2 * blocks * tokens * width,
        ),
        name="feed",
    )(o, second, x2, third, third, og, gains, biases)


def feed_back_kernel(
    g4_ref,
    g4b_ref,
    slope_ref,
    w1_ref,
    w2_ref,
    x3_ref,
    wo_ref,
    gain_ref,
    du_ref,
    g3_ref,
    g3b_ref,
    do_ref,
    sums_ref,
    total,
):
    step = pl.program_id(0)

    def store(at, y):
        lanes = pl.ds(at, w2_ref.shape[4])
        du_ref[0, :, lanes] = (y * slope_ref[0, :, lanes].astype(f32)).astype(bf16)

    project(g4b_ref[...], w2_ref, store)
    part = dot(du_ref[0], whole_weight(w1_ref), NT)

    @pl.when(step == 0)
    def _():
        total[...] = part

    @pl.when(step > 0)
    def _():
        total[...] += part

    @pl.when(step == pl.num_programs(0) - 1)
    def _():
        back, gain_grad, bias_grad = norm_back(x3_ref[...], gain_ref[3:4], total[...])
        g3 = g4_ref[...] + back
        g3_ref[...] = g3
        g3b = g3.astype(bf16)
        g3b_ref[...] = g3b
        sums_ref[0:1] = gain_grad
        sums_ref[1:2] = bias_grad

        def keep(at, y):
            do_ref[0, :, pl.ds(at, wo_ref.shape[4])] = y.astype(bf16)

        project(g3b, wo_ref, keep)


def feed_back(g4, g4b, slope, second, x3, third, gains):
    blocks, tokens, width = slope.shape
    row = full((tokens, width))
    part = pl.BlockSpec((1, tokens, width), lambda s: (s, 0, 0))
    wide = jax.ShapeDtypeStruct((tokens, width), f32)
    slim = jax.ShapeDtypeStruct((tokens, width), bf16)
    return pl.pallas_call(
        feed_back_kernel,
        out_shape=(
            jax.ShapeDtypeStruct((blocks, tokens, width), bf16),
            wide,
            slim,
            jax.ShapeDtypeStruct((1, tokens, width), bf16),
            jax.ShapeDtypeStruct((2, width), f32),
        ),
        grid=(blocks,),
        in_specs=[
            row,
            row,
            part,
            weight_spec(third, lambda s: s),
            weight_spec(third, lambda s: s + blocks),
            row,
            weight_spec(second, lambda s: 4),
            full(gains.shape),
        ],
        out_specs=(part, row, row, full((1, tokens, width)), full((2, width))),
        scratch_shapes=[pltpu.VMEM((tokens, width), f32)],
        compiler_params=params(60),
        cost_estimate=cost(
            (4 * blocks + 2) * tokens * width * width,
            (18 + 4 * blocks) * tokens * width + (2 + 4 * blocks) * width * width,
        ),
        name="feed_back",
    )(g4, g4b, slope, third, third, x3, second, gains)


def attend_back_kernel(
    q_ref, own_ref, par_ref, p_ref, o_ref, do_ref, dq_ref, down_ref, dpar_ref
):
    flat = do_ref[0].astype(f32).T * o_ref[0].astype(f32).T
    outs = []
    for h in range(LANES // HEAD_DIM):
        lanes = slice(h * HEAD_DIM, (h + 1) * HEAD_DIM)
        q = q_ref[0][:, lanes]
        grad = do_ref[0][:, lanes]
        inner = jnp.sum(flat[lanes], axis=0, keepdims=True)
        back = None
        for i, (kv_ref, d_ref) in enumerate(((own_ref, down_ref), (par_ref, dpar_ref))):
            keys = kv_ref[0][:, lanes]
            probs = p_ref[h, i]
            d_probs = dot(kv_ref[1][:, lanes], grad, NT)
            d_scores = (probs.astype(f32) * (d_probs - inner)).astype(bf16)
            d_ref[1, :, lanes] = dot(probs, grad).astype(bf16)
            d_ref[0, :, lanes] = dot(d_scores, q).astype(bf16)
            some = dot(keys, d_scores, TN)
            back = some if back is None else back + some
        outs.append(back)
    dq_ref[0] = (jnp.concatenate(outs, axis=0).T * HEAD_DIM**-0.5).astype(bf16)


def attend_back(q, own, par, probs, o, do):
    _, tokens, width = q.shape
    heads = width // HEAD_DIM
    pair = LANES // HEAD_DIM
    one = pl.BlockSpec((1, tokens, LANES), lambda s: (0, 0, s))
    two = pl.BlockSpec((2, tokens, LANES), lambda s: (0, 0, s))
    kv = jax.ShapeDtypeStruct((2, tokens, width), bf16)
    return pl.pallas_call(
        attend_back_kernel,
        out_shape=(jax.ShapeDtypeStruct((1, tokens, width), bf16), kv, kv),
        grid=(heads // pair,),
        in_specs=[
            one,
            two,
            two,
            pl.BlockSpec((pair, 2, tokens, tokens), lambda s: (s, 0, 0, 0)),
            one,
            one,
        ],
        out_specs=(one, two, two),
        compiler_params=params(),
        cost_estimate=cost(64 * tokens * tokens * width, 4 * heads * tokens * tokens),
        name="attend_back",
    )(q, own, par, probs, o, do)


def middle_back_kernel(
    dq_ref, wq_ref, x2_ref, g3_ref, wo_ref, gain_ref, g2_ref, g2b_ref, do_ref, sums_ref
):
    d_normed = dot(dq_ref[0], whole_weight(wq_ref), NT)
    back, gain_grad, bias_grad = norm_back(x2_ref[...], gain_ref[2:3], d_normed)
    g2 = g3_ref[...] + back
    g2_ref[...] = g2
    g2b = g2.astype(bf16)
    g2b_ref[...] = g2b
    sums_ref[0:1] = gain_grad
    sums_ref[1:2] = bias_grad

    def keep(at, y):
        do_ref[0, :, pl.ds(at, wo_ref.shape[4])] = y.astype(bf16)

    project(g2b, wo_ref, keep)


def middle_back(dq, second, x2, g3, gains):
    _, tokens, width = dq.shape
    row = full((tokens, width))
    return pl.pallas_call(
        middle_back_kernel,
        out_shape=(
            jax.ShapeDtypeStruct((tokens, width), f32),
            jax.ShapeDtypeStruct((tokens, width), bf16),
            jax.ShapeDtypeStruct((1, tokens, width), bf16),
            jax.ShapeDtypeStruct((2, width), f32),
        ),
        grid=(1,),
        in_specs=[
            full(dq.shape),
            weight_spec(second, lambda s: 1),
            row,
            row,
            weight_spec(second, lambda s: 0),
            full(gains.shape),
        ],
        out_specs=(row, row, full((1, tokens, width)), full((2, width))),
        compiler_params=params(),
        cost_estimate=cost(4 * tokens * width * width, 18 * tokens * width + 4 * width * width),
        name="middle_back",
    )(dq, second, x2, g3, second, gains)


def source_back_kernel(mine_ref, came_ref, w_ref, out_ref, sum_ref, total):
    step = pl.program_id(0)
    grads = (mine_ref[0].astype(f32) + came_ref[0].astype(f32)).astype(bf16)
    sum_ref[0] = grads
    part = dot(grads, whole_weight(w_ref), NT)

    @pl.when(step == 0)
    def _():
        total[...] = part

    @pl.when(step == pl.num_programs(0) - 1)
    def _():
        out_ref[...] = (total[...] + part).astype(bf16)


def source_back(mine, came, second):
    parts, tokens, width = mine.shape
    part = pl.BlockSpec((1, tokens, width), lambda s: (s, 0, 0))
    return pl.pallas_call(
        source_back_kernel,
        out_shape=(
            jax.ShapeDtypeStruct((tokens, width), bf16),
            jax.ShapeDtypeStruct((parts, tokens, width), bf16),
        ),
        grid=(parts,),
        in_specs=[part, part, weight_spec(second, lambda s: s + 2)],
        out_specs=(full((tokens, width)), part),
        scratch_shapes=[pltpu.VMEM((tokens, width), f32)],
        compiler_params=params(),
        cost_estimate=cost(4 * tokens * width * width, 14 * tokens * width + 4 * width * width),
        name="source_back",
    )(mine, came, second)


def exit_kernel(
    dq_ref, mine_ref, came_ref, w_ref, x1_ref, x0_ref, g2_ref, gain_ref, g0_ref, sum_ref, sums_ref, total
):
    step = pl.program_id(0)

    @pl.when(step == 0)
    def _():
        total[...] = dot(dq_ref[0], whole_weight(w_ref), NT)

    @pl.when(step > 0)
    def _():
        grads = (mine_ref[0].astype(f32) + came_ref[0].astype(f32)).astype(bf16)
        sum_ref[0] = grads
        total[...] += dot(grads, whole_weight(w_ref), NT)

    @pl.when(step == pl.num_programs(0) - 1)
    def _():
        back, gain_one, bias_one = norm_back(x1_ref[...], gain_ref[1:2], total[...])
        g1 = g2_ref[...] + back
        g0, gain_zero, bias_zero = norm_back(x0_ref[...], gain_ref[0:1], g1)
        g0_ref[...] = g0.T.astype(bf16)
        sums_ref[0:1] = gain_zero
        sums_ref[1:2] = bias_zero
        sums_ref[2:3] = gain_one
        sums_ref[3:4] = bias_one


def exit_back(dq, mine, came, first, x1, x0, g2, gains):
    _, tokens, width = dq.shape
    row = full((tokens, width))
    part = pl.BlockSpec((1, tokens, width), lambda s: (jnp.maximum(s - 1, 0), 0, 0))
    return pl.pallas_call(
        exit_kernel,
        out_shape=(
            jax.ShapeDtypeStruct((width, tokens), bf16),
            jax.ShapeDtypeStruct((2, tokens, width), bf16),
            jax.ShapeDtypeStruct((4, width), f32),
        ),
        grid=(3,),
        in_specs=[
            full(dq.shape),
            part,
            part,
            weight_spec(first, lambda s: s + 1),
            row,
            row,
            row,
            full(gains.shape),
        ],
        out_specs=(full((width, tokens)), part, full((4, width))),
        scratch_shapes=[pltpu.VMEM((tokens, width), f32)],
        compiler_params=params(),
        cost_estimate=cost(6 * tokens * width * width, 28 * tokens * width + 6 * width * width),
        name="exit_back",
    )(dq, mine, came, first, x1, x0, g2, gains)


def weight_grad_kernel(chips, aliased, info_ref, xo_ref, xp_ref, yo_ref, yp_ref, *refs):
    out_ref, turned = refs[-2], refs[-1]
    tokens, width = xo_ref.shape
    rows = width // (chips * CORES)
    core = info_ref[0]

    @pl.when(pl.program_id(0) == 0)
    def _():
        for i, x_ref in enumerate((xo_ref, xp_ref)):
            at = slice(i * tokens, (i + 1) * tokens)
            if rows % LANES == 0:
                for j in range(chips):
                    lanes = pl.ds(pl.multiple_of((2 * j + core) * rows, rows), rows)
                    turned[j * rows : (j + 1) * rows, at] = x_ref[:, lanes].astype(f32).T.astype(bf16)
            else:
                tall = x_ref[...].astype(f32).T.reshape(chips, CORES, rows, tokens)
                mine = jnp.where(core == 0, tall[:, 0], tall[:, 1])
                turned[:, at] = mine.reshape(chips * rows, tokens).astype(bf16)

    y_own, y_par = yo_ref[0], yp_ref[0]
    blocks, span = out_ref.shape[1], out_ref.shape[4]
    result = dot(turned[:, :tokens], y_own) + dot(turned[:, tokens:], y_par)
    for m in range(blocks):
        part = result[:, m * span : (m + 1) * span].astype(bf16)
        out_ref[:, m, 0] = part.reshape(chips, rows, span)


def weight_grad(info, x_own, x_par, y_own, y_par, shape, at, before=None):
    parts, tokens, width = y_own.shape
    chips = shape[0]
    row = full(x_own.shape)
    part = pl.BlockSpec((1, tokens, width), lambda s, info: (s, 0, 0))
    extra = [] if before is None else [before]
    return pl.pallas_call(
        functools.partial(weight_grad_kernel, chips, before is not None),
        out_shape=jax.ShapeDtypeStruct(shape, bf16),
        grid_spec=pltpu.PrefetchScalarGridSpec(
            num_scalar_prefetch=1,
            grid=(parts,),
            in_specs=[row, row, part, part] + [pl.BlockSpec(memory_space=pl.ANY) for _ in extra],
            out_specs=pl.BlockSpec(
                (chips, shape[1], 1, shape[3], shape[4]), lambda s, info: (0, 0, s + at, 0, 0)
            ),
            scratch_shapes=[pltpu.VMEM((x_own.shape[1] // 2, 2 * tokens), bf16)],
        ),
        input_output_aliases={} if before is None else {5: 0},
        compiler_params=params(),
        cost_estimate=cost(
            2 * parts * tokens * width * width, 5 * parts * tokens * width + 4 * tokens * width
        ),
        name="weight_grad",
    )(info, x_own, x_par, y_own, y_par, *extra)


def swap(value):
    return lax.ppermute(value, "core", [(0, 1), (1, 0)])


def line_moves(mp):
    rounds = []
    for turn in range(2):
        moves = []
        for c in range(CORES):
            for m in range(mp):
                target, slot = (1 if m in (1, 2) else 0), m // 2
                moves.append((c * mp + m, target * mp + 2 * c + (slot ^ turn)))
        rounds.append(moves)
    return rounds


def to_chips(value, mp):
    m = lax.axis_index("mp")
    slot, odd = m // 2, m % 2
    came = []
    for turn, moves in enumerate(line_moves(mp)):
        sent = jnp.where((slot ^ turn) == 0, value[0], value[1])
        came.append(lax.ppermute(sent, LINE, moves))
    return jnp.concatenate(
        [jnp.where(odd == 0, came[0], came[1]), jnp.where(odd == 0, came[1], came[0])], axis=0
    )


def from_chips(value, mp):
    m = lax.axis_index("mp")
    slot, odd = m // 2, m % 2
    half = value.shape[0] // 2
    came = []
    for turn, moves in enumerate(line_moves(mp)):
        sent = jnp.where((odd ^ turn) == 0, value[:half], value[half:])
        came.append(lax.ppermute(sent, LINE, [(b, a) for a, b in moves]))
    return jnp.stack(
        [jnp.where(slot == 0, came[0], came[1]), jnp.where(slot == 0, came[1], came[0])]
    )


def packed(*weights):
    return jnp.concatenate([w.reshape(-1, w.shape[-1]) for w in weights], axis=0)


def gathered(rows, dp, mp, parts):
    value = lax.all_gather(rows, ALL, axis=0, tiled=False)
    return value.reshape(dp, mp, parts, rows.shape[0] // parts, rows.shape[1])


def scattered(grads):
    part = lax.psum_scatter(grads, "chip", scatter_dimension=0, tiled=False)
    return lax.psum_scatter(part, "mp", scatter_dimension=0, tiled=False).astype(f32)


def body(
    chips,
    mp,
    target_ids,
    tgt_lengths,
    encoder_states,
    src_lengths,
    table,
    pos_table,
    self_query_key_value_weight,
    self_output_weight,
    cross_query_weight,
    cross_key_value_weight,
    cross_output_weight,
    feedforward_input_weight,
    feedforward_output_weight,
    norm_gains,
    norm_biases,
    out_grad,
):
    dp = chips * CORES
    n = dp * mp
    seqs, block = target_ids.shape
    assert seqs * CORES == mp == 4
    tokens = seqs * block
    width = norm_gains.shape[1]
    vocab = table.shape[1]
    feats = table.shape[0]
    rows = pos_table.shape[0]
    core, m = lax.axis_index("core"), lax.axis_index("mp")

    def split(weight):
        return weight.reshape(rows, -1, block).transpose(1, 0, 2)

    all_ids = lax.all_gather(target_ids.reshape(-1), "mp", axis=0, tiled=False)
    all_ids = lax.all_gather(all_ids, ("chip", "core"), axis=0, tiled=False)
    first = gathered(packed(pos_table, split(self_query_key_value_weight)), dp, mp, 4)
    second = gathered(
        packed(
            self_output_weight, cross_query_weight, split(cross_key_value_weight), cross_output_weight
        ),
        dp,
        mp,
        5,
    )
    sub = feedforward_input_weight.shape[1] // block
    third = gathered(
        packed(split(feedforward_input_weight), split(feedforward_output_weight)), dp, mp, 2 * sub
    )

    lengths = jnp.stack([tgt_lengths, src_lengths])
    other = swap(lengths)
    lengths = jnp.where(
        core == 0,
        jnp.concatenate([lengths, other], axis=1),
        jnp.concatenate([other, lengths], axis=1),
    )
    lengths = lax.dynamic_index_in_dim(lengths, m, axis=1, keepdims=False)
    info = jnp.stack(
        [core, lengths[0], lengths[1], core, 3 - core, 1 - core, 2 + core, jnp.zeros_like(core)]
    ).astype(i32)

    ids = all_ids.reshape(chips, CORES, mp, seqs, block)
    ids = jnp.stack([ids[:, :, 0], ids[:, :, 3], ids[:, :, 1], ids[:, :, 2]], axis=2)
    ids = ids.reshape(chips, CORES, CORES, 2, seqs, block).transpose(0, 2, 1, 4, 3, 5)
    ids = ids.reshape(n, 1, tokens)
    height = vocab // (LANES // feats)
    row, group = ids % height, ids // height
    flat_row = row.reshape(-1)

    picked = gather_tokens(table, flat_row, group)
    emb = lax.all_to_all(picked, ALL, split_axis=0, concat_axis=0, tiled=True)
    emb = emb.reshape(width, tokens)

    states = to_chips(encoder_states, mp)
    og = to_chips(out_grad.astype(bf16), mp)

    x0, x1, a, q, kv = entry(info, emb, first, norm_gains, norm_biases)
    kv_par = swap(kv)
    ckv = source_keys(states, second)
    ckv_par = swap(ckv)
    o, probs = attend(info, q, kv, kv_par, True)
    x2, c, cq = middle(o, second, x1, norm_gains, norm_biases)
    oc, cprobs = attend(info, cq, ckv, ckv_par, False)
    x3, f, g, slope, hid, g4, g4b, sums4 = feed(
        oc, second, x2, third, og, norm_gains, norm_biases
    )
    hidden_out = from_chips(hid, mp).astype(f32)

    du, g3, g3b, doc, sums3 = feed_back(g4, g4b, slope, second, x3, third, norm_gains)
    shape = (chips, mp, 2 * sub, rows, block)
    grads = weight_grad(info, f, swap(f), du, swap(du), shape, 0)
    grads = weight_grad(info, g4b, swap(g4b), g, swap(g), shape, sub, grads)
    feed_grads = scattered(grads)

    dcq, dckv_own, dckv_par = attend_back(cq, ckv, ckv_par, cprobs, oc, doc)
    dckv_came = swap(dckv_par)
    g2, g2b, do, sums2 = middle_back(dcq, second, x2, g3, norm_gains)
    enc_grad, dckv = source_back(dckv_own, dckv_came, second)
    encoder_grad = from_chips(enc_grad, mp).astype(f32)
    shape = (chips, mp, 4, rows, block)
    grads = weight_grad(info, g3b, swap(g3b), oc, swap(oc), shape, 0)
    grads = weight_grad(info, c, swap(c), dcq, swap(dcq), shape, 1, grads)
    grads = weight_grad(info, states, swap(states), dckv, swap(dckv), shape, 2, grads)
    cross_grads = scattered(grads)

    dq, dkv_own, dkv_par = attend_back(q, kv, kv_par, probs, o, do)
    dkv_came = swap(dkv_par)
    g0, dkv, sums01 = exit_back(dq, dkv_own, dkv_came, first, x1, x0, g2, norm_gains)
    sent = g0.reshape(n, feats, tokens)
    arrived = lax.all_to_all(sent, ALL, split_axis=0, concat_axis=0, tiled=True)
    grads = weight_grad(info, g2b, swap(g2b), o, swap(o), shape, 0)
    grads = weight_grad(info, a, swap(a), dq, swap(dq), shape, 1, grads)
    grads = weight_grad(info, a, swap(a), dkv, swap(dkv), shape, 2, grads)
    self_grads = scattered(grads)

    table_grad, places = scatter_tokens(arrived, flat_row, row, group, vocab, mp)

    blocks = places.reshape(CORES, feats, 2, block).transpose(0, 2, 1, 3).reshape(4, feats, block)
    blocks = jnp.stack([blocks[0], blocks[2], blocks[3], blocks[1]])
    parts = []
    for k in range(mp):
        mine = lax.dynamic_index_in_dim(blocks, (m + k) % mp, axis=0, keepdims=False)
        parts.append(
            mine if k == 0 else lax.ppermute(mine, "mp", [(i, (i + k) % mp) for i in range(mp)])
        )
    pos_grad = []
    for source in range(mp):
        value = parts[0]
        for k in range(1, mp):
            value = jnp.where((m - source) % mp == k, parts[k], value)
        pos_grad.append(value)
    pos_grad = jnp.concatenate(pos_grad, axis=0)

    sums = jnp.concatenate([sums01, sums2, sums3, sums4], axis=0)
    sums = lax.psum(sums, ALL)

    def join(parts):
        return parts.transpose(1, 0, 2)

    return (
        hidden_out,
        table_grad,
        pos_grad,
        join(self_grads[1:4]),
        self_grads[0],
        cross_grads[1],
        join(cross_grads[2:4]),
        cross_grads[0],
        join(feed_grads[:sub]).reshape(rows, -1),
        join(feed_grads[sub:]).reshape(rows, -1),
        sums[0::2],
        sums[1::2],
        encoder_grad,
    )


def solution(mesh):
    dp, mp = mesh.devices.shape
    chips = dp // CORES
    fine = Mesh(mesh.devices.reshape(chips, CORES, mp), ALL)
    both = ("chip", "core")
    placed = (
        P(both, "mp"),
        P(both),
        P(both, "mp", None),
        P(both),
        P(ALL, None),
        P(both, "mp"),
        P(both, None, "mp"),
        P(both, "mp"),
        P(both, "mp"),
        P(both, None, "mp"),
        P(both, "mp"),
        P(both, "mp"),
        P(both, "mp"),
        P(),
        P(),
        P(both, "mp", None),
    )
    return jax.shard_map(
        functools.partial(body, chips, mp),
        mesh=fine,
        in_specs=placed,
        out_specs=(
            P(both, "mp", None),
            P(ALL, None),
            P(both, "mp"),
            P(both, None, "mp"),
            P(both, "mp"),
            P(both, "mp"),
            P(both, None, "mp"),
            P(both, "mp"),
            P(both, "mp"),
            P(both, "mp"),
            P(),
            P(),
            P(both, "mp", None),
        ),
        check_vma=False,
    )
```

```python
import functools

import jax
import jax.numpy as jnp
from jax import lax
from jax.experimental import pallas as pl
from jax.experimental.pallas import tpu as pltpu
from jax.sharding import Mesh
from jax.sharding import PartitionSpec as P

HEAD_DIM = 64
EPSILON = 1e-05
NEGATIVE = -1e30
LANES = 128
ALL = ("chip", "core", "mp")
LINE = ("core", "mp")
CORES = 2

f32 = jnp.float32
bf16 = jnp.bfloat16
i32 = jnp.int32

NT = (((1,), (1,)), ((), ()))
NN = (((1,), (0,)), ((), ()))
TN = (((0,), (0,)), ((), ()))


def dot(a, b, dims=NN):
    return lax.dot_general(a, b, dims, preferred_element_type=f32)


def params(mib=56):
    return pltpu.CompilerParams(vmem_limit_bytes=mib << 20)


def cost(microseconds):
    return pl.CostEstimate(flops=0, bytes_accessed=int(microseconds * 3.2e6), transcendentals=0)


def normed(values):
    centred = values - jnp.mean(values, axis=-1, keepdims=True)
    inverse = lax.rsqrt(jnp.mean(centred * centred, axis=-1, keepdims=True) + EPSILON)
    return centred * inverse, inverse


def norm_back(values, gain, grad):
    hat, inverse = normed(values)
    scaled = grad * gain
    first = jnp.mean(scaled, axis=-1, keepdims=True)
    second = jnp.mean(scaled * hat, axis=-1, keepdims=True)
    back = inverse * (scaled - first - hat * second)
    gain_grad = jnp.sum(grad * hat, axis=0, keepdims=True)
    bias_grad = jnp.sum(grad, axis=0, keepdims=True)
    return back, gain_grad, bias_grad


def in_order(pieces, info_ref):
    for bit, place in ((0, 0), (1, 7), (2, 8)):
        far = info_ref[place] == 1
        turned = []
        for i, piece in enumerate(pieces):
            turned.append(jnp.where(far, pieces[i ^ (1 << bit)], piece))
        pieces = turned
    return pieces


def joined(blocks, info_ref):
    flat = [b.reshape(-1, b.shape[-1]) for b in blocks]
    return flat[0] if len(flat) == 1 else jnp.concatenate(in_order(flat, info_ref), axis=0)


def columns(w_refs, m, info_ref):
    return joined([w[:, pl.ds(m, 1)] for w in w_refs], info_ref)


def whole_weight(w_refs, info_ref):
    parts = [columns(w_refs, m, info_ref) for m in range(w_refs[0].shape[1])]
    return jnp.concatenate(parts, axis=1)


def project(x, w_refs, info_ref, store):
    width = w_refs[0].shape[4]

    def step(m, carry):
        store(pl.multiple_of(m * width, width), dot(x, columns(w_refs, m, info_ref)))
        return carry

    lax.fori_loop(0, w_refs[0].shape[1], step, 0)


def weight_specs(weights, index):
    return [
        pl.BlockSpec(
            (w.shape[0], w.shape[1], 1, w.shape[3], w.shape[4]),
            lambda s, info, skip=skip: (0, 0, index(s) + skip, 0, 0),
        )
        for w, skip in weights
    ]


def call(kernel, info, grid, operands, outs, scratch=(), mib=56, **others):
    arrays, specs, sizes = [], [], []
    for value, spec in operands:
        group = isinstance(value, (list, tuple))
        sizes.append(len(value) if group else None)
        arrays.extend([w for w, _ in value] if group else [value])
        specs.extend(spec if group else [spec])

    def body(info_ref, *refs):
        given, rest, at = [], refs, 0
        for size in sizes:
            given.append(refs[at] if size is None else list(refs[at : at + size]))
            at += 1 if size is None else size
        kernel(info_ref, *given, *rest[at:])

    return pl.pallas_call(
        body,
        out_shape=[o for o, _ in outs],
        grid_spec=pltpu.PrefetchScalarGridSpec(
            num_scalar_prefetch=1,
            grid=grid,
            in_specs=specs,
            out_specs=[o for _, o in outs],
            scratch_shapes=list(scratch),
        ),
        compiler_params=params(mib),
        **others,
    )(info, *arrays)


def full(shape):
    return pl.BlockSpec(shape, lambda *a: (0,) * len(shape))


def gather_kernel(groups, fill, rows_ref, group_ref, *refs):
    tables, out_ref, turned, picked = refs[:groups], refs[groups], refs[-2], refs[-1]
    step = pl.program_id(0)
    feats, width = tables[0].shape
    tokens = picked.shape[0]

    @pl.when(step < fill)
    def _():
        stacked = jnp.concatenate([t[...].astype(f32) for t in tables], axis=0).astype(bf16)
        row = lax.broadcasted_iota(i32, (256, 256), 0)
        eye = jnp.where(row == lax.broadcasted_iota(i32, (256, 256), 1), 1.0, 0.0).astype(bf16)
        for k in range(width // 256):
            at = pl.multiple_of(step * width + k * 256, 256)
            turned[pl.ds(at, 256), :] = dot(eye, stacked[:, k * 256 : (k + 1) * 256], NT)

    @pl.when(step >= fill)
    def _():
        base = (step - fill) * tokens

        def some(k, carry):
            for u in range(16):
                t = k * 16 + u
                picked[pl.ds(t, 1), :] = turned[pl.ds(rows_ref[base + t], 1), :]
            return carry

        lax.fori_loop(0, tokens // 16, some, 0)
        row = lax.broadcasted_iota(i32, (LANES, LANES), 0)
        eye = jnp.where(row == lax.broadcasted_iota(i32, (LANES, LANES), 1), 1.0, 0.0)
        across = dot(eye.astype(bf16), picked[...].astype(bf16), NT)
        own = lax.broadcasted_iota(i32, (LANES, tokens), 0) // feats == group_ref[0]
        kept = jnp.where(own, across, 0.0)
        total = kept[:feats]
        for g in range(1, groups):
            total = total + kept[g * feats : (g + 1) * feats]
        out_ref[0] = total.astype(out_ref.dtype)


def gather_tokens(table, rows, group):
    feats, vocab = table.shape
    groups = LANES // feats
    height = vocab // groups
    n, _, tokens = group.shape
    width = min(2048, height)
    fill = height // width

    def table_spec(g):
        return pl.BlockSpec(
            (feats, width), lambda s, r, g=g: (0, g * fill + jnp.minimum(s, fill - 1))
        )

    return pl.pallas_call(
        functools.partial(gather_kernel, groups, fill),
        out_shape=jax.ShapeDtypeStruct((n, feats, tokens), bf16),
        grid_spec=pltpu.PrefetchScalarGridSpec(
            num_scalar_prefetch=1,
            grid=(fill + n,),
            in_specs=[pl.BlockSpec((1, 1, tokens), lambda s, r: (jnp.maximum(s - fill, 0), 0, 0))]
            + [table_spec(g) for g in range(groups)],
            out_specs=pl.BlockSpec(
                (1, feats, tokens), lambda s, r: (jnp.maximum(s - fill, 0), 0, 0)
            ),
            scratch_shapes=[pltpu.VMEM((height, LANES), f32), pltpu.VMEM((tokens, LANES), f32)],
        ),
        compiler_params=params(),
        cost_estimate=cost(45),
        name="gather_tokens",
    )(rows, group, *([table] * groups))


BATCH = 16


def scatter_kernel(
    groups, per_core, rows_ref, row_ref, group_ref, grad_ref, out_ref, pos_ref, acc, update, turned, sem
):
    step = pl.program_id(0)
    feats, tokens = grad_ref.shape[1:]
    height = acc.shape[0]
    width = turned.shape[2]

    @pl.when(step == 0)
    def _():
        def clear(k, carry):
            acc[pl.ds(pl.multiple_of(k * 256, 256), 256), :] = jnp.zeros((256, LANES), f32)
            return carry

        lax.fori_loop(0, height // 256, clear, 0)
        pos_ref[...] = jnp.zeros_like(pos_ref)

    grads = grad_ref[0].astype(f32)
    core = lax.rem(lax.div(step, per_core), CORES)
    pos_ref[core] += grads
    tall = jnp.concatenate([grads] * groups, axis=0)
    own = lax.broadcasted_iota(i32, (LANES, tokens), 0) // feats == group_ref[0]
    tall = jnp.where(own, tall, 0.0).astype(bf16)
    row = lax.broadcasted_iota(i32, (LANES, LANES), 0)
    col = lax.broadcasted_iota(i32, (LANES, LANES), 1)
    near = row // BATCH == col // BATCH
    for b in range(tokens // LANES):
        at = slice(b * LANES, (b + 1) * LANES)
        along = jnp.broadcast_to(row_ref[0][:, at].astype(f32), (LANES, LANES))
        same = jnp.where((along == along.T) & near, 1.0, 0.0).astype(bf16)
        update[at, :] = dot(same, tall[:, at], NT)
    base = step * tokens

    def some(k, carry):
        where = [rows_ref[base + k * BATCH + u] for u in range(BATCH)]
        fresh = [
            acc[pl.ds(where[u], 1), :] + update[pl.ds(k * BATCH + u, 1), :] for u in range(BATCH)
        ]
        for u in range(BATCH):
            acc[pl.ds(where[u], 1), :] = fresh[u]
        return carry

    lax.fori_loop(0, tokens // BATCH, some, 0)

    @pl.when(step == pl.num_programs(0) - 1)
    def _():
        def copy(i, slot, g):
            at = pl.multiple_of(g * height + i * width, width)
            return pltpu.make_async_copy(
                turned.at[slot, pl.ds(g * feats, feats)],
                out_ref.at[:, pl.ds(at, width)],
                sem.at[slot, g],
            )

        def turn(i, carry):
            slot = lax.rem(i, 2)

            @pl.when(i >= 2)
            def _():
                for g in range(groups):
                    copy(i - 2, slot, g).wait()

            at = pl.multiple_of(i * width, width)
            turned[slot] = (acc[pl.ds(at, width), :] * 32.0).T
            for g in range(groups):
                copy(i, slot, g).start()
            return carry

        count = height // width
        lax.fori_loop(0, count, turn, 0)
        for i in range(max(count - 2, 0), count):
            for g in range(groups):
                copy(i, i % 2, g).wait()


def scatter_tokens(grads, rows, row, group, vocab, per_core):
    n, feats, tokens = grads.shape
    groups = LANES // feats
    height = vocab // groups
    width = min(1024, height)
    token_spec = pl.BlockSpec((1, 1, tokens), lambda s, r: (s, 0, 0))
    return pl.pallas_call(
        functools.partial(scatter_kernel, groups, per_core),
        out_shape=(
            jax.ShapeDtypeStruct((feats, vocab), f32),
            jax.ShapeDtypeStruct((CORES, feats, tokens), f32),
        ),
        grid_spec=pltpu.PrefetchScalarGridSpec(
            num_scalar_prefetch=1,
            grid=(n,),
            in_specs=[
                token_spec,
                token_spec,
                pl.BlockSpec((1, feats, tokens), lambda s, r: (s, 0, 0)),
            ],
            out_specs=(
                pl.BlockSpec(memory_space=pl.ANY),
                full((CORES, feats, tokens)),
            ),
            scratch_shapes=[
                pltpu.VMEM((height, LANES), f32),
                pltpu.VMEM((tokens, LANES), f32),
                pltpu.VMEM((2, LANES, width), f32),
                pltpu.SemaphoreType.DMA((2, groups)),
            ],
        ),
        compiler_params=params(),
        cost_estimate=cost(57),
        name="scatter_tokens",
    )(rows, row, group, grads)


def entry_kernel(
    info_ref, emb_ref, pos_a, pos_b, wq_ref, wkv_ref, gain_ref, bias_ref, x0_ref, x1_ref, a_ref, q_ref, kv_ref
):
    step = pl.program_id(0)
    half = x0_ref.shape[0] // 2

    @pl.when(step == 0)
    def _():
        for i, pos in enumerate((pos_a, pos_b)):
            at = slice(i * half, (i + 1) * half)
            places = joined([p[...] for p in pos], info_ref)
            x0 = (emb_ref[:, at].astype(f32) * 32.0 + places.astype(f32)).T
            x1 = normed(x0)[0] * gain_ref[0:1] + bias_ref[0:1]
            a = normed(x1)[0] * gain_ref[1:2] + bias_ref[1:2]
            x0_ref[at] = x0
            x1_ref[at] = x1
            a_ref[at] = a.astype(bf16)

    x = a_ref[...]
    span = wq_ref[0].shape[4]

    @pl.when(step == 0)
    def _():
        def store(at, y):
            q_ref[0, :, pl.ds(at, span)] = (y * HEAD_DIM**-0.5).astype(bf16)

        project(x, wq_ref, info_ref, store)

    @pl.when(step > 0)
    def _():
        def store(at, y):
            kv_ref[0, :, pl.ds(at, span)] = y.astype(bf16)

        project(x, wkv_ref, info_ref, store)


def entry(info, emb, first, gains, biases):
    width, tokens = emb.shape
    wq, wkv = first

    def pos_specs(i):
        return [
            pl.BlockSpec(
                (w.shape[0], 1, 1, w.shape[3], w.shape[4]),
                lambda s, info, skip=skip: (0, info[3 + i], skip, 0, 0),
            )
            for w, skip in wq
        ]

    row = full((tokens, width))
    rows = jax.ShapeDtypeStruct((tokens, width), f32)
    return call(
        entry_kernel,
        info,
        (3,),
        [
            (emb, full(emb.shape)),
            (wq, pos_specs(0)),
            (wq, pos_specs(1)),
            (wq, weight_specs(wq, lambda s: 1)),
            (wkv, weight_specs(wkv, lambda s: jnp.maximum(s - 1, 0))),
            (gains, full(gains.shape)),
            (biases, full(biases.shape)),
        ],
        [
            (rows, row),
            (rows, row),
            (jax.ShapeDtypeStruct((tokens, width), bf16), row),
            (jax.ShapeDtypeStruct((1, tokens, width), bf16), full((1, tokens, width))),
            (
                jax.ShapeDtypeStruct((2, tokens, width), bf16),
                pl.BlockSpec((1, tokens, width), lambda s, info: (jnp.maximum(s - 1, 0), 0, 0)),
            ),
        ],
        cost_estimate=cost(15),
        name="entry",
    )


def slots(pair, info_ref):
    odd = info_ref[9] == 1
    one, two = pair[0][...], pair[1][...]
    return jnp.where(odd, two, one), jnp.where(odd, one, two)


def put_slots(pair, info_ref, values):
    for odd in range(2):

        @pl.when(info_ref[9] == odd)
        def _():
            pair[odd][...] = values[0].astype(bf16)
            pair[1 - odd][...] = values[1].astype(bf16)


def source_kernel(info_ref, came_a, came_b, w_refs, x_ref, kv_ref):
    @pl.when(pl.program_id(0) == 0)
    def _():
        half = came_a.shape[0]
        x_ref[:half], x_ref[half:] = slots((came_a, came_b), info_ref)

    def store(at, y):
        kv_ref[0, :, pl.ds(at, w_refs[0].shape[4])] = y.astype(bf16)

    project(x_ref[...], w_refs, info_ref, store)


def source_keys(info, came, weights):
    half, width = came[0].shape
    tokens = 2 * half
    return call(
        source_kernel,
        info,
        (2,),
        [
            (came[0], full((half, width))),
            (came[1], full((half, width))),
            (weights, weight_specs(weights, lambda s: s)),
        ],
        [
            (jax.ShapeDtypeStruct((tokens, width), bf16), full((tokens, width))),
            (
                jax.ShapeDtypeStruct((2, tokens, width), bf16),
                pl.BlockSpec((1, tokens, width), lambda s, info: (s, 0, 0)),
            ),
        ],
        cost_estimate=cost(8),
        name="source_keys",
    )


def attend_kernel(causal, info_ref, q_ref, own_ref, par_ref, o_ref, p_ref, hide):
    tokens = q_ref.shape[1]
    half = tokens // 2
    core = info_ref[0]

    @pl.when(pl.program_id(0) == 0)
    def _():
        length = info_ref[1] if causal else info_ref[2]
        key = lax.broadcasted_iota(i32, (tokens, tokens), 0)
        query = lax.broadcasted_iota(i32, (tokens, tokens), 1)
        upper = key >= half
        own = key + jnp.where(upper, info_ref[4] - 1, info_ref[3]) * half
        par = key + jnp.where(upper, info_ref[6] - 1, info_ref[5]) * half
        at = query + jnp.where(query >= half, info_ref[4] - 1, info_ref[3]) * half
        for i, place in enumerate((own, par)):
            seen = place < length
            if causal:
                seen = seen & (place <= at)
            hide[i] = jnp.where(seen, 0.0, NEGATIVE)

    outs = []
    for h in range(LANES // HEAD_DIM):
        lanes = slice(h * HEAD_DIM, (h + 1) * HEAD_DIM)
        q = q_ref[0][:, lanes]
        s_own = dot(own_ref[0][:, lanes], q, NT) + hide[0]
        s_par = dot(par_ref[0][:, lanes], q, NT) + hide[1]
        top = jnp.maximum(
            jnp.max(s_own, axis=0, keepdims=True), jnp.max(s_par, axis=0, keepdims=True)
        )
        e_own = jnp.exp(s_own - top)
        e_par = jnp.exp(s_par - top)
        total = jnp.sum(e_own, axis=0, keepdims=True) + jnp.sum(e_par, axis=0, keepdims=True)
        scale = 1.0 / total
        p_own = (e_own * scale).astype(bf16)
        p_par = (e_par * scale).astype(bf16)
        p_ref[h, 0] = p_own
        p_ref[h, 1] = p_par
        outs.append(dot(own_ref[1][:, lanes], p_own, TN) + dot(par_ref[1][:, lanes], p_par, TN))
    o_ref[0] = jnp.concatenate(outs, axis=0).T.astype(bf16)


def attend(info, q, own, par, causal):
    _, tokens, width = q.shape
    heads = width // HEAD_DIM
    pair = LANES // HEAD_DIM
    one = pl.BlockSpec((1, tokens, LANES), lambda s, info: (0, 0, s))
    two = pl.BlockSpec((2, tokens, LANES), lambda s, info: (0, 0, s))
    return pl.pallas_call(
        functools.partial(attend_kernel, causal),
        out_shape=(
            jax.ShapeDtypeStruct((1, tokens, width), bf16),
            jax.ShapeDtypeStruct((heads, 2, tokens, tokens), bf16),
        ),
        grid_spec=pltpu.PrefetchScalarGridSpec(
            num_scalar_prefetch=1,
            grid=(heads // pair,),
            in_specs=[one, two, two],
            out_specs=(
                one,
                pl.BlockSpec((pair, 2, tokens, tokens), lambda s, info: (s, 0, 0, 0)),
            ),
            scratch_shapes=[pltpu.VMEM((2, tokens, tokens), f32)],
        ),
        compiler_params=params(),
        cost_estimate=cost(22),
        name="attend",
    )(info, q, own, par)


def middle_kernel(info_ref, o_ref, w_ref, x_ref, wq_ref, gain_ref, bias_ref, x2_ref, c_ref, q_ref):
    x2 = x_ref[...] + dot(o_ref[0], whole_weight(w_ref, info_ref), NT)
    x2_ref[...] = x2
    c = (normed(x2)[0] * gain_ref[2:3] + bias_ref[2:3]).astype(bf16)
    c_ref[...] = c

    def store(at, y):
        q_ref[0, :, pl.ds(at, wq_ref[0].shape[4])] = (y * HEAD_DIM**-0.5).astype(bf16)

    project(c, wq_ref, info_ref, store)


def middle(info, o, weights, x1, gains, biases):
    _, tokens, width = o.shape
    row = full((tokens, width))
    return call(
        middle_kernel,
        info,
        (1,),
        [
            (o, full(o.shape)),
            (weights, weight_specs(weights, lambda s: 0)),
            (x1, row),
            (weights, weight_specs(weights, lambda s: 1)),
            (gains, full(gains.shape)),
            (biases, full(biases.shape)),
        ],
        [
            (jax.ShapeDtypeStruct((tokens, width), f32), row),
            (jax.ShapeDtypeStruct((tokens, width), bf16), row),
            (jax.ShapeDtypeStruct((1, tokens, width), bf16), full((1, tokens, width))),
        ],
        cost_estimate=cost(9),
        name="middle",
    )


def feed_kernel(
    info_ref,
    o_ref,
    wo_ref,
    x_ref,
    w1_ref,
    w2_ref,
    gain_ref,
    bias_ref,
    x3_ref,
    f_ref,
    g_ref,
    slope_ref,
    x4_ref,
):
    step = pl.program_id(0)

    @pl.when(step == 0)
    def _():
        x3 = x_ref[...] + dot(o_ref[0], whole_weight(wo_ref, info_ref), NT)
        x3_ref[...] = x3
        f_ref[...] = (normed(x3)[0] * gain_ref[3:4] + bias_ref[3:4]).astype(bf16)
        x4_ref[...] = x3

    def store(at, u):
        bell = 0.5 + 0.5 * lax.erf(u * 0.7071067811865476)
        lanes = pl.ds(at, w1_ref[0].shape[4])
        g_ref[0, :, lanes] = (u * bell).astype(bf16)
        slope = bell + u * (0.3989422804014327 * jnp.exp(-0.5 * u * u))
        slope_ref[0, :, lanes] = slope.astype(bf16)

    project(f_ref[...], w1_ref, info_ref, store)
    x4_ref[...] += dot(g_ref[0], whole_weight(w2_ref, info_ref), NT)


def feed(info, o, wo, x2, w1, w2, gains, biases, slabs):
    _, tokens, width = o.shape
    blocks = slabs
    row = full((tokens, width))
    part = pl.BlockSpec((1, tokens, width), lambda s, info: (s, 0, 0))
    wide = jax.ShapeDtypeStruct((tokens, width), f32)
    slim = jax.ShapeDtypeStruct((tokens, width), bf16)
    many = jax.ShapeDtypeStruct((blocks, tokens, width), bf16)
    return call(
        feed_kernel,
        info,
        (blocks,),
        [
            (o, full(o.shape)),
            (wo, weight_specs(wo, lambda s: 2)),
            (x2, row),
            (w1, weight_specs(w1, lambda s: s)),
            (w2, weight_specs(w2, lambda s: s)),
            (gains, full(gains.shape)),
            (biases, full(biases.shape)),
        ],
        [(wide, row), (slim, row), (many, part), (many, part), (wide, row)],
        mib=60,
        cost_estimate=cost(28),
        name="feed",
    )


def feed_back_kernel(
    info_ref,
    x4_ref,
    og_a,
    og_b,
    slope_ref,
    w1_ref,
    w2_ref,
    x3_ref,
    wo_ref,
    gain_ref,
    bias_ref,
    hid_a,
    hid_b,
    g4b_ref,
    du_ref,
    g3_ref,
    g3b_ref,
    do_ref,
    sums_ref,
    total,
):
    step = pl.program_id(0)

    @pl.when(step == 0)
    def _():
        x4 = x4_ref[...]
        half = og_a.shape[0]
        hidden = normed(x4)[0] * gain_ref[4:5] + bias_ref[4:5]
        put_slots((hid_a, hid_b), info_ref, (hidden[:half], hidden[half:]))
        out_grad = jnp.concatenate(slots((og_a, og_b), info_ref), axis=0).astype(f32)
        g4, gain_grad, bias_grad = norm_back(x4, gain_ref[4:5], out_grad)
        g3_ref[...] = g4
        g4b_ref[...] = g4.astype(bf16)
        sums_ref[2:3] = gain_grad
        sums_ref[3:4] = bias_grad

    def store(at, y):
        lanes = pl.ds(at, w2_ref[0].shape[4])
        du_ref[0, :, lanes] = (y * slope_ref[0, :, lanes].astype(f32)).astype(bf16)

    project(g4b_ref[...], w2_ref, info_ref, store)
    part = dot(du_ref[0], whole_weight(w1_ref, info_ref), NT)

    @pl.when(step == 0)
    def _():
        total[...] = part

    @pl.when(step > 0)
    def _():
        total[...] += part

    @pl.when(step == pl.num_programs(0) - 1)
    def _():
        back, gain_grad, bias_grad = norm_back(x3_ref[...], gain_ref[3:4], total[...])
        g3 = g3_ref[...] + back
        g3_ref[...] = g3
        g3b = g3.astype(bf16)
        g3b_ref[...] = g3b
        sums_ref[0:1] = gain_grad
        sums_ref[1:2] = bias_grad

        def keep(at, y):
            do_ref[0, :, pl.ds(at, wo_ref[0].shape[4])] = y.astype(bf16)

        project(g3b, wo_ref, info_ref, keep)


def feed_back(info, x4, og, slope, wo, x3, w1, w2, gains, biases):
    blocks, tokens, width = slope.shape
    row = full((tokens, width))
    part_row = full((tokens // 2, width))
    part_shape = jax.ShapeDtypeStruct((tokens // 2, width), bf16)
    part = pl.BlockSpec((1, tokens, width), lambda s, info: (s, 0, 0))
    wide = jax.ShapeDtypeStruct((tokens, width), f32)
    slim = jax.ShapeDtypeStruct((tokens, width), bf16)
    return call(
        feed_back_kernel,
        info,
        (blocks,),
        [
            (x4, row),
            (og[0], part_row),
            (og[1], part_row),
            (slope, part),
            (w1, weight_specs(w1, lambda s: s)),
            (w2, weight_specs(w2, lambda s: s)),
            (x3, row),
            (wo, weight_specs(wo, lambda s: 2)),
            (gains, full(gains.shape)),
            (biases, full(biases.shape)),
        ],
        [
            (part_shape, part_row),
            (part_shape, part_row),
            (slim, row),
            (jax.ShapeDtypeStruct((blocks, tokens, width), bf16), part),
            (wide, row),
            (slim, row),
            (jax.ShapeDtypeStruct((1, tokens, width), bf16), full((1, tokens, width))),
            (jax.ShapeDtypeStruct((4, width), f32), full((4, width))),
        ],
        [pltpu.VMEM((tokens, width), f32)],
        60,
        cost_estimate=cost(28),
        name="feed_back",
    )


def attend_back_kernel(
    q_ref, own_ref, par_ref, p_ref, o_ref, do_ref, dq_ref, down_ref, dpar_ref
):
    flat = do_ref[0].astype(f32).T * o_ref[0].astype(f32).T
    outs = []
    for h in range(LANES // HEAD_DIM):
        lanes = slice(h * HEAD_DIM, (h + 1) * HEAD_DIM)
        q = q_ref[0][:, lanes]
        grad = do_ref[0][:, lanes]
        inner = jnp.sum(flat[lanes], axis=0, keepdims=True)
        back = None
        for i, (kv_ref, d_ref) in enumerate(((own_ref, down_ref), (par_ref, dpar_ref))):
            keys = kv_ref[0][:, lanes]
            probs = p_ref[h, i]
            d_probs = dot(kv_ref[1][:, lanes], grad, NT)
            d_scores = (probs.astype(f32) * (d_probs - inner)).astype(bf16)
            d_ref[1, :, lanes] = dot(probs, grad).astype(bf16)
            d_ref[0, :, lanes] = dot(d_scores, q).astype(bf16)
            some = dot(keys, d_scores, TN)
            back = some if back is None else back + some
        outs.append(back)
    dq_ref[0] = (jnp.concatenate(outs, axis=0).T * HEAD_DIM**-0.5).astype(bf16)


def attend_back(q, own, par, probs, o, do):
    _, tokens, width = q.shape
    heads = width // HEAD_DIM
    pair = LANES // HEAD_DIM
    one = pl.BlockSpec((1, tokens, LANES), lambda s: (0, 0, s))
    two = pl.BlockSpec((2, tokens, LANES), lambda s: (0, 0, s))
    kv = jax.ShapeDtypeStruct((2, tokens, width), bf16)
    return pl.pallas_call(
        attend_back_kernel,
        out_shape=(jax.ShapeDtypeStruct((1, tokens, width), bf16), kv, kv),
        grid=(heads // pair,),
        in_specs=[
            one,
            two,
            two,
            pl.BlockSpec((pair, 2, tokens, tokens), lambda s: (s, 0, 0, 0)),
            one,
            one,
        ],
        out_specs=(one, two, two),
        compiler_params=params(),
        cost_estimate=cost(21),
        name="attend_back",
    )(q, own, par, probs, o, do)


def middle_back_kernel(
    info_ref, dq_ref, wq_ref, x2_ref, g3_ref, wo_ref, gain_ref, g2_ref, g2b_ref, do_ref, sums_ref
):
    d_normed = dot(dq_ref[0], whole_weight(wq_ref, info_ref), NT)
    back, gain_grad, bias_grad = norm_back(x2_ref[...], gain_ref[2:3], d_normed)
    g2 = g3_ref[...] + back
    g2_ref[...] = g2
    g2b = g2.astype(bf16)
    g2b_ref[...] = g2b
    sums_ref[0:1] = gain_grad
    sums_ref[1:2] = bias_grad

    def keep(at, y):
        do_ref[0, :, pl.ds(at, wo_ref[0].shape[4])] = y.astype(bf16)

    project(g2b, wo_ref, info_ref, keep)


def middle_back(info, dq, weights, x2, g3, gains):
    _, tokens, width = dq.shape
    row = full((tokens, width))
    return call(
        middle_back_kernel,
        info,
        (1,),
        [
            (dq, full(dq.shape)),
            (weights, weight_specs(weights, lambda s: 1)),
            (x2, row),
            (g3, row),
            (weights, weight_specs(weights, lambda s: 0)),
            (gains, full(gains.shape)),
        ],
        [
            (jax.ShapeDtypeStruct((tokens, width), f32), row),
            (jax.ShapeDtypeStruct((tokens, width), bf16), row),
            (jax.ShapeDtypeStruct((1, tokens, width), bf16), full((1, tokens, width))),
            (jax.ShapeDtypeStruct((2, width), f32), full((2, width))),
        ],
        cost_estimate=cost(10),
        name="middle_back",
    )


def source_back_kernel(info_ref, mine_ref, came_ref, w_ref, out_a, out_b, sum_ref, total):
    step = pl.program_id(0)
    grads = (mine_ref[0].astype(f32) + came_ref[0].astype(f32)).astype(bf16)
    sum_ref[0] = grads
    part = dot(grads, whole_weight(w_ref, info_ref), NT)

    @pl.when(step == 0)
    def _():
        total[...] = part

    @pl.when(step == pl.num_programs(0) - 1)
    def _():
        half = out_a.shape[0]
        both = total[...] + part
        put_slots((out_a, out_b), info_ref, (both[:half], both[half:]))


def source_back(info, mine, came, weights):
    parts, tokens, width = mine.shape
    part = pl.BlockSpec((1, tokens, width), lambda s, info: (s, 0, 0))
    return call(
        source_back_kernel,
        info,
        (parts,),
        [(mine, part), (came, part), (weights, weight_specs(weights, lambda s: s))],
        [
            (jax.ShapeDtypeStruct((tokens // 2, width), bf16), full((tokens // 2, width))),
            (jax.ShapeDtypeStruct((tokens // 2, width), bf16), full((tokens // 2, width))),
            (jax.ShapeDtypeStruct((parts, tokens, width), bf16), part),
        ],
        [pltpu.VMEM((tokens, width), f32)],
        cost_estimate=cost(7),
        name="source_back",
    )


def exit_kernel(
    info_ref,
    dq_ref,
    mine_ref,
    came_ref,
    wq_ref,
    wkv_ref,
    x1_ref,
    x0_ref,
    g2_ref,
    gain_ref,
    g0_ref,
    sum_ref,
    sums_ref,
    total,
):
    step = pl.program_id(0)

    @pl.when(step == 0)
    def _():
        total[...] = dot(dq_ref[0], whole_weight(wq_ref, info_ref), NT)

    @pl.when(step > 0)
    def _():
        grads = (mine_ref[0].astype(f32) + came_ref[0].astype(f32)).astype(bf16)
        sum_ref[0] = grads
        total[...] += dot(grads, whole_weight(wkv_ref, info_ref), NT)

    @pl.when(step == pl.num_programs(0) - 1)
    def _():
        back, gain_one, bias_one = norm_back(x1_ref[...], gain_ref[1:2], total[...])
        g1 = g2_ref[...] + back
        g0, gain_zero, bias_zero = norm_back(x0_ref[...], gain_ref[0:1], g1)
        g0_ref[...] = g0.T.astype(bf16)
        sums_ref[0:1] = gain_zero
        sums_ref[1:2] = bias_zero
        sums_ref[2:3] = gain_one
        sums_ref[3:4] = bias_one


def exit_back(info, dq, mine, came, first, x1, x0, g2, gains):
    _, tokens, width = dq.shape
    wq, wkv = first
    row = full((tokens, width))
    part = pl.BlockSpec((1, tokens, width), lambda s, info: (jnp.maximum(s - 1, 0), 0, 0))
    return call(
        exit_kernel,
        info,
        (3,),
        [
            (dq, full(dq.shape)),
            (mine, part),
            (came, part),
            (wq, weight_specs(wq, lambda s: 1)),
            (wkv, weight_specs(wkv, lambda s: jnp.maximum(s - 1, 0))),
            (x1, row),
            (x0, row),
            (g2, row),
            (gains, full(gains.shape)),
        ],
        [
            (jax.ShapeDtypeStruct((width, tokens), bf16), full((width, tokens))),
            (jax.ShapeDtypeStruct((2, tokens, width), bf16), part),
            (jax.ShapeDtypeStruct((4, width), f32), full((4, width))),
        ],
        [pltpu.VMEM((tokens, width), f32)],
        cost_estimate=cost(15),
        name="exit_back",
    )


def weight_grad_kernel(chips, aliased, info_ref, xo_ref, xp_ref, yo_ref, yp_ref, *refs):
    out_ref, turned = refs[-2], refs[-1]
    tokens, width = xo_ref.shape
    rows = width // (chips * CORES)
    core = info_ref[0]

    @pl.when(pl.program_id(0) == 0)
    def _():
        for i, x_ref in enumerate((xo_ref, xp_ref)):
            at = slice(i * tokens, (i + 1) * tokens)
            if rows % LANES == 0:
                for j in range(chips):
                    lanes = pl.ds(pl.multiple_of((2 * j + core) * rows, rows), rows)
                    turned[j * rows : (j + 1) * rows, at] = x_ref[:, lanes].astype(f32).T.astype(bf16)
            else:
                tall = x_ref[...].astype(f32).T.reshape(chips, CORES, rows, tokens)
                mine = jnp.where(core == 0, tall[:, 0], tall[:, 1])
                turned[:, at] = mine.reshape(chips * rows, tokens).astype(bf16)

    y_own, y_par = yo_ref[0], yp_ref[0]
    blocks, span = out_ref.shape[1], out_ref.shape[4]
    result = dot(turned[:, :tokens], y_own) + dot(turned[:, tokens:], y_par)
    for m in range(blocks):
        part = result[:, m * span : (m + 1) * span].astype(bf16)
        out_ref[:, m, 0] = part.reshape(chips, rows, span)


def weight_grad(info, x_own, x_par, y_own, y_par, shape, at, before=None):
    parts, tokens, width = y_own.shape
    chips = shape[0]
    row = full(x_own.shape)
    part = pl.BlockSpec((1, tokens, width), lambda s, info: (s, 0, 0))
    extra = [] if before is None else [before]
    return pl.pallas_call(
        functools.partial(weight_grad_kernel, chips, before is not None),
        out_shape=jax.ShapeDtypeStruct(shape, bf16),
        grid_spec=pltpu.PrefetchScalarGridSpec(
            num_scalar_prefetch=1,
            grid=(parts,),
            in_specs=[row, row, part, part] + [pl.BlockSpec(memory_space=pl.ANY) for _ in extra],
            out_specs=pl.BlockSpec(
                (chips, shape[1], 1, shape[3], shape[4]), lambda s, info: (0, 0, s + at, 0, 0)
            ),
            scratch_shapes=[pltpu.VMEM((x_own.shape[1] // 2, 2 * tokens), bf16)],
        ),
        input_output_aliases={} if before is None else {5: 0},
        compiler_params=params(),
        cost_estimate=cost(3 + 2 * parts),
        name="weight_grad",
    )(info, x_own, x_par, y_own, y_par, *extra)


def swap(value):
    return lax.ppermute(value, "core", [(0, 1), (1, 0)])


def line_moves(mp):
    rounds = []
    for turn in range(2):
        moves = []
        for c in range(CORES):
            for m in range(mp):
                target, slot = (1 if m in (1, 2) else 0), m // 2
                moves.append((c * mp + m, target * mp + 2 * c + (slot ^ turn)))
        rounds.append(moves)
    return rounds


def to_chips(value, mp):
    slot = lax.axis_index("mp") // 2
    return [
        lax.ppermute(jnp.where((slot ^ turn) == 0, value[0], value[1]), LINE, moves)
        for turn, moves in enumerate(line_moves(mp))
    ]


def from_chips(pair, mp):
    return [
        lax.ppermute(sent, LINE, [(b, a) for a, b in moves])
        for sent, moves in zip(pair, line_moves(mp))
    ]


def placed_again(came):
    slot = lax.axis_index("mp") // 2
    one, two = [c.astype(f32) for c in came]
    return jnp.stack([jnp.where(slot == 0, one, two), jnp.where(slot == 0, two, one)])


def packed(*weights):
    return jnp.concatenate([w.reshape(-1, w.shape[-1]) for w in weights], axis=0)


X_SWAP = [(0, 1), (1, 0), (2, 3), (3, 2)]
Y_SWAP = [(0, 2), (2, 0), (1, 3), (3, 1)]
def gathered(rows, unit, chips, mp):
    value = lax.all_gather(rows, ALL, axis=0, tiled=False)
    return value.reshape(chips * CORES, mp, -1, unit, rows.shape[-1])


def gathered_line(rows, unit, mp):
    value = lax.all_gather(rows, "mp", axis=0, tiled=False)
    return value.reshape(mp, -1, unit, rows.shape[-1])


class Spread:
    def __init__(self, value, cut):
        self.own, self.cut = [value], cut
        self.near, self.far, self.both = [], [], []
        self.swapped = {}

    def begin(self, *others):
        self.own = tied(self.own, *others)
        sets = [self.own[0][:, : self.cut], self.own[0][:, self.cut :]]
        self.near = [lax.ppermute(w, "chip", p) for w, p in zip(sets, (X_SWAP, Y_SWAP))]
        self.far = [lax.ppermute(w, "chip", p) for w, p in zip(sets, (Y_SWAP, X_SWAP))]

    def finish(self, *others):
        self.near = tied(self.near, *others)
        self.both = [lax.ppermute(w, "chip", p) for w, p in zip(self.near, (Y_SWAP, X_SWAP))]

    def swap(self, *names):
        for name in names:
            self.swapped[name] = [swap(w) for w in getattr(self, name)]

    def hold(self, *others):
        state = [self.own, self.near, self.far, self.both, self.swapped]
        state, others = lax.optimization_barrier((state, others))
        self.own, self.near, self.far, self.both, self.swapped = state
        return others if len(others) > 1 else others[0]

    def pieces(self):
        found = []
        for i in range(2):
            pieces = []
            for name in ("own", "near", "far", "both") if i == 0 else ("own", "far", "near", "both"):
                at, skip = (0, i * self.cut) if name == "own" else (i, 0)
                for group in (getattr(self, name), self.swapped[name]):
                    pieces.append((group[at][None], skip))
            found.append(pieces)
        return found


def tied(value, *others):
    return after(value, *others) if others else value


def scattered(grads, axis):
    return lax.psum_scatter(grads, axis, scatter_dimension=0, tiled=False)


def sent_over(grads, axis, size):
    me = lax.axis_index(axis)
    terms = []
    for k in range(size):
        if axis == "chip" and size == 4:
            to, perm = me ^ k, [(i, i ^ k) for i in range(size)]
        else:
            to, perm = (me + k) % size, [(i, (i + k) % size) for i in range(size)]
        part = lax.dynamic_index_in_dim(grads, to, axis=0, keepdims=False)
        terms.append(part if k == 0 else lax.ppermute(part, axis, perm))
    return terms


def summed(terms):
    return sum([t.astype(f32) for t in terms[1:]], start=terms[0].astype(f32))


def total_over(value, axis, size):
    terms = [
        lax.ppermute(value, axis, [(i, (i + k) % size) for i in range(size)])
        for k in range(1, size)
    ]
    return sum(terms, start=value)


def after(value, *others):
    return lax.optimization_barrier((value, others))[0]


def body(
    chips,
    mp,
    target_ids,
    tgt_lengths,
    encoder_states,
    src_lengths,
    table,
    pos_table,
    self_query_key_value_weight,
    self_output_weight,
    cross_query_weight,
    cross_key_value_weight,
    cross_output_weight,
    feedforward_input_weight,
    feedforward_output_weight,
    norm_gains,
    norm_biases,
    out_grad,
):
    dp = chips * CORES
    n = dp * mp
    seqs, block = target_ids.shape
    assert seqs * CORES == mp == 4
    tokens = seqs * block
    width = norm_gains.shape[1]
    vocab = table.shape[1]
    feats = table.shape[0]
    rows = pos_table.shape[0]
    core, m, chip = lax.axis_index("core"), lax.axis_index("mp"), lax.axis_index("chip")

    def split(weight):
        return weight.reshape(rows, -1, block).transpose(1, 0, 2)

    own_ids = jnp.broadcast_to(target_ids.reshape(1, tokens), (n, tokens))
    all_ids = lax.all_to_all(own_ids, ALL, split_axis=0, concat_axis=0, tiled=True)
    sub = feedforward_input_weight.shape[1] // block
    first = packed(pos_table, split(self_query_key_value_weight))
    second = packed(
        self_output_weight, cross_query_weight, split(cross_key_value_weight), cross_output_weight
    )
    third = packed(split(feedforward_input_weight), split(feedforward_output_weight))
    sub = feedforward_input_weight.shape[1] // block
    late = gathered(jnp.concatenate([second, third]), rows, chips, mp)
    second = [(late, 0)], [(late, 2)]
    third = [(late, 5)], [(late, 5 + sub)]
    stepped = chips == 4
    if stepped:
        copies = jnp.broadcast_to(first[None], (mp,) + first.shape)
        copies = lax.all_to_all(after(copies, all_ids), "mp", split_axis=0, concat_axis=0, tiled=True)
        first = Spread(copies.reshape(mp, -1, rows, block), 2)
    else:
        first = gathered(first, rows, chips, mp)
        first = [(first, 0)], [(first, 2)]

    lengths = jnp.stack([tgt_lengths, src_lengths])
    other = swap(lengths)
    lengths = jnp.where(
        core == 0,
        jnp.concatenate([lengths, other], axis=1),
        jnp.concatenate([other, lengths], axis=1),
    )
    lengths = lax.dynamic_index_in_dim(lengths, m, axis=1, keepdims=False)
    info = jnp.stack(
        [
            core,
            lengths[0],
            lengths[1],
            core,
            3 - core,
            1 - core,
            2 + core,
            chip % 2,
            chip // 2,
            m % 2,
        ]
    ).astype(i32)

    ids = all_ids.reshape(chips, CORES, mp, seqs, block)
    ids = jnp.stack([ids[:, :, 0], ids[:, :, 3], ids[:, :, 1], ids[:, :, 2]], axis=2)
    ids = ids.reshape(chips, CORES, CORES, 2, seqs, block).transpose(0, 2, 1, 4, 3, 5)
    ids = ids.reshape(n, 1, tokens)
    height = vocab // (LANES // feats)
    row, group = ids % height, ids // height
    flat_row = row.reshape(-1)

    picked = gather_tokens(table, flat_row, group)
    if stepped:
        picked = first.hold(picked)
        first.begin(picked)
        first.finish()
        first.swap("own", "near", "far", "both")
        first = first.pieces()
    emb = lax.all_to_all(picked, ALL, split_axis=0, concat_axis=0, tiled=True)
    emb = emb.reshape(width, tokens)

    x0, x1, a, q, kv = entry(info, emb, first, norm_gains, norm_biases)
    states = to_chips(after(encoder_states, a), mp)
    kv_par = swap(kv)
    outs = attend(info, q, kv, kv_par, True)
    (o, probs), states = lax.optimization_barrier((outs, states))
    states, ckv = source_keys(info, states, second[1])
    ckv_par = swap(ckv)
    x2, c, cq = middle(info, after(o, ckv), second[0], x1, norm_gains, norm_biases)
    oc, cprobs = attend(info, cq, ckv, ckv_par, False)
    og = to_chips(after(out_grad.astype(bf16), oc), mp)
    w1, w2 = third
    oc_par, c_par = swap(oc), swap(after(c, oc))
    outs = feed(info, oc, second[1], x2, w1, w2, norm_gains, norm_biases, sub)
    (x3, f, g, slope, x4), og, oc_par, c_par = lax.optimization_barrier((outs, og, oc_par, c_par))
    f_par, g_par = swap(f), swap(g)
    a_par, o_par, states_par = [swap(after(v, x4)) for v in (a, o, states)]
    outs = feed_back(info, x4, og, slope, second[1], x3, w1, w2, norm_gains, norm_biases)
    outs, f_par, g_par, a_par, o_par, states_par = lax.optimization_barrier(
        (outs, f_par, g_par, a_par, o_par, states_par)
    )
    *hid, g4b, du, g3, g3b, doc, sums34 = outs
    g4b_par, g3b_par, du_par = swap(g4b), swap(g3b), swap(du)
    hidden_out = from_chips(tied(hid, g4b_par), mp)
    shape = (chips, mp, sub, rows, block)
    grads = weight_grad(info, g4b, g4b_par, g, g_par, shape, 0)
    part_one = scattered(grads, "chip")
    shape = (chips, mp, sub + 1, rows, block)
    grads = weight_grad(info, after(g3b, grads), g3b_par, oc, oc_par, shape, sub)
    grads = weight_grad(info, after(f, grads), f_par, du, du_par, shape, 0, grads)
    doc, hidden_out = lax.optimization_barrier((after(doc, grads), hidden_out))

    outs = attend_back(cq, ckv, ckv_par, cprobs, oc, doc)
    (dcq, dckv_own, dckv_par), part_one = lax.optimization_barrier((outs, part_one))
    part_one = scattered(part_one, "mp")
    hidden_out = placed_again(hidden_out)
    dckv_came, dcq_par = swap(dckv_par), swap(dcq)
    outs = middle_back(info, dcq, second[0], x2, g3, norm_gains)
    (g2, g2b, do, sums2), dckv_came, dcq_par, dckv_own = lax.optimization_barrier(
        (outs, dckv_came, dcq_par, dckv_own)
    )
    g2b_par = swap(g2b)
    outs = source_back(info, dckv_own, dckv_came, second[1])
    outs, part_one = lax.optimization_barrier((outs, part_one))
    part_two = scattered(after(grads, part_one), "chip")
    *enc_grad, dckv = outs
    dckv_after = swap(dckv)
    shape = (chips, mp, 4, rows, block)
    grads = weight_grad(info, c, c_par, after(dcq, dckv), dcq_par, shape, 0)
    grads = weight_grad(info, g2b, g2b_par, o, o_par, shape, 1, grads)
    grads = weight_grad(info, states, states_par, dckv, dckv_after, shape, 2, grads)
    do = after(do, grads)
    cross_terms = lax.all_to_all(grads, "chip", split_axis=0, concat_axis=0, tiled=True)
    encoder_grad = from_chips(tied(enc_grad, grads), mp)

    outs = attend_back(q, kv, kv_par, probs, o, do)
    (dq, dkv_own, dkv_par), encoder_grad = lax.optimization_barrier((outs, encoder_grad))
    dkv_came = swap(dkv_par)
    dq_par = swap(dq)
    outs = exit_back(info, dq, dkv_own, dkv_came, first, x1, x0, g2, norm_gains)
    (g0, dkv, sums01), dq_par, cross_terms = lax.optimization_barrier((outs, dq_par, cross_terms))
    sent = g0.reshape(n, feats, tokens)
    arrived = lax.all_to_all(sent, ALL, split_axis=0, concat_axis=0, tiled=True)
    encoder_grad = placed_again(encoder_grad)
    cross_part = jnp.sum(cross_terms.astype(f32), axis=0).astype(bf16)
    sums = jnp.concatenate((sums01, sums2, sums34), axis=0)
    sums_par = swap(sums)
    shape = (chips, mp, 3, rows, block)
    dkv_after = swap(dkv)
    grads = weight_grad(info, a, a_par, dq, dq_par, shape, 0)
    grads, sums_par = lax.optimization_barrier((grads, sums_par))
    sums = total_over(sums + sums_par, "chip", chips)
    grads = weight_grad(info, a, a_par, dkv, dkv_after, shape, 1, grads)
    sums, grads, arrived, part_two = lax.optimization_barrier((sums, grads, arrived, part_two))
    sums_up = scattered(jnp.concatenate([part_two, cross_part], axis=1), "mp")
    self_terms = lax.all_to_all(grads, "chip", split_axis=0, concat_axis=0, tiled=True)
    sums = total_over(sums, "mp", mp)

    outs = scatter_tokens(arrived, flat_row, row, group, vocab, mp)
    (table_grad, places), self_terms, sums = lax.optimization_barrier((outs, self_terms, sums))
    self_part = jnp.sum(self_terms.astype(f32), axis=0).astype(bf16)
    self_grads = summed(sent_over(self_part, "mp", mp))
    sums_up = sums_up.astype(f32)
    feed_out_grads = part_one.astype(f32)
    feed_in_grads, cross_grads = sums_up[: sub + 1], sums_up[sub + 1 :]

    blocks = places.reshape(CORES, feats, 2, block).transpose(0, 2, 1, 3).reshape(4, feats, block)
    blocks = jnp.stack([blocks[0], blocks[2], blocks[3], blocks[1]])
    parts = []
    for k in range(mp):
        mine = lax.dynamic_index_in_dim(blocks, (m + k) % mp, axis=0, keepdims=False)
        parts.append(
            mine if k == 0 else lax.ppermute(mine, "mp", [(i, (i + k) % mp) for i in range(mp)])
        )
    pos_grad = []
    for source in range(mp):
        value = parts[0]
        for k in range(1, mp):
            value = jnp.where((m - source) % mp == k, parts[k], value)
        pos_grad.append(value)
    pos_grad = jnp.concatenate(pos_grad, axis=0)

    def join(parts):
        return parts.transpose(1, 0, 2)

    return (
        hidden_out,
        table_grad,
        pos_grad,
        join(self_grads),
        cross_grads[1],
        cross_grads[0],
        join(cross_grads[2:4]),
        feed_in_grads[sub],
        join(feed_in_grads[:sub]).reshape(rows, -1),
        join(feed_out_grads).reshape(rows, -1),
        sums[0::2],
        sums[1::2],
        encoder_grad,
    )


def solution(mesh):
    dp, mp = mesh.devices.shape
    chips = dp // CORES
    fine = Mesh(mesh.devices.reshape(chips, CORES, mp), ALL)
    both = ("chip", "core")
    placed = (
        P(both, "mp"),
        P(both),
        P(both, "mp", None),
        P(both),
        P(ALL, None),
        P(both, "mp"),
        P(both, None, "mp"),
        P(both, "mp"),
        P(both, "mp"),
        P(both, None, "mp"),
        P(both, "mp"),
        P(both, "mp"),
        P(both, "mp"),
        P(),
        P(),
        P(both, "mp", None),
    )
    return jax.shard_map(
        functools.partial(body, chips, mp),
        mesh=fine,
        in_specs=placed,
        out_specs=(
            P(both, "mp", None),
            P(ALL, None),
            P(both, "mp"),
            P(both, None, "mp"),
            P(both, "mp"),
            P(both, "mp"),
            P(both, None, "mp"),
            P(both, "mp"),
            P(both, "mp"),
            P(both, "mp"),
            P(),
            P(),
            P(both, "mp", None),
        ),
        check_vma=False,
    )
```

```python
import functools

import jax
import jax.numpy as jnp
from jax import lax
from jax.experimental import pallas as pl
from jax.experimental.pallas import tpu as pltpu
from jax.sharding import Mesh
from jax.sharding import PartitionSpec as P

HEAD_DIM = 64
EPSILON = 1e-05
NEGATIVE = -1e30
LANES = 128
ALL = ("chip", "core", "mp")
LINE = ("core", "mp")
CORES = 2

f32 = jnp.float32
bf16 = jnp.bfloat16
i32 = jnp.int32

NT = (((1,), (1,)), ((), ()))
NN = (((1,), (0,)), ((), ()))
TN = (((0,), (0,)), ((), ()))


def dot(a, b, dims=NN):
    return lax.dot_general(a, b, dims, preferred_element_type=f32)


def params(mib=56):
    return pltpu.CompilerParams(vmem_limit_bytes=mib << 20)


def cost(microseconds):
    return pl.CostEstimate(flops=0, bytes_accessed=int(microseconds * 3.2e6), transcendentals=0)


def normed(values):
    centred = values - jnp.mean(values, axis=-1, keepdims=True)
    inverse = lax.rsqrt(jnp.mean(centred * centred, axis=-1, keepdims=True) + EPSILON)
    return centred * inverse, inverse


def norm_back(values, gain, grad):
    hat, inverse = normed(values)
    scaled = grad * gain
    first = jnp.mean(scaled, axis=-1, keepdims=True)
    second = jnp.mean(scaled * hat, axis=-1, keepdims=True)
    back = inverse * (scaled - first - hat * second)
    gain_grad = jnp.sum(grad * hat, axis=0, keepdims=True)
    bias_grad = jnp.sum(grad, axis=0, keepdims=True)
    return back, gain_grad, bias_grad


def in_order(pieces, info_ref):
    for bit, place in ((0, 0), (1, 7), (2, 8)):
        far = info_ref[place] == 1
        turned = []
        for i, piece in enumerate(pieces):
            turned.append(jnp.where(far, pieces[i ^ (1 << bit)], piece))
        pieces = turned
    return pieces


def joined(blocks, info_ref):
    flat = [b.reshape(-1, b.shape[-1]) for b in blocks]
    return flat[0] if len(flat) == 1 else jnp.concatenate(in_order(flat, info_ref), axis=0)


def columns(w_refs, m, info_ref):
    return joined([w[:, pl.ds(m, 1)] for w in w_refs], info_ref)


def whole_weight(w_refs, info_ref):
    parts = [columns(w_refs, m, info_ref) for m in range(w_refs[0].shape[1])]
    return jnp.concatenate(parts, axis=1)


def project(x, w_refs, info_ref, store):
    width = w_refs[0].shape[4]

    def step(m, carry):
        store(pl.multiple_of(m * width, width), dot(x, columns(w_refs, m, info_ref)))
        return carry

    lax.fori_loop(0, w_refs[0].shape[1], step, 0)


def weight_specs(weights, index):
    return [
        pl.BlockSpec(
            (w.shape[0], w.shape[1], 1, w.shape[3], w.shape[4]),
            lambda s, info, skip=skip: (0, 0, index(s) + skip, 0, 0),
        )
        for w, skip in weights
    ]


def call(kernel, info, grid, operands, outs, scratch=(), mib=56, **others):
    arrays, specs, sizes = [], [], []
    for value, spec in operands:
        group = isinstance(value, (list, tuple))
        sizes.append(len(value) if group else None)
        arrays.extend([w for w, _ in value] if group else [value])
        specs.extend(spec if group else [spec])

    def body(info_ref, *refs):
        given, rest, at = [], refs, 0
        for size in sizes:
            given.append(refs[at] if size is None else list(refs[at : at + size]))
            at += 1 if size is None else size
        kernel(info_ref, *given, *rest[at:])

    return pl.pallas_call(
        body,
        out_shape=[o for o, _ in outs],
        grid_spec=pltpu.PrefetchScalarGridSpec(
            num_scalar_prefetch=1,
            grid=grid,
            in_specs=specs,
            out_specs=[o for _, o in outs],
            scratch_shapes=list(scratch),
        ),
        compiler_params=params(mib),
        **others,
    )(info, *arrays)


def full(shape):
    return pl.BlockSpec(shape, lambda *a: (0,) * len(shape))


def gather_kernel(groups, fill, rows_ref, group_ref, *refs):
    tables, out_ref, turned, picked = refs[:groups], refs[groups], refs[-2], refs[-1]
    step = pl.program_id(0)
    feats, width = tables[0].shape
    tokens = picked.shape[0]

    @pl.when(step < fill)
    def _():
        stacked = jnp.concatenate([t[...].astype(f32) for t in tables], axis=0).astype(bf16)
        row = lax.broadcasted_iota(i32, (256, 256), 0)
        eye = jnp.where(row == lax.broadcasted_iota(i32, (256, 256), 1), 1.0, 0.0).astype(bf16)
        for k in range(width // 256):
            at = pl.multiple_of(step * width + k * 256, 256)
            turned[pl.ds(at, 256), :] = dot(eye, stacked[:, k * 256 : (k + 1) * 256], NT)

    @pl.when(step >= fill)
    def _():
        base = (step - fill) * tokens

        def some(k, carry):
            for u in range(16):
                t = k * 16 + u
                picked[pl.ds(t, 1), :] = turned[pl.ds(rows_ref[base + t], 1), :]
            return carry

        lax.fori_loop(0, tokens // 16, some, 0)
        row = lax.broadcasted_iota(i32, (LANES, LANES), 0)
        eye = jnp.where(row == lax.broadcasted_iota(i32, (LANES, LANES), 1), 1.0, 0.0)
        across = dot(eye.astype(bf16), picked[...].astype(bf16), NT)
        own = lax.broadcasted_iota(i32, (LANES, tokens), 0) // feats == group_ref[0]
        kept = jnp.where(own, across, 0.0)
        total = kept[:feats]
        for g in range(1, groups):
            total = total + kept[g * feats : (g + 1) * feats]
        out_ref[0] = total.astype(out_ref.dtype)


def gather_tokens(table, rows, group):
    feats, vocab = table.shape
    groups = LANES // feats
    height = vocab // groups
    n, _, tokens = group.shape
    width = min(2048, height)
    fill = height // width

    def table_spec(g):
        return pl.BlockSpec(
            (feats, width), lambda s, r, g=g: (0, g * fill + jnp.minimum(s, fill - 1))
        )

    return pl.pallas_call(
        functools.partial(gather_kernel, groups, fill),
        out_shape=jax.ShapeDtypeStruct((n, feats, tokens), bf16),
        grid_spec=pltpu.PrefetchScalarGridSpec(
            num_scalar_prefetch=1,
            grid=(fill + n,),
            in_specs=[pl.BlockSpec((1, 1, tokens), lambda s, r: (jnp.maximum(s - fill, 0), 0, 0))]
            + [table_spec(g) for g in range(groups)],
            out_specs=pl.BlockSpec(
                (1, feats, tokens), lambda s, r: (jnp.maximum(s - fill, 0), 0, 0)
            ),
            scratch_shapes=[pltpu.VMEM((height, LANES), f32), pltpu.VMEM((tokens, LANES), f32)],
        ),
        compiler_params=params(),
        cost_estimate=cost(45),
        name="gather_tokens",
    )(rows, group, *([table] * groups))


BATCH = 16


def scatter_kernel(
    groups, per_core, rows_ref, row_ref, group_ref, grad_ref, out_ref, pos_ref, acc, update, turned, sem
):
    step = pl.program_id(0)
    feats, tokens = grad_ref.shape[1:]
    height = acc.shape[0]
    width = turned.shape[2]

    @pl.when(step == 0)
    def _():
        def clear(k, carry):
            acc[pl.ds(pl.multiple_of(k * 256, 256), 256), :] = jnp.zeros((256, LANES), f32)
            return carry

        lax.fori_loop(0, height // 256, clear, 0)
        pos_ref[...] = jnp.zeros_like(pos_ref)

    grads = grad_ref[0].astype(f32)
    core = lax.rem(lax.div(step, per_core), CORES)
    pos_ref[core] += grads
    tall = jnp.concatenate([grads] * groups, axis=0)
    own = lax.broadcasted_iota(i32, (LANES, tokens), 0) // feats == group_ref[0]
    tall = jnp.where(own, tall, 0.0).astype(bf16)
    row = lax.broadcasted_iota(i32, (LANES, LANES), 0)
    col = lax.broadcasted_iota(i32, (LANES, LANES), 1)
    near = row // BATCH == col // BATCH
    for b in range(tokens // LANES):
        at = slice(b * LANES, (b + 1) * LANES)
        along = jnp.broadcast_to(row_ref[0][:, at].astype(f32), (LANES, LANES))
        same = jnp.where((along == along.T) & near, 1.0, 0.0).astype(bf16)
        update[at, :] = dot(same, tall[:, at], NT)
    base = step * tokens

    def some(k, carry):
        where = [rows_ref[base + k * BATCH + u] for u in range(BATCH)]
        fresh = [
            acc[pl.ds(where[u], 1), :] + update[pl.ds(k * BATCH + u, 1), :] for u in range(BATCH)
        ]
        for u in range(BATCH):
            acc[pl.ds(where[u], 1), :] = fresh[u]
        return carry

    lax.fori_loop(0, tokens // BATCH, some, 0)

    @pl.when(step == pl.num_programs(0) - 1)
    def _():
        def copy(i, slot, g):
            at = pl.multiple_of(g * height + i * width, width)
            return pltpu.make_async_copy(
                turned.at[slot, pl.ds(g * feats, feats)],
                out_ref.at[:, pl.ds(at, width)],
                sem.at[slot, g],
            )

        def turn(i, carry):
            slot = lax.rem(i, 2)

            @pl.when(i >= 2)
            def _():
                for g in range(groups):
                    copy(i - 2, slot, g).wait()

            at = pl.multiple_of(i * width, width)
            turned[slot] = (acc[pl.ds(at, width), :] * 32.0).T
            for g in range(groups):
                copy(i, slot, g).start()
            return carry

        count = height // width
        lax.fori_loop(0, count, turn, 0)
        for i in range(max(count - 2, 0), count):
            for g in range(groups):
                copy(i, i % 2, g).wait()


def scatter_tokens(grads, rows, row, group, vocab, per_core):
    n, feats, tokens = grads.shape
    groups = LANES // feats
    height = vocab // groups
    width = min(1024, height)
    token_spec = pl.BlockSpec((1, 1, tokens), lambda s, r: (s, 0, 0))
    return pl.pallas_call(
        functools.partial(scatter_kernel, groups, per_core),
        out_shape=(
            jax.ShapeDtypeStruct((feats, vocab), f32),
            jax.ShapeDtypeStruct((CORES, feats, tokens), f32),
        ),
        grid_spec=pltpu.PrefetchScalarGridSpec(
            num_scalar_prefetch=1,
            grid=(n,),
            in_specs=[
                token_spec,
                token_spec,
                pl.BlockSpec((1, feats, tokens), lambda s, r: (s, 0, 0)),
            ],
            out_specs=(
                pl.BlockSpec(memory_space=pl.ANY),
                full((CORES, feats, tokens)),
            ),
            scratch_shapes=[
                pltpu.VMEM((height, LANES), f32),
                pltpu.VMEM((tokens, LANES), f32),
                pltpu.VMEM((2, LANES, width), f32),
                pltpu.SemaphoreType.DMA((2, groups)),
            ],
        ),
        compiler_params=params(),
        cost_estimate=cost(57),
        name="scatter_tokens",
    )(rows, row, group, grads)


def entry_kernel(
    info_ref, emb_ref, pos_a, pos_b, wq_ref, wkv_ref, gain_ref, bias_ref, x0_ref, x1_ref, a_ref, q_ref, kv_ref
):
    step = pl.program_id(0)
    half = x0_ref.shape[0] // 2

    @pl.when(step == 0)
    def _():
        for i, pos in enumerate((pos_a, pos_b)):
            at = slice(i * half, (i + 1) * half)
            places = joined([p[...] for p in pos], info_ref)
            x0 = (emb_ref[:, at].astype(f32) * 32.0 + places.astype(f32)).T
            x1 = normed(x0)[0] * gain_ref[0:1] + bias_ref[0:1]
            a = normed(x1)[0] * gain_ref[1:2] + bias_ref[1:2]
            x0_ref[at] = x0
            x1_ref[at] = x1
            a_ref[at] = a.astype(bf16)

    x = a_ref[...]
    span = wq_ref[0].shape[4]

    @pl.when(step == 0)
    def _():
        def store(at, y):
            q_ref[0, :, pl.ds(at, span)] = (y * HEAD_DIM**-0.5).astype(bf16)

        project(x, wq_ref, info_ref, store)

    @pl.when(step > 0)
    def _():
        def store(at, y):
            kv_ref[0, :, pl.ds(at, span)] = y.astype(bf16)

        project(x, wkv_ref, info_ref, store)


def entry(info, emb, first, gains, biases):
    width, tokens = emb.shape
    wq, wkv = first

    def pos_specs(i):
        return [
            pl.BlockSpec(
                (w.shape[0], 1, 1, w.shape[3], w.shape[4]),
                lambda s, info, skip=skip: (0, info[3 + i], skip, 0, 0),
            )
            for w, skip in wq
        ]

    row = full((tokens, width))
    rows = jax.ShapeDtypeStruct((tokens, width), f32)
    return call(
        entry_kernel,
        info,
        (3,),
        [
            (emb, full(emb.shape)),
            (wq, pos_specs(0)),
            (wq, pos_specs(1)),
            (wq, weight_specs(wq, lambda s: 1)),
            (wkv, weight_specs(wkv, lambda s: jnp.maximum(s - 1, 0))),
            (gains, full(gains.shape)),
            (biases, full(biases.shape)),
        ],
        [
            (rows, row),
            (rows, row),
            (jax.ShapeDtypeStruct((tokens, width), bf16), row),
            (jax.ShapeDtypeStruct((1, tokens, width), bf16), full((1, tokens, width))),
            (
                jax.ShapeDtypeStruct((2, tokens, width), bf16),
                pl.BlockSpec((1, tokens, width), lambda s, info: (jnp.maximum(s - 1, 0), 0, 0)),
            ),
        ],
        cost_estimate=cost(15),
        name="entry",
    )


def slots(pair, info_ref):
    odd = info_ref[9] == 1
    one, two = pair[0][...], pair[1][...]
    return jnp.where(odd, two, one), jnp.where(odd, one, two)


def put_slots(pair, info_ref, values):
    for odd in range(2):

        @pl.when(info_ref[9] == odd)
        def _():
            pair[odd][...] = values[0].astype(bf16)
            pair[1 - odd][...] = values[1].astype(bf16)


def source_kernel(info_ref, came_a, came_b, w_refs, x_ref, kv_ref):
    @pl.when(pl.program_id(0) == 0)
    def _():
        half = came_a.shape[0]
        x_ref[:half], x_ref[half:] = slots((came_a, came_b), info_ref)

    def store(at, y):
        kv_ref[0, :, pl.ds(at, w_refs[0].shape[4])] = y.astype(bf16)

    project(x_ref[...], w_refs, info_ref, store)


def source_keys(info, came, weights):
    half, width = came[0].shape
    tokens = 2 * half
    return call(
        source_kernel,
        info,
        (2,),
        [
            (came[0], full((half, width))),
            (came[1], full((half, width))),
            (weights, weight_specs(weights, lambda s: s)),
        ],
        [
            (jax.ShapeDtypeStruct((tokens, width), bf16), full((tokens, width))),
            (
                jax.ShapeDtypeStruct((2, tokens, width), bf16),
                pl.BlockSpec((1, tokens, width), lambda s, info: (s, 0, 0)),
            ),
        ],
        cost_estimate=cost(8),
        name="source_keys",
    )


def attend_kernel(causal, info_ref, q_ref, own_ref, par_ref, o_ref, p_ref, hide):
    tokens = q_ref.shape[1]
    half = tokens // 2
    core = info_ref[0]

    @pl.when(pl.program_id(0) == 0)
    def _():
        length = info_ref[1] if causal else info_ref[2]
        key = lax.broadcasted_iota(i32, (tokens, tokens), 0)
        query = lax.broadcasted_iota(i32, (tokens, tokens), 1)
        upper = key >= half
        own = key + jnp.where(upper, info_ref[4] - 1, info_ref[3]) * half
        par = key + jnp.where(upper, info_ref[6] - 1, info_ref[5]) * half
        at = query + jnp.where(query >= half, info_ref[4] - 1, info_ref[3]) * half
        for i, place in enumerate((own, par)):
            seen = place < length
            if causal:
                seen = seen & (place <= at)
            hide[i] = jnp.where(seen, 0.0, NEGATIVE)

    outs = []
    for h in range(LANES // HEAD_DIM):
        lanes = slice(h * HEAD_DIM, (h + 1) * HEAD_DIM)
        q = q_ref[0][:, lanes]
        s_own = dot(own_ref[0][:, lanes], q, NT) + hide[0]
        s_par = dot(par_ref[0][:, lanes], q, NT) + hide[1]
        top = jnp.maximum(
            jnp.max(s_own, axis=0, keepdims=True), jnp.max(s_par, axis=0, keepdims=True)
        )
        e_own = jnp.exp(s_own - top)
        e_par = jnp.exp(s_par - top)
        total = jnp.sum(e_own, axis=0, keepdims=True) + jnp.sum(e_par, axis=0, keepdims=True)
        scale = 1.0 / total
        p_own = (e_own * scale).astype(bf16)
        p_par = (e_par * scale).astype(bf16)
        p_ref[h, 0] = p_own
        p_ref[h, 1] = p_par
        outs.append(dot(own_ref[1][:, lanes], p_own, TN) + dot(par_ref[1][:, lanes], p_par, TN))
    o_ref[0] = jnp.concatenate(outs, axis=0).T.astype(bf16)


def attend(info, q, own, par, causal):
    _, tokens, width = q.shape
    heads = width // HEAD_DIM
    pair = LANES // HEAD_DIM
    one = pl.BlockSpec((1, tokens, LANES), lambda s, info: (0, 0, s))
    two = pl.BlockSpec((2, tokens, LANES), lambda s, info: (0, 0, s))
    return pl.pallas_call(
        functools.partial(attend_kernel, causal),
        out_shape=(
            jax.ShapeDtypeStruct((1, tokens, width), bf16),
            jax.ShapeDtypeStruct((heads, 2, tokens, tokens), bf16),
        ),
        grid_spec=pltpu.PrefetchScalarGridSpec(
            num_scalar_prefetch=1,
            grid=(heads // pair,),
            in_specs=[one, two, two],
            out_specs=(
                one,
                pl.BlockSpec((pair, 2, tokens, tokens), lambda s, info: (s, 0, 0, 0)),
            ),
            scratch_shapes=[pltpu.VMEM((2, tokens, tokens), f32)],
        ),
        compiler_params=params(),
        cost_estimate=cost(22),
        name="attend",
    )(info, q, own, par)


def middle_kernel(info_ref, o_ref, w_ref, x_ref, wq_ref, gain_ref, bias_ref, x2_ref, c_ref, q_ref):
    x2 = x_ref[...] + dot(o_ref[0], whole_weight(w_ref, info_ref), NT)
    x2_ref[...] = x2
    c = (normed(x2)[0] * gain_ref[2:3] + bias_ref[2:3]).astype(bf16)
    c_ref[...] = c

    def store(at, y):
        q_ref[0, :, pl.ds(at, wq_ref[0].shape[4])] = (y * HEAD_DIM**-0.5).astype(bf16)

    project(c, wq_ref, info_ref, store)


def middle(info, o, weights, x1, gains, biases):
    _, tokens, width = o.shape
    row = full((tokens, width))
    return call(
        middle_kernel,
        info,
        (1,),
        [
            (o, full(o.shape)),
            (weights, weight_specs(weights, lambda s: 0)),
            (x1, row),
            (weights, weight_specs(weights, lambda s: 1)),
            (gains, full(gains.shape)),
            (biases, full(biases.shape)),
        ],
        [
            (jax.ShapeDtypeStruct((tokens, width), f32), row),
            (jax.ShapeDtypeStruct((tokens, width), bf16), row),
            (jax.ShapeDtypeStruct((1, tokens, width), bf16), full((1, tokens, width))),
        ],
        cost_estimate=cost(9),
        name="middle",
    )


def feed_kernel(
    info_ref,
    o_ref,
    wo_ref,
    x_ref,
    w1_ref,
    w2_ref,
    gain_ref,
    bias_ref,
    x3_ref,
    f_ref,
    g_ref,
    slope_ref,
    x4_ref,
):
    step = pl.program_id(0)

    @pl.when(step == 0)
    def _():
        x3 = x_ref[...] + dot(o_ref[0], whole_weight(wo_ref, info_ref), NT)
        x3_ref[...] = x3
        f_ref[...] = (normed(x3)[0] * gain_ref[3:4] + bias_ref[3:4]).astype(bf16)
        x4_ref[...] = x3

    def store(at, u):
        bell = 0.5 + 0.5 * lax.erf(u * 0.7071067811865476)
        lanes = pl.ds(at, w1_ref[0].shape[4])
        g_ref[0, :, lanes] = (u * bell).astype(bf16)
        slope = bell + u * (0.3989422804014327 * jnp.exp(-0.5 * u * u))
        slope_ref[0, :, lanes] = slope.astype(bf16)

    project(f_ref[...], w1_ref, info_ref, store)
    x4_ref[...] += dot(g_ref[0], whole_weight(w2_ref, info_ref), NT)


def feed(info, o, wo, x2, w1, w2, gains, biases, slabs):
    _, tokens, width = o.shape
    blocks = slabs
    row = full((tokens, width))
    part = pl.BlockSpec((1, tokens, width), lambda s, info: (s, 0, 0))
    wide = jax.ShapeDtypeStruct((tokens, width), f32)
    slim = jax.ShapeDtypeStruct((tokens, width), bf16)
    many = jax.ShapeDtypeStruct((blocks, tokens, width), bf16)
    return call(
        feed_kernel,
        info,
        (blocks,),
        [
            (o, full(o.shape)),
            (wo, weight_specs(wo, lambda s: 2)),
            (x2, row),
            (w1, weight_specs(w1, lambda s: s)),
            (w2, weight_specs(w2, lambda s: s)),
            (gains, full(gains.shape)),
            (biases, full(biases.shape)),
        ],
        [(wide, row), (slim, row), (many, part), (many, part), (wide, row)],
        mib=60,
        cost_estimate=cost(28),
        name="feed",
    )


def feed_back_kernel(
    info_ref,
    x4_ref,
    og_a,
    og_b,
    slope_ref,
    w1_ref,
    w2_ref,
    x3_ref,
    wo_ref,
    gain_ref,
    bias_ref,
    hid_a,
    hid_b,
    g4b_ref,
    du_ref,
    g3_ref,
    g3b_ref,
    do_ref,
    sums_ref,
    total,
):
    step = pl.program_id(0)

    @pl.when(step == 0)
    def _():
        x4 = x4_ref[...]
        half = og_a.shape[0]
        hidden = normed(x4)[0] * gain_ref[4:5] + bias_ref[4:5]
        put_slots((hid_a, hid_b), info_ref, (hidden[:half], hidden[half:]))
        out_grad = jnp.concatenate(slots((og_a, og_b), info_ref), axis=0).astype(f32)
        g4, gain_grad, bias_grad = norm_back(x4, gain_ref[4:5], out_grad)
        g3_ref[...] = g4
        g4b_ref[...] = g4.astype(bf16)
        sums_ref[2:3] = gain_grad
        sums_ref[3:4] = bias_grad

    def store(at, y):
        lanes = pl.ds(at, w2_ref[0].shape[4])
        du_ref[0, :, lanes] = (y * slope_ref[0, :, lanes].astype(f32)).astype(bf16)

    project(g4b_ref[...], w2_ref, info_ref, store)
    part = dot(du_ref[0], whole_weight(w1_ref, info_ref), NT)

    @pl.when(step == 0)
    def _():
        total[...] = part

    @pl.when(step > 0)
    def _():
        total[...] += part

    @pl.when(step == pl.num_programs(0) - 1)
    def _():
        back, gain_grad, bias_grad = norm_back(x3_ref[...], gain_ref[3:4], total[...])
        g3 = g3_ref[...] + back
        g3_ref[...] = g3
        g3b = g3.astype(bf16)
        g3b_ref[...] = g3b
        sums_ref[0:1] = gain_grad
        sums_ref[1:2] = bias_grad

        def keep(at, y):
            do_ref[0, :, pl.ds(at, wo_ref[0].shape[4])] = y.astype(bf16)

        project(g3b, wo_ref, info_ref, keep)


def feed_back(info, x4, og, slope, wo, x3, w1, w2, gains, biases):
    blocks, tokens, width = slope.shape
    row = full((tokens, width))
    part_row = full((tokens // 2, width))
    part_shape = jax.ShapeDtypeStruct((tokens // 2, width), bf16)
    part = pl.BlockSpec((1, tokens, width), lambda s, info: (s, 0, 0))
    wide = jax.ShapeDtypeStruct((tokens, width), f32)
    slim = jax.ShapeDtypeStruct((tokens, width), bf16)
    return call(
        feed_back_kernel,
        info,
        (blocks,),
        [
            (x4, row),
            (og[0], part_row),
            (og[1], part_row),
            (slope, part),
            (w1, weight_specs(w1, lambda s: s)),
            (w2, weight_specs(w2, lambda s: s)),
            (x3, row),
            (wo, weight_specs(wo, lambda s: 2)),
            (gains, full(gains.shape)),
            (biases, full(biases.shape)),
        ],
        [
            (part_shape, part_row),
            (part_shape, part_row),
            (slim, row),
            (jax.ShapeDtypeStruct((blocks, tokens, width), bf16), part),
            (wide, row),
            (slim, row),
            (jax.ShapeDtypeStruct((1, tokens, width), bf16), full((1, tokens, width))),
            (jax.ShapeDtypeStruct((4, width), f32), full((4, width))),
        ],
        [pltpu.VMEM((tokens, width), f32)],
        60,
        cost_estimate=cost(28),
        name="feed_back",
    )


def attend_back_kernel(
    q_ref, own_ref, par_ref, p_ref, o_ref, do_ref, dq_ref, down_ref, dpar_ref
):
    flat = do_ref[0].astype(f32).T * o_ref[0].astype(f32).T
    outs = []
    for h in range(LANES // HEAD_DIM):
        lanes = slice(h * HEAD_DIM, (h + 1) * HEAD_DIM)
        q = q_ref[0][:, lanes]
        grad = do_ref[0][:, lanes]
        inner = jnp.sum(flat[lanes], axis=0, keepdims=True)
        back = None
        for i, (kv_ref, d_ref) in enumerate(((own_ref, down_ref), (par_ref, dpar_ref))):
            keys = kv_ref[0][:, lanes]
            probs = p_ref[h, i]
            d_probs = dot(kv_ref[1][:, lanes], grad, NT)
            d_scores = (probs.astype(f32) * (d_probs - inner)).astype(bf16)
            d_ref[1, :, lanes] = dot(probs, grad).astype(bf16)
            d_ref[0, :, lanes] = dot(d_scores, q).astype(bf16)
            some = dot(keys, d_scores, TN)
            back = some if back is None else back + some
        outs.append(back)
    dq_ref[0] = (jnp.concatenate(outs, axis=0).T * HEAD_DIM**-0.5).astype(bf16)


def attend_back(q, own, par, probs, o, do):
    _, tokens, width = q.shape
    heads = width // HEAD_DIM
    pair = LANES // HEAD_DIM
    one = pl.BlockSpec((1, tokens, LANES), lambda s: (0, 0, s))
    two = pl.BlockSpec((2, tokens, LANES), lambda s: (0, 0, s))
    kv = jax.ShapeDtypeStruct((2, tokens, width), bf16)
    return pl.pallas_call(
        attend_back_kernel,
        out_shape=(jax.ShapeDtypeStruct((1, tokens, width), bf16), kv, kv),
        grid=(heads // pair,),
        in_specs=[
            one,
            two,
            two,
            pl.BlockSpec((pair, 2, tokens, tokens), lambda s: (s, 0, 0, 0)),
            one,
            one,
        ],
        out_specs=(one, two, two),
        compiler_params=params(),
        cost_estimate=cost(21),
        name="attend_back",
    )(q, own, par, probs, o, do)


def causal_back_kernel(
    info_ref, q_ref, own_ref, par_ref, p_ref, o_ref, do_ref, dq_ref, down_ref, dpar_ref, back
):
    tokens = q_ref.shape[1]
    half = tokens // 2
    low, high, every = slice(0, half), slice(half, tokens), slice(0, tokens)
    flat = do_ref[0].astype(f32).T * o_ref[0].astype(f32).T
    inner = [
        jnp.sum(flat[h * HEAD_DIM : (h + 1) * HEAD_DIM], axis=0, keepdims=True)
        for h in range(LANES // HEAD_DIM)
    ]
    back[...] = jnp.zeros_like(back)

    def segments(i, kv_ref, d_ref, spans):
        for h in range(LANES // HEAD_DIM):
            lanes = slice(h * HEAD_DIM, (h + 1) * HEAD_DIM)
            for keys, queries in spans:
                grad = do_ref[0, queries, lanes]
                probs = p_ref[h, i, keys, queries]
                d_probs = dot(kv_ref[1, keys, lanes], grad, NT)
                d_scores = (probs.astype(f32) * (d_probs - inner[h][:, queries])).astype(bf16)
                d_ref[1, keys, lanes] = dot(probs, grad).astype(bf16)
                d_ref[0, keys, lanes] = dot(d_scores, q_ref[0, queries, lanes]).astype(bf16)
                back[lanes, queries] += dot(kv_ref[0, keys, lanes], d_scores, TN)

    segments(0, own_ref, down_ref, [(low, every), (high, high)])

    @pl.when(info_ref[0] == 0)
    def _():
        segments(1, par_ref, dpar_ref, [(every, high)])

    @pl.when(info_ref[0] == 1)
    def _():
        segments(1, par_ref, dpar_ref, [(low, every)])
        dpar_ref[:, high, :] = jnp.zeros((2, half, LANES), bf16)

    dq_ref[0] = (back[...].T * HEAD_DIM**-0.5).astype(bf16)


def causal_back(info, q, own, par, probs, o, do):
    _, tokens, width = q.shape
    heads = width // HEAD_DIM
    pair = LANES // HEAD_DIM
    one = pl.BlockSpec((1, tokens, LANES), lambda s, info: (0, 0, s))
    two = pl.BlockSpec((2, tokens, LANES), lambda s, info: (0, 0, s))
    kv = jax.ShapeDtypeStruct((2, tokens, width), bf16)
    return call(
        causal_back_kernel,
        info,
        (heads // pair,),
        [
            (q, one),
            (own, two),
            (par, two),
            (probs, pl.BlockSpec((pair, 2, tokens, tokens), lambda s, info: (s, 0, 0, 0))),
            (o, one),
            (do, one),
        ],
        [(jax.ShapeDtypeStruct((1, tokens, width), bf16), one), (kv, two), (kv, two)],
        [pltpu.VMEM((LANES, tokens), f32)],
        cost_estimate=cost(19),
        name="causal_back",
    )


def middle_back_kernel(
    info_ref, dq_ref, wq_ref, x2_ref, g3_ref, wo_ref, gain_ref, g2_ref, g2b_ref, do_ref, sums_ref
):
    d_normed = dot(dq_ref[0], whole_weight(wq_ref, info_ref), NT)
    back, gain_grad, bias_grad = norm_back(x2_ref[...], gain_ref[2:3], d_normed)
    g2 = g3_ref[...] + back
    g2_ref[...] = g2
    g2b = g2.astype(bf16)
    g2b_ref[...] = g2b
    sums_ref[0:1] = gain_grad
    sums_ref[1:2] = bias_grad

    def keep(at, y):
        do_ref[0, :, pl.ds(at, wo_ref[0].shape[4])] = y.astype(bf16)

    project(g2b, wo_ref, info_ref, keep)


def middle_back(info, dq, weights, x2, g3, gains):
    _, tokens, width = dq.shape
    row = full((tokens, width))
    return call(
        middle_back_kernel,
        info,
        (1,),
        [
            (dq, full(dq.shape)),
            (weights, weight_specs(weights, lambda s: 1)),
            (x2, row),
            (g3, row),
            (weights, weight_specs(weights, lambda s: 0)),
            (gains, full(gains.shape)),
        ],
        [
            (jax.ShapeDtypeStruct((tokens, width), f32), row),
            (jax.ShapeDtypeStruct((tokens, width), bf16), row),
            (jax.ShapeDtypeStruct((1, tokens, width), bf16), full((1, tokens, width))),
            (jax.ShapeDtypeStruct((2, width), f32), full((2, width))),
        ],
        cost_estimate=cost(10),
        name="middle_back",
    )


def source_back_kernel(info_ref, mine_ref, came_ref, w_ref, out_a, out_b, sum_ref, total):
    step = pl.program_id(0)
    grads = (mine_ref[0].astype(f32) + came_ref[0].astype(f32)).astype(bf16)
    sum_ref[0] = grads
    part = dot(grads, whole_weight(w_ref, info_ref), NT)

    @pl.when(step == 0)
    def _():
        total[...] = part

    @pl.when(step == pl.num_programs(0) - 1)
    def _():
        half = out_a.shape[0]
        both = total[...] + part
        put_slots((out_a, out_b), info_ref, (both[:half], both[half:]))


def source_back(info, mine, came, weights):
    parts, tokens, width = mine.shape
    part = pl.BlockSpec((1, tokens, width), lambda s, info: (s, 0, 0))
    return call(
        source_back_kernel,
        info,
        (parts,),
        [(mine, part), (came, part), (weights, weight_specs(weights, lambda s: s))],
        [
            (jax.ShapeDtypeStruct((tokens // 2, width), bf16), full((tokens // 2, width))),
            (jax.ShapeDtypeStruct((tokens // 2, width), bf16), full((tokens // 2, width))),
            (jax.ShapeDtypeStruct((parts, tokens, width), bf16), part),
        ],
        [pltpu.VMEM((tokens, width), f32)],
        cost_estimate=cost(7),
        name="source_back",
    )


def exit_kernel(
    info_ref,
    dq_ref,
    mine_ref,
    came_ref,
    wq_ref,
    wkv_ref,
    x1_ref,
    x0_ref,
    g2_ref,
    gain_ref,
    g0_ref,
    sum_ref,
    sums_ref,
    total,
):
    step = pl.program_id(0)

    @pl.when(step == 0)
    def _():
        total[...] = dot(dq_ref[0], whole_weight(wq_ref, info_ref), NT)

    @pl.when(step > 0)
    def _():
        grads = (mine_ref[0].astype(f32) + came_ref[0].astype(f32)).astype(bf16)
        sum_ref[0] = grads
        total[...] += dot(grads, whole_weight(wkv_ref, info_ref), NT)

    @pl.when(step == pl.num_programs(0) - 1)
    def _():
        back, gain_one, bias_one = norm_back(x1_ref[...], gain_ref[1:2], total[...])
        g1 = g2_ref[...] + back
        g0, gain_zero, bias_zero = norm_back(x0_ref[...], gain_ref[0:1], g1)
        g0_ref[...] = g0.T.astype(bf16)
        sums_ref[0:1] = gain_zero
        sums_ref[1:2] = bias_zero
        sums_ref[2:3] = gain_one
        sums_ref[3:4] = bias_one


def exit_back(info, dq, mine, came, first, x1, x0, g2, gains):
    _, tokens, width = dq.shape
    wq, wkv = first
    row = full((tokens, width))
    part = pl.BlockSpec((1, tokens, width), lambda s, info: (jnp.maximum(s - 1, 0), 0, 0))
    return call(
        exit_kernel,
        info,
        (3,),
        [
            (dq, full(dq.shape)),
            (mine, part),
            (came, part),
            (wq, weight_specs(wq, lambda s: 1)),
            (wkv, weight_specs(wkv, lambda s: jnp.maximum(s - 1, 0))),
            (x1, row),
            (x0, row),
            (g2, row),
            (gains, full(gains.shape)),
        ],
        [
            (jax.ShapeDtypeStruct((width, tokens), bf16), full((width, tokens))),
            (jax.ShapeDtypeStruct((2, tokens, width), bf16), part),
            (jax.ShapeDtypeStruct((4, width), f32), full((4, width))),
        ],
        [pltpu.VMEM((tokens, width), f32)],
        cost_estimate=cost(15),
        name="exit_back",
    )


def weight_grad_kernel(chips, aliased, info_ref, xo_ref, xp_ref, yo_ref, yp_ref, *refs):
    out_ref, turned = refs[-2], refs[-1]
    tokens, width = xo_ref.shape
    rows = width // (chips * CORES)
    core = info_ref[0]

    @pl.when(pl.program_id(0) == 0)
    def _():
        for i, x_ref in enumerate((xo_ref, xp_ref)):
            at = slice(i * tokens, (i + 1) * tokens)
            if rows % LANES == 0:
                for j in range(chips):
                    lanes = pl.ds(pl.multiple_of((2 * j + core) * rows, rows), rows)
                    turned[j * rows : (j + 1) * rows, at] = x_ref[:, lanes].astype(f32).T.astype(bf16)
            else:
                tall = x_ref[...].astype(f32).T.reshape(chips, CORES, rows, tokens)
                mine = jnp.where(core == 0, tall[:, 0], tall[:, 1])
                turned[:, at] = mine.reshape(chips * rows, tokens).astype(bf16)

    y_own, y_par = yo_ref[0], yp_ref[0]
    blocks, span = out_ref.shape[1], out_ref.shape[4]
    result = dot(turned[:, :tokens], y_own) + dot(turned[:, tokens:], y_par)
    for m in range(blocks):
        part = result[:, m * span : (m + 1) * span].astype(bf16)
        out_ref[:, m, 0] = part.reshape(chips, rows, span)


def weight_grad(info, x_own, x_par, y_own, y_par, shape, at, before=None):
    parts, tokens, width = y_own.shape
    chips = shape[0]
    row = full(x_own.shape)
    part = pl.BlockSpec((1, tokens, width), lambda s, info: (s, 0, 0))
    extra = [] if before is None else [before]
    return pl.pallas_call(
        functools.partial(weight_grad_kernel, chips, before is not None),
        out_shape=jax.ShapeDtypeStruct(shape, bf16),
        grid_spec=pltpu.PrefetchScalarGridSpec(
            num_scalar_prefetch=1,
            grid=(parts,),
            in_specs=[row, row, part, part] + [pl.BlockSpec(memory_space=pl.ANY) for _ in extra],
            out_specs=pl.BlockSpec(
                (chips, shape[1], 1, shape[3], shape[4]), lambda s, info: (0, 0, s + at, 0, 0)
            ),
            scratch_shapes=[pltpu.VMEM((x_own.shape[1] // 2, 2 * tokens), bf16)],
        ),
        input_output_aliases={} if before is None else {5: 0},
        compiler_params=params(),
        cost_estimate=cost(3 + 2 * parts),
        name="weight_grad",
    )(info, x_own, x_par, y_own, y_par, *extra)


def swap(value):
    return lax.ppermute(value, "core", [(0, 1), (1, 0)])


def line_moves(mp):
    rounds = []
    for turn in range(2):
        moves = []
        for c in range(CORES):
            for m in range(mp):
                target, slot = (1 if m in (1, 2) else 0), m // 2
                moves.append((c * mp + m, target * mp + 2 * c + (slot ^ turn)))
        rounds.append(moves)
    return rounds


def to_chips(value, mp):
    slot = lax.axis_index("mp") // 2
    return [
        lax.ppermute(jnp.where((slot ^ turn) == 0, value[0], value[1]), LINE, moves)
        for turn, moves in enumerate(line_moves(mp))
    ]


def from_chips(pair, mp):
    return [
        lax.ppermute(sent, LINE, [(b, a) for a, b in moves])
        for sent, moves in zip(pair, line_moves(mp))
    ]


def placed_again(came):
    slot = lax.axis_index("mp") // 2
    one, two = [c.astype(f32) for c in came]
    return jnp.stack([jnp.where(slot == 0, one, two), jnp.where(slot == 0, two, one)])


def packed(*weights):
    return jnp.concatenate([w.reshape(-1, w.shape[-1]) for w in weights], axis=0)


X_SWAP = [(0, 1), (1, 0), (2, 3), (3, 2)]
Y_SWAP = [(0, 2), (2, 0), (1, 3), (3, 1)]
def gathered(rows, unit, chips, mp):
    value = lax.all_gather(rows, ALL, axis=0, tiled=False)
    return value.reshape(chips * CORES, mp, -1, unit, rows.shape[-1])


def gathered_line(rows, unit, mp):
    value = lax.all_gather(rows, "mp", axis=0, tiled=False)
    return value.reshape(mp, -1, unit, rows.shape[-1])


class Spread:
    def __init__(self, value, cut):
        self.own, self.cut = [value], cut
        self.near, self.far, self.both = [], [], []
        self.swapped = {}

    def begin(self, *others):
        self.own = tied(self.own, *others)
        sets = [self.own[0][:, : self.cut], self.own[0][:, self.cut :]]
        self.near = [lax.ppermute(w, "chip", p) for w, p in zip(sets, (X_SWAP, Y_SWAP))]
        self.far = [lax.ppermute(w, "chip", p) for w, p in zip(sets, (Y_SWAP, X_SWAP))]

    def finish(self, *others):
        self.near = tied(self.near, *others)
        self.both = [lax.ppermute(w, "chip", p) for w, p in zip(self.near, (Y_SWAP, X_SWAP))]

    def swap(self, *names):
        for name in names:
            self.swapped[name] = [swap(w) for w in getattr(self, name)]

    def hold(self, *others):
        state = [self.own, self.near, self.far, self.both, self.swapped]
        state, others = lax.optimization_barrier((state, others))
        self.own, self.near, self.far, self.both, self.swapped = state
        return others if len(others) > 1 else others[0]

    def pieces(self):
        found = []
        for i in range(2):
            pieces = []
            for name in ("own", "near", "far", "both") if i == 0 else ("own", "far", "near", "both"):
                at, skip = (0, i * self.cut) if name == "own" else (i, 0)
                for group in (getattr(self, name), self.swapped[name]):
                    pieces.append((group[at][None], skip))
            found.append(pieces)
        return found


def tied(value, *others):
    return after(value, *others) if others else value


def scattered(grads, axis):
    return lax.psum_scatter(grads, axis, scatter_dimension=0, tiled=False)


def sent_over(grads, axis, size):
    me = lax.axis_index(axis)
    terms = []
    for k in range(size):
        if axis == "chip" and size == 4:
            to, perm = me ^ k, [(i, i ^ k) for i in range(size)]
        else:
            to, perm = (me + k) % size, [(i, (i + k) % size) for i in range(size)]
        part = lax.dynamic_index_in_dim(grads, to, axis=0, keepdims=False)
        terms.append(part if k == 0 else lax.ppermute(part, axis, perm))
    return terms


def summed(terms):
    return sum([t.astype(f32) for t in terms[1:]], start=terms[0].astype(f32))


def total_over(value, axis, size):
    terms = [
        lax.ppermute(value, axis, [(i, (i + k) % size) for i in range(size)])
        for k in range(1, size)
    ]
    return sum(terms, start=value)


def after(value, *others):
    return lax.optimization_barrier((value, others))[0]


def body(
    chips,
    mp,
    target_ids,
    tgt_lengths,
    encoder_states,
    src_lengths,
    table,
    pos_table,
    self_query_key_value_weight,
    self_output_weight,
    cross_query_weight,
    cross_key_value_weight,
    cross_output_weight,
    feedforward_input_weight,
    feedforward_output_weight,
    norm_gains,
    norm_biases,
    out_grad,
):
    dp = chips * CORES
    n = dp * mp
    seqs, block = target_ids.shape
    assert seqs * CORES == mp == 4
    tokens = seqs * block
    width = norm_gains.shape[1]
    vocab = table.shape[1]
    feats = table.shape[0]
    rows = pos_table.shape[0]
    core, m, chip = lax.axis_index("core"), lax.axis_index("mp"), lax.axis_index("chip")

    def split(weight):
        return weight.reshape(rows, -1, block).transpose(1, 0, 2)

    own_ids = jnp.broadcast_to(target_ids.reshape(1, tokens), (n, tokens))
    all_ids = lax.all_to_all(own_ids, ALL, split_axis=0, concat_axis=0, tiled=True)
    sub = feedforward_input_weight.shape[1] // block
    first = packed(pos_table, split(self_query_key_value_weight))
    second = packed(
        self_output_weight, cross_query_weight, split(cross_key_value_weight), cross_output_weight
    )
    third = packed(split(feedforward_input_weight), split(feedforward_output_weight))
    sub = feedforward_input_weight.shape[1] // block
    late = gathered(jnp.concatenate([second, third]), rows, chips, mp)
    second = [(late, 0)], [(late, 2)]
    third = [(late, 5)], [(late, 5 + sub)]
    stepped = chips == 4
    if stepped:
        copies = jnp.broadcast_to(first[None], (mp,) + first.shape)
        copies = lax.all_to_all(after(copies, all_ids), "mp", split_axis=0, concat_axis=0, tiled=True)
        first = Spread(copies.reshape(mp, -1, rows, block), 2)
    else:
        first = gathered(first, rows, chips, mp)
        first = [(first, 0)], [(first, 2)]

    lengths = jnp.stack([tgt_lengths, src_lengths])
    other = swap(lengths)
    lengths = jnp.where(
        core == 0,
        jnp.concatenate([lengths, other], axis=1),
        jnp.concatenate([other, lengths], axis=1),
    )
    lengths = lax.dynamic_index_in_dim(lengths, m, axis=1, keepdims=False)
    info = jnp.stack(
        [
            core,
            lengths[0],
            lengths[1],
            core,
            3 - core,
            1 - core,
            2 + core,
            chip % 2,
            chip // 2,
            m % 2,
        ]
    ).astype(i32)

    ids = all_ids.reshape(chips, CORES, mp, seqs, block)
    ids = jnp.stack([ids[:, :, 0], ids[:, :, 3], ids[:, :, 1], ids[:, :, 2]], axis=2)
    ids = ids.reshape(chips, CORES, CORES, 2, seqs, block).transpose(0, 2, 1, 4, 3, 5)
    ids = ids.reshape(n, 1, tokens)
    height = vocab // (LANES // feats)
    row, group = ids % height, ids // height
    flat_row = row.reshape(-1)

    picked = gather_tokens(table, flat_row, group)
    if stepped:
        picked = first.hold(picked)
        first.begin(picked)
        first.finish()
        first.swap("own", "near", "far", "both")
        first = first.pieces()
    emb = lax.all_to_all(picked, ALL, split_axis=0, concat_axis=0, tiled=True)
    emb = emb.reshape(width, tokens)

    x0, x1, a, q, kv = entry(info, emb, first, norm_gains, norm_biases)
    states = to_chips(after(encoder_states, a), mp)
    kv_par = swap(kv)
    outs = attend(info, q, kv, kv_par, True)
    (o, probs), states = lax.optimization_barrier((outs, states))
    states, ckv = source_keys(info, states, second[1])
    ckv_par = swap(ckv)
    x2, c, cq = middle(info, after(o, ckv), second[0], x1, norm_gains, norm_biases)
    oc, cprobs = attend(info, cq, ckv, ckv_par, False)
    og = to_chips(after(out_grad.astype(bf16), oc), mp)
    w1, w2 = third
    oc_par, c_par = swap(oc), swap(after(c, oc))
    outs = feed(info, oc, second[1], x2, w1, w2, norm_gains, norm_biases, sub)
    (x3, f, g, slope, x4), og, oc_par, c_par = lax.optimization_barrier((outs, og, oc_par, c_par))
    f_par, g_par = swap(f), swap(g)
    a_par, o_par, states_par = [swap(after(v, x4)) for v in (a, o, states)]
    outs = feed_back(info, x4, og, slope, second[1], x3, w1, w2, norm_gains, norm_biases)
    outs, f_par, g_par, a_par, o_par, states_par = lax.optimization_barrier(
        (outs, f_par, g_par, a_par, o_par, states_par)
    )
    *hid, g4b, du, g3, g3b, doc, sums34 = outs
    g4b_par, g3b_par, du_par = swap(g4b), swap(g3b), swap(du)
    hidden_out = from_chips(tied(hid, g4b_par), mp)
    shape = (chips, mp, sub, rows, block)
    grads = weight_grad(info, g4b, g4b_par, g, g_par, shape, 0)
    part_one = scattered(grads, "chip")
    shape = (chips, mp, sub + 1, rows, block)
    grads = weight_grad(info, after(g3b, grads), g3b_par, oc, oc_par, shape, sub)
    grads = weight_grad(info, after(f, grads), f_par, du, du_par, shape, 0, grads)
    doc, hidden_out = lax.optimization_barrier((after(doc, grads), hidden_out))

    outs = attend_back(cq, ckv, ckv_par, cprobs, oc, doc)
    (dcq, dckv_own, dckv_par), part_one = lax.optimization_barrier((outs, part_one))
    part_two = scattered(after(grads, part_one), "chip")
    dckv_came, dcq_par = swap(dckv_par), swap(dcq)
    outs = middle_back(info, dcq, second[0], x2, g3, norm_gains)
    (g2, g2b, do, sums2), dckv_came, dcq_par, dckv_own = lax.optimization_barrier(
        (outs, dckv_came, dcq_par, dckv_own)
    )
    g2b_par = swap(g2b)
    outs = source_back(info, dckv_own, dckv_came, second[1])
    *enc_grad, dckv = outs
    dckv_after = swap(dckv)
    shape = (chips, mp, 4, rows, block)
    grads = weight_grad(info, c, c_par, after(dcq, dckv), dcq_par, shape, 0)
    grads = weight_grad(info, g2b, g2b_par, o, o_par, shape, 1, grads)
    grads = weight_grad(info, states, states_par, dckv, dckv_after, shape, 2, grads)
    do = after(do, grads)
    cross_terms = lax.all_to_all(grads, "chip", split_axis=0, concat_axis=0, tiled=True)
    encoder_grad = from_chips(tied(enc_grad, grads), mp)

    outs = causal_back(info, q, kv, kv_par, probs, o, do)
    (dq, dkv_own, dkv_par), encoder_grad = lax.optimization_barrier((outs, encoder_grad))
    dkv_came = swap(dkv_par)
    dq_par = swap(dq)
    outs = exit_back(info, dq, dkv_own, dkv_came, first, x1, x0, g2, norm_gains)
    (g0, dkv, sums01), dq_par, cross_terms = lax.optimization_barrier((outs, dq_par, cross_terms))
    sent = g0.reshape(n, feats, tokens)
    arrived = lax.all_to_all(sent, ALL, split_axis=0, concat_axis=0, tiled=True)
    cross_part = jnp.sum(cross_terms.astype(f32), axis=0).astype(bf16)
    sums = jnp.concatenate((sums01, sums2, sums34), axis=0)
    sums_par = swap(sums)
    shape = (chips, mp, 3, rows, block)
    dkv_after = swap(dkv)
    grads = weight_grad(info, a, a_par, dq, dq_par, shape, 0)
    grads, sums_par = lax.optimization_barrier((grads, sums_par))
    sums = total_over(sums + sums_par, "chip", chips)
    grads = weight_grad(info, a, a_par, dkv, dkv_after, shape, 1, grads)
    sums, grads, arrived, part_two = lax.optimization_barrier((sums, grads, arrived, part_two))
    sums_up = scattered(jnp.concatenate([part_one, part_two, cross_part], axis=1), "mp")
    self_terms = lax.all_to_all(grads, "chip", split_axis=0, concat_axis=0, tiled=True)
    sums = total_over(sums, "mp", mp)

    outs = scatter_tokens(arrived, flat_row, row, group, vocab, mp)
    (table_grad, places), self_terms, sums = lax.optimization_barrier((outs, self_terms, sums))
    hidden_out = placed_again(tied(hidden_out, places))
    encoder_grad = placed_again(tied(encoder_grad, places))
    self_part = jnp.sum(self_terms.astype(f32), axis=0).astype(bf16)
    self_grads = summed(sent_over(self_part, "mp", mp))
    sums_up = sums_up.astype(f32)
    feed_out_grads, feed_in_grads, cross_grads = (
        sums_up[:sub],
        sums_up[sub : 2 * sub + 1],
        sums_up[2 * sub + 1 :],
    )

    blocks = places.reshape(CORES, feats, 2, block).transpose(0, 2, 1, 3).reshape(4, feats, block)
    blocks = jnp.stack([blocks[0], blocks[2], blocks[3], blocks[1]])
    parts = []
    for k in range(mp):
        mine = lax.dynamic_index_in_dim(blocks, (m + k) % mp, axis=0, keepdims=False)
        parts.append(
            mine if k == 0 else lax.ppermute(mine, "mp", [(i, (i + k) % mp) for i in range(mp)])
        )
    pos_grad = []
    for source in range(mp):
        value = parts[0]
        for k in range(1, mp):
            value = jnp.where((m - source) % mp == k, parts[k], value)
        pos_grad.append(value)
    pos_grad = jnp.concatenate(pos_grad, axis=0)

    def join(parts):
        return parts.transpose(1, 0, 2)

    return (
        hidden_out,
        table_grad,
        pos_grad,
        join(self_grads),
        cross_grads[1],
        cross_grads[0],
        join(cross_grads[2:4]),
        feed_in_grads[sub],
        join(feed_in_grads[:sub]).reshape(rows, -1),
        join(feed_out_grads).reshape(rows, -1),
        sums[0::2],
        sums[1::2],
        encoder_grad,
    )


def solution(mesh):
    dp, mp = mesh.devices.shape
    chips = dp // CORES
    fine = Mesh(mesh.devices.reshape(chips, CORES, mp), ALL)
    both = ("chip", "core")
    placed = (
        P(both, "mp"),
        P(both),
        P(both, "mp", None),
        P(both),
        P(ALL, None),
        P(both, "mp"),
        P(both, None, "mp"),
        P(both, "mp"),
        P(both, "mp"),
        P(both, None, "mp"),
        P(both, "mp"),
        P(both, "mp"),
        P(both, "mp"),
        P(),
        P(),
        P(both, "mp", None),
    )
    return jax.shard_map(
        functools.partial(body, chips, mp),
        mesh=fine,
        in_specs=placed,
        out_specs=(
            P(both, "mp", None),
            P(ALL, None),
            P(both, "mp"),
            P(both, None, "mp"),
            P(both, "mp"),
            P(both, "mp"),
            P(both, None, "mp"),
            P(both, "mp"),
            P(both, "mp"),
            P(both, "mp"),
            P(),
            P(),
            P(both, "mp", None),
        ),
        check_vma=False,
    )
```

```python
import functools
import math

import jax
import jax.numpy as jnp
from jax import lax
from jax.experimental import pallas as pl
from jax.experimental.pallas import tpu as pltpu
from jax.sharding import Mesh
from jax.sharding import PartitionSpec as P

HEAD_DIM = 64
EPSILON = 1e-05
NEGATIVE = -1e30
LANES = 128
ALL = ("chip", "core", "mp")
LINE = ("core", "mp")
CORES = 2

f32 = jnp.float32
bf16 = jnp.bfloat16
i32 = jnp.int32

NT = (((1,), (1,)), ((), ()))
NN = (((1,), (0,)), ((), ()))
TN = (((0,), (0,)), ((), ()))


def dot(a, b, dims=NN):
    return lax.dot_general(a, b, dims, preferred_element_type=f32)


def params(mib=56):
    return pltpu.CompilerParams(vmem_limit_bytes=mib << 20)


def cost(microseconds):
    return pl.CostEstimate(flops=0, bytes_accessed=int(microseconds * 3.2e6), transcendentals=0)


def normed(values):
    centred = values - jnp.mean(values, axis=-1, keepdims=True)
    inverse = lax.rsqrt(jnp.mean(centred * centred, axis=-1, keepdims=True) + EPSILON)
    return centred * inverse, inverse


def norm_back(values, gain, grad):
    hat, inverse = normed(values)
    scaled = grad * gain
    first = jnp.mean(scaled, axis=-1, keepdims=True)
    second = jnp.mean(scaled * hat, axis=-1, keepdims=True)
    back = inverse * (scaled - first - hat * second)
    gain_grad = jnp.sum(grad * hat, axis=0, keepdims=True)
    bias_grad = jnp.sum(grad, axis=0, keepdims=True)
    return back, gain_grad, bias_grad


def in_order(pieces, info_ref):
    for bit, place in ((0, 0), (1, 7), (2, 8)):
        far = info_ref[place] == 1
        turned = []
        for i, piece in enumerate(pieces):
            turned.append(jnp.where(far, pieces[i ^ (1 << bit)], piece))
        pieces = turned
    return pieces


def joined(blocks, info_ref):
    flat = [b.reshape(-1, b.shape[-1]) for b in blocks]
    return flat[0] if len(flat) == 1 else jnp.concatenate(in_order(flat, info_ref), axis=0)


def columns(w_refs, m, info_ref):
    return joined([w[:, pl.ds(m, 1)] for w in w_refs], info_ref)


def whole_weight(w_refs, info_ref):
    parts = [columns(w_refs, m, info_ref) for m in range(w_refs[0].shape[1])]
    return jnp.concatenate(parts, axis=1)


def project(x, w_refs, info_ref, store):
    width = w_refs[0].shape[4]

    def step(m, carry):
        store(pl.multiple_of(m * width, width), dot(x, columns(w_refs, m, info_ref)))
        return carry

    lax.fori_loop(0, w_refs[0].shape[1], step, 0)


def weight_specs(weights, index):
    return [
        pl.BlockSpec(
            (w.shape[0], w.shape[1], 1, w.shape[3], w.shape[4]),
            lambda s, info, skip=skip: (0, 0, index(s) + skip, 0, 0),
        )
        for w, skip in weights
    ]


def call(kernel, info, grid, operands, outs, scratch=(), mib=56, **others):
    arrays, specs, sizes = [], [], []
    for value, spec in operands:
        group = isinstance(value, (list, tuple))
        sizes.append(len(value) if group else None)
        arrays.extend([w for w, _ in value] if group else [value])
        specs.extend(spec if group else [spec])

    def body(info_ref, *refs):
        given, rest, at = [], refs, 0
        for size in sizes:
            given.append(refs[at] if size is None else list(refs[at : at + size]))
            at += 1 if size is None else size
        kernel(info_ref, *given, *rest[at:])

    return pl.pallas_call(
        body,
        out_shape=[o for o, _ in outs],
        grid_spec=pltpu.PrefetchScalarGridSpec(
            num_scalar_prefetch=1,
            grid=grid,
            in_specs=specs,
            out_specs=[o for _, o in outs],
            scratch_shapes=list(scratch),
        ),
        compiler_params=params(mib),
        **others,
    )(info, *arrays)


def full(shape):
    return pl.BlockSpec(shape, lambda *a: (0,) * len(shape))


def gather_kernel(groups, fill, rows_ref, group_ref, *refs):
    tables, out_ref, turned, picked = refs[:groups], refs[groups], refs[-2], refs[-1]
    step = pl.program_id(0)
    feats, width = tables[0].shape
    tokens = picked.shape[0]

    @pl.when(step < fill)
    def _():
        stacked = jnp.concatenate([t[...].astype(f32) for t in tables], axis=0).astype(bf16)
        row = lax.broadcasted_iota(i32, (256, 256), 0)
        eye = jnp.where(row == lax.broadcasted_iota(i32, (256, 256), 1), 1.0, 0.0).astype(bf16)
        for k in range(width // 256):
            at = pl.multiple_of(step * width + k * 256, 256)
            turned[pl.ds(at, 256), :] = dot(eye, stacked[:, k * 256 : (k + 1) * 256], NT)

    @pl.when(step >= fill)
    def _():
        base = (step - fill) * tokens

        def some(k, carry):
            for u in range(16):
                t = k * 16 + u
                picked[pl.ds(t, 1), :] = turned[pl.ds(rows_ref[base + t], 1), :]
            return carry

        lax.fori_loop(0, tokens // 16, some, 0)
        row = lax.broadcasted_iota(i32, (LANES, LANES), 0)
        eye = jnp.where(row == lax.broadcasted_iota(i32, (LANES, LANES), 1), 1.0, 0.0)
        across = dot(eye.astype(bf16), picked[...].astype(bf16), NT)
        own = lax.broadcasted_iota(i32, (LANES, tokens), 0) // feats == group_ref[0]
        kept = jnp.where(own, across, 0.0)
        total = kept[:feats]
        for g in range(1, groups):
            total = total + kept[g * feats : (g + 1) * feats]
        out_ref[0] = total.astype(out_ref.dtype)


def gather_tokens(table, rows, group):
    feats, vocab = table.shape
    groups = LANES // feats
    height = vocab // groups
    n, _, tokens = group.shape
    width = min(2048, height)
    fill = height // width

    def table_spec(g):
        return pl.BlockSpec(
            (feats, width), lambda s, r, g=g: (0, g * fill + jnp.minimum(s, fill - 1))
        )

    return pl.pallas_call(
        functools.partial(gather_kernel, groups, fill),
        out_shape=jax.ShapeDtypeStruct((n, feats, tokens), bf16),
        grid_spec=pltpu.PrefetchScalarGridSpec(
            num_scalar_prefetch=1,
            grid=(fill + n,),
            in_specs=[pl.BlockSpec((1, 1, tokens), lambda s, r: (jnp.maximum(s - fill, 0), 0, 0))]
            + [table_spec(g) for g in range(groups)],
            out_specs=pl.BlockSpec(
                (1, feats, tokens), lambda s, r: (jnp.maximum(s - fill, 0), 0, 0)
            ),
            scratch_shapes=[pltpu.VMEM((height, LANES), f32), pltpu.VMEM((tokens, LANES), f32)],
        ),
        compiler_params=params(),
        cost_estimate=cost(45),
        name="gather_tokens",
    )(rows, group, *([table] * groups))


BATCH = 16
WIDTH = 4096
SENDERS = 8


def scatter_kernel(
    groups, per_core, rows_ref, row_ref, group_ref, grad_ref, out_ref, pos_ref, acc, update, turned, sem
):
    step = pl.program_id(0)
    senders, feats, tokens = grad_ref.shape
    height = acc.shape[0]
    width = turned.shape[2]

    @pl.when(step == 0)
    def _():
        def clear(k, carry):
            acc[pl.ds(pl.multiple_of(k * 256, 256), 256), :] = jnp.zeros((256, LANES), f32)
            return carry

        lax.fori_loop(0, height // 256, clear, 0)
        pos_ref[...] = jnp.zeros_like(pos_ref)

    row = lax.broadcasted_iota(i32, (LANES, LANES), 0)
    col = lax.broadcasted_iota(i32, (LANES, LANES), 1)
    near = row // BATCH == col // BATCH

    def sender(d, carry):
        place = step * senders + d
        grads = grad_ref[d].astype(f32)
        core = lax.rem(lax.div(place, per_core), CORES)
        pos_ref[core] += grads
        tall = jnp.concatenate([grads] * groups, axis=0)
        own = lax.broadcasted_iota(i32, (LANES, tokens), 0) // feats == group_ref[d]
        tall = jnp.where(own, tall, 0.0).astype(bf16)
        for b in range(tokens // LANES):
            at = slice(b * LANES, (b + 1) * LANES)
            along = jnp.broadcast_to(row_ref[d][:, at].astype(f32), (LANES, LANES))
            same = jnp.where((along == along.T) & near, 1.0, 0.0).astype(bf16)
            update[at, :] = dot(same, tall[:, at], NT)
        base = place * tokens

        def some(k, carry):
            where = [rows_ref[base + k * BATCH + u] for u in range(BATCH)]
            fresh = [
                acc[pl.ds(where[u], 1), :] + update[pl.ds(k * BATCH + u, 1), :]
                for u in range(BATCH)
            ]
            for u in range(BATCH):
                acc[pl.ds(where[u], 1), :] = fresh[u]
            return carry

        lax.fori_loop(0, tokens // BATCH, some, 0, unroll=True)
        return carry

    lax.fori_loop(0, senders, sender, 0)

    @pl.when(step == pl.num_programs(0) - 1)
    def _():
        def copy(i, slot, g):
            at = pl.multiple_of(g * height + i * width, width)
            return pltpu.make_async_copy(
                turned.at[slot, pl.ds(g * feats, feats)],
                out_ref.at[:, pl.ds(at, width)],
                sem.at[slot, g],
            )

        def turn(i, carry):
            slot = lax.rem(i, 2)

            @pl.when(i >= 2)
            def _():
                for g in range(groups):
                    copy(i - 2, slot, g).wait()

            at = pl.multiple_of(i * width, width)
            turned[slot] = (acc[pl.ds(at, width), :] * 32.0).T
            for g in range(groups):
                copy(i, slot, g).start()
            return carry

        count = height // width
        lax.fori_loop(0, count, turn, 0)
        for i in range(max(count - 2, 0), count):
            for g in range(groups):
                copy(i, i % 2, g).wait()


def scatter_tokens(grads, rows, row, group, vocab, per_core):
    n, feats, tokens = grads.shape
    groups = LANES // feats
    height = vocab // groups
    width = min(WIDTH, height)
    senders = math.gcd(n, SENDERS)
    token_spec = pl.BlockSpec((senders, 1, tokens), lambda s, r: (s, 0, 0))
    return pl.pallas_call(
        functools.partial(scatter_kernel, groups, per_core),
        out_shape=(
            jax.ShapeDtypeStruct((feats, vocab), f32),
            jax.ShapeDtypeStruct((CORES, feats, tokens), f32),
        ),
        grid_spec=pltpu.PrefetchScalarGridSpec(
            num_scalar_prefetch=1,
            grid=(n // senders,),
            in_specs=[
                token_spec,
                token_spec,
                pl.BlockSpec((senders, feats, tokens), lambda s, r: (s, 0, 0)),
            ],
            out_specs=(
                pl.BlockSpec(memory_space=pl.ANY),
                full((CORES, feats, tokens)),
            ),
            scratch_shapes=[
                pltpu.VMEM((height, LANES), f32),
                pltpu.VMEM((tokens, LANES), f32),
                pltpu.VMEM((2, LANES, width), f32),
                pltpu.SemaphoreType.DMA((2, groups)),
            ],
        ),
        compiler_params=params(),
        cost_estimate=cost(39),
        name="scatter_tokens",
    )(rows, row, group, grads)


def entry_kernel(
    info_ref, emb_ref, pos_a, pos_b, wq_ref, wkv_ref, gain_ref, bias_ref, x0_ref, x1_ref, a_ref, q_ref, kv_ref
):
    step = pl.program_id(0)
    half = x0_ref.shape[0] // 2

    @pl.when(step == 0)
    def _():
        for i, pos in enumerate((pos_a, pos_b)):
            at = slice(i * half, (i + 1) * half)
            places = joined([p[...] for p in pos], info_ref)
            x0 = (emb_ref[:, at].astype(f32) * 32.0 + places.astype(f32)).T
            x1 = normed(x0)[0] * gain_ref[0:1] + bias_ref[0:1]
            a = normed(x1)[0] * gain_ref[1:2] + bias_ref[1:2]
            x0_ref[at] = x0
            x1_ref[at] = x1
            a_ref[at] = a.astype(bf16)

    x = a_ref[...]
    span = wq_ref[0].shape[4]

    @pl.when(step == 0)
    def _():
        def store(at, y):
            q_ref[0, :, pl.ds(at, span)] = (y * HEAD_DIM**-0.5).astype(bf16)

        project(x, wq_ref, info_ref, store)

    @pl.when(step > 0)
    def _():
        def store(at, y):
            kv_ref[0, :, pl.ds(at, span)] = y.astype(bf16)

        project(x, wkv_ref, info_ref, store)


def entry(info, emb, first, gains, biases):
    width, tokens = emb.shape
    wq, wkv = first

    def pos_specs(i):
        return [
            pl.BlockSpec(
                (w.shape[0], 1, 1, w.shape[3], w.shape[4]),
                lambda s, info, skip=skip: (0, info[3 + i], skip, 0, 0),
            )
            for w, skip in wq
        ]

    row = full((tokens, width))
    rows = jax.ShapeDtypeStruct((tokens, width), f32)
    return call(
        entry_kernel,
        info,
        (3,),
        [
            (emb, full(emb.shape)),
            (wq, pos_specs(0)),
            (wq, pos_specs(1)),
            (wq, weight_specs(wq, lambda s: 1)),
            (wkv, weight_specs(wkv, lambda s: jnp.maximum(s - 1, 0))),
            (gains, full(gains.shape)),
            (biases, full(biases.shape)),
        ],
        [
            (rows, row),
            (rows, row),
            (jax.ShapeDtypeStruct((tokens, width), bf16), row),
            (jax.ShapeDtypeStruct((1, tokens, width), bf16), full((1, tokens, width))),
            (
                jax.ShapeDtypeStruct((2, tokens, width), bf16),
                pl.BlockSpec((1, tokens, width), lambda s, info: (jnp.maximum(s - 1, 0), 0, 0)),
            ),
        ],
        cost_estimate=cost(15),
        name="entry",
    )


def slots(pair, info_ref):
    odd = info_ref[9] == 1
    one, two = pair[0][...], pair[1][...]
    return jnp.where(odd, two, one), jnp.where(odd, one, two)


def put_slots(pair, info_ref, values):
    for odd in range(2):

        @pl.when(info_ref[9] == odd)
        def _():
            pair[odd][...] = values[0].astype(bf16)
            pair[1 - odd][...] = values[1].astype(bf16)


def source_kernel(info_ref, came_a, came_b, w_refs, x_ref, kv_ref):
    @pl.when(pl.program_id(0) == 0)
    def _():
        half = came_a.shape[0]
        x_ref[:half], x_ref[half:] = slots((came_a, came_b), info_ref)

    def store(at, y):
        kv_ref[0, :, pl.ds(at, w_refs[0].shape[4])] = y.astype(bf16)

    project(x_ref[...], w_refs, info_ref, store)


def source_keys(info, came, weights):
    half, width = came[0].shape
    tokens = 2 * half
    return call(
        source_kernel,
        info,
        (2,),
        [
            (came[0], full((half, width))),
            (came[1], full((half, width))),
            (weights, weight_specs(weights, lambda s: s)),
        ],
        [
            (jax.ShapeDtypeStruct((tokens, width), bf16), full((tokens, width))),
            (
                jax.ShapeDtypeStruct((2, tokens, width), bf16),
                pl.BlockSpec((1, tokens, width), lambda s, info: (s, 0, 0)),
            ),
        ],
        cost_estimate=cost(8),
        name="source_keys",
    )


def attend_kernel(causal, info_ref, q_ref, own_ref, par_ref, o_ref, p_ref, hide):
    tokens = q_ref.shape[1]
    half = tokens // 2
    core = info_ref[0]

    @pl.when(pl.program_id(0) == 0)
    def _():
        length = info_ref[1] if causal else info_ref[2]
        key = lax.broadcasted_iota(i32, (tokens, tokens), 0)
        query = lax.broadcasted_iota(i32, (tokens, tokens), 1)
        upper = key >= half
        own = key + jnp.where(upper, info_ref[4] - 1, info_ref[3]) * half
        par = key + jnp.where(upper, info_ref[6] - 1, info_ref[5]) * half
        at = query + jnp.where(query >= half, info_ref[4] - 1, info_ref[3]) * half
        for i, place in enumerate((own, par)):
            seen = place < length
            if causal:
                seen = seen & (place <= at)
            hide[i] = jnp.where(seen, 0.0, NEGATIVE)

    outs = []
    for h in range(LANES // HEAD_DIM):
        lanes = slice(h * HEAD_DIM, (h + 1) * HEAD_DIM)
        q = q_ref[0][:, lanes]
        s_own = dot(own_ref[0][:, lanes], q, NT) + hide[0]
        s_par = dot(par_ref[0][:, lanes], q, NT) + hide[1]
        top = jnp.maximum(
            jnp.max(s_own, axis=0, keepdims=True), jnp.max(s_par, axis=0, keepdims=True)
        )
        e_own = jnp.exp(s_own - top)
        e_par = jnp.exp(s_par - top)
        total = jnp.sum(e_own, axis=0, keepdims=True) + jnp.sum(e_par, axis=0, keepdims=True)
        scale = 1.0 / total
        p_own = (e_own * scale).astype(bf16)
        p_par = (e_par * scale).astype(bf16)
        p_ref[h, 0] = p_own
        p_ref[h, 1] = p_par
        outs.append(dot(own_ref[1][:, lanes], p_own, TN) + dot(par_ref[1][:, lanes], p_par, TN))
    o_ref[0] = jnp.concatenate(outs, axis=0).T.astype(bf16)


def attend(info, q, own, par, causal):
    _, tokens, width = q.shape
    heads = width // HEAD_DIM
    pair = LANES // HEAD_DIM
    one = pl.BlockSpec((1, tokens, LANES), lambda s, info: (0, 0, s))
    two = pl.BlockSpec((2, tokens, LANES), lambda s, info: (0, 0, s))
    return pl.pallas_call(
        functools.partial(attend_kernel, causal),
        out_shape=(
            jax.ShapeDtypeStruct((1, tokens, width), bf16),
            jax.ShapeDtypeStruct((heads, 2, tokens, tokens), bf16),
        ),
        grid_spec=pltpu.PrefetchScalarGridSpec(
            num_scalar_prefetch=1,
            grid=(heads // pair,),
            in_specs=[one, two, two],
            out_specs=(
                one,
                pl.BlockSpec((pair, 2, tokens, tokens), lambda s, info: (s, 0, 0, 0)),
            ),
            scratch_shapes=[pltpu.VMEM((2, tokens, tokens), f32)],
        ),
        compiler_params=params(),
        cost_estimate=cost(22),
        name="attend",
    )(info, q, own, par)


def middle_kernel(info_ref, o_ref, w_ref, x_ref, wq_ref, gain_ref, bias_ref, x2_ref, c_ref, q_ref):
    x2 = x_ref[...] + dot(o_ref[0], whole_weight(w_ref, info_ref), NT)
    x2_ref[...] = x2
    c = (normed(x2)[0] * gain_ref[2:3] + bias_ref[2:3]).astype(bf16)
    c_ref[...] = c

    def store(at, y):
        q_ref[0, :, pl.ds(at, wq_ref[0].shape[4])] = (y * HEAD_DIM**-0.5).astype(bf16)

    project(c, wq_ref, info_ref, store)


def middle(info, o, weights, x1, gains, biases):
    _, tokens, width = o.shape
    row = full((tokens, width))
    return call(
        middle_kernel,
        info,
        (1,),
        [
            (o, full(o.shape)),
            (weights, weight_specs(weights, lambda s: 0)),
            (x1, row),
            (weights, weight_specs(weights, lambda s: 1)),
            (gains, full(gains.shape)),
            (biases, full(biases.shape)),
        ],
        [
            (jax.ShapeDtypeStruct((tokens, width), f32), row),
            (jax.ShapeDtypeStruct((tokens, width), bf16), row),
            (jax.ShapeDtypeStruct((1, tokens, width), bf16), full((1, tokens, width))),
        ],
        cost_estimate=cost(9),
        name="middle",
    )


def feed_kernel(
    info_ref,
    o_ref,
    wo_ref,
    x_ref,
    w1_ref,
    w2_ref,
    gain_ref,
    bias_ref,
    x3_ref,
    f_ref,
    g_ref,
    slope_ref,
    x4_ref,
):
    step = pl.program_id(0)

    @pl.when(step == 0)
    def _():
        x3 = x_ref[...] + dot(o_ref[0], whole_weight(wo_ref, info_ref), NT)
        x3_ref[...] = x3
        f_ref[...] = (normed(x3)[0] * gain_ref[3:4] + bias_ref[3:4]).astype(bf16)
        x4_ref[...] = x3

    def store(at, u):
        bell = 0.5 + 0.5 * lax.erf(u * 0.7071067811865476)
        lanes = pl.ds(at, w1_ref[0].shape[4])
        g_ref[0, :, lanes] = (u * bell).astype(bf16)
        slope = bell + u * (0.3989422804014327 * jnp.exp(-0.5 * u * u))
        slope_ref[0, :, lanes] = slope.astype(bf16)

    project(f_ref[...], w1_ref, info_ref, store)
    x4_ref[...] += dot(g_ref[0], whole_weight(w2_ref, info_ref), NT)


def feed(info, o, wo, x2, w1, w2, gains, biases, slabs):
    _, tokens, width = o.shape
    blocks = slabs
    row = full((tokens, width))
    part = pl.BlockSpec((1, tokens, width), lambda s, info: (s, 0, 0))
    wide = jax.ShapeDtypeStruct((tokens, width), f32)
    slim = jax.ShapeDtypeStruct((tokens, width), bf16)
    many = jax.ShapeDtypeStruct((blocks, tokens, width), bf16)
    return call(
        feed_kernel,
        info,
        (blocks,),
        [
            (o, full(o.shape)),
            (wo, weight_specs(wo, lambda s: 2)),
            (x2, row),
            (w1, weight_specs(w1, lambda s: s)),
            (w2, weight_specs(w2, lambda s: s)),
            (gains, full(gains.shape)),
            (biases, full(biases.shape)),
        ],
        [(wide, row), (slim, row), (many, part), (many, part), (wide, row)],
        mib=60,
        cost_estimate=cost(28),
        name="feed",
    )


def feed_back_kernel(
    info_ref,
    x4_ref,
    og_a,
    og_b,
    slope_ref,
    w1_ref,
    w2_ref,
    x3_ref,
    wo_ref,
    gain_ref,
    bias_ref,
    hid_a,
    hid_b,
    g4b_ref,
    du_ref,
    g3_ref,
    g3b_ref,
    do_ref,
    sums_ref,
    total,
):
    step = pl.program_id(0)

    @pl.when(step == 0)
    def _():
        x4 = x4_ref[...]
        half = og_a.shape[0]
        hidden = normed(x4)[0] * gain_ref[4:5] + bias_ref[4:5]
        put_slots((hid_a, hid_b), info_ref, (hidden[:half], hidden[half:]))
        out_grad = jnp.concatenate(slots((og_a, og_b), info_ref), axis=0).astype(f32)
        g4, gain_grad, bias_grad = norm_back(x4, gain_ref[4:5], out_grad)
        g3_ref[...] = g4
        g4b_ref[...] = g4.astype(bf16)
        sums_ref[2:3] = gain_grad
        sums_ref[3:4] = bias_grad

    def store(at, y):
        lanes = pl.ds(at, w2_ref[0].shape[4])
        du_ref[0, :, lanes] = (y * slope_ref[0, :, lanes].astype(f32)).astype(bf16)

    project(g4b_ref[...], w2_ref, info_ref, store)
    part = dot(du_ref[0], whole_weight(w1_ref, info_ref), NT)

    @pl.when(step == 0)
    def _():
        total[...] = part

    @pl.when(step > 0)
    def _():
        total[...] += part

    @pl.when(step == pl.num_programs(0) - 1)
    def _():
        back, gain_grad, bias_grad = norm_back(x3_ref[...], gain_ref[3:4], total[...])
        g3 = g3_ref[...] + back
        g3_ref[...] = g3
        g3b = g3.astype(bf16)
        g3b_ref[...] = g3b
        sums_ref[0:1] = gain_grad
        sums_ref[1:2] = bias_grad

        def keep(at, y):
            do_ref[0, :, pl.ds(at, wo_ref[0].shape[4])] = y.astype(bf16)

        project(g3b, wo_ref, info_ref, keep)


def feed_back(info, x4, og, slope, wo, x3, w1, w2, gains, biases):
    blocks, tokens, width = slope.shape
    row = full((tokens, width))
    part_row = full((tokens // 2, width))
    part_shape = jax.ShapeDtypeStruct((tokens // 2, width), bf16)
    part = pl.BlockSpec((1, tokens, width), lambda s, info: (s, 0, 0))
    wide = jax.ShapeDtypeStruct((tokens, width), f32)
    slim = jax.ShapeDtypeStruct((tokens, width), bf16)
    return call(
        feed_back_kernel,
        info,
        (blocks,),
        [
            (x4, row),
            (og[0], part_row),
            (og[1], part_row),
            (slope, part),
            (w1, weight_specs(w1, lambda s: s)),
            (w2, weight_specs(w2, lambda s: s)),
            (x3, row),
            (wo, weight_specs(wo, lambda s: 2)),
            (gains, full(gains.shape)),
            (biases, full(biases.shape)),
        ],
        [
            (part_shape, part_row),
            (part_shape, part_row),
            (slim, row),
            (jax.ShapeDtypeStruct((blocks, tokens, width), bf16), part),
            (wide, row),
            (slim, row),
            (jax.ShapeDtypeStruct((1, tokens, width), bf16), full((1, tokens, width))),
            (jax.ShapeDtypeStruct((4, width), f32), full((4, width))),
        ],
        [pltpu.VMEM((tokens, width), f32)],
        60,
        cost_estimate=cost(28),
        name="feed_back",
    )


def attend_back_kernel(
    q_ref, own_ref, par_ref, p_ref, o_ref, do_ref, dq_ref, down_ref, dpar_ref
):
    flat = do_ref[0].astype(f32).T * o_ref[0].astype(f32).T
    outs = []
    for h in range(LANES // HEAD_DIM):
        lanes = slice(h * HEAD_DIM, (h + 1) * HEAD_DIM)
        q = q_ref[0][:, lanes]
        grad = do_ref[0][:, lanes]
        inner = jnp.sum(flat[lanes], axis=0, keepdims=True)
        back = None
        for i, (kv_ref, d_ref) in enumerate(((own_ref, down_ref), (par_ref, dpar_ref))):
            keys = kv_ref[0][:, lanes]
            probs = p_ref[h, i]
            d_probs = dot(kv_ref[1][:, lanes], grad, NT)
            d_scores = (probs.astype(f32) * (d_probs - inner)).astype(bf16)
            d_ref[1, :, lanes] = dot(probs, grad).astype(bf16)
            d_ref[0, :, lanes] = dot(d_scores, q).astype(bf16)
            some = dot(keys, d_scores, TN)
            back = some if back is None else back + some
        outs.append(back)
    dq_ref[0] = (jnp.concatenate(outs, axis=0).T * HEAD_DIM**-0.5).astype(bf16)


def attend_back(q, own, par, probs, o, do):
    _, tokens, width = q.shape
    heads = width // HEAD_DIM
    pair = LANES // HEAD_DIM
    one = pl.BlockSpec((1, tokens, LANES), lambda s: (0, 0, s))
    two = pl.BlockSpec((2, tokens, LANES), lambda s: (0, 0, s))
    kv = jax.ShapeDtypeStruct((2, tokens, width), bf16)
    return pl.pallas_call(
        attend_back_kernel,
        out_shape=(jax.ShapeDtypeStruct((1, tokens, width), bf16), kv, kv),
        grid=(heads // pair,),
        in_specs=[
            one,
            two,
            two,
            pl.BlockSpec((pair, 2, tokens, tokens), lambda s: (s, 0, 0, 0)),
            one,
            one,
        ],
        out_specs=(one, two, two),
        compiler_params=params(),
        cost_estimate=cost(21),
        name="attend_back",
    )(q, own, par, probs, o, do)


def causal_back_kernel(
    info_ref, q_ref, own_ref, par_ref, p_ref, o_ref, do_ref, dq_ref, down_ref, dpar_ref, back
):
    tokens = q_ref.shape[1]
    half = tokens // 2
    low, high, every = slice(0, half), slice(half, tokens), slice(0, tokens)
    flat = do_ref[0].astype(f32).T * o_ref[0].astype(f32).T
    inner = [
        jnp.sum(flat[h * HEAD_DIM : (h + 1) * HEAD_DIM], axis=0, keepdims=True)
        for h in range(LANES // HEAD_DIM)
    ]
    back[...] = jnp.zeros_like(back)

    def segments(i, kv_ref, d_ref, spans):
        for h in range(LANES // HEAD_DIM):
            lanes = slice(h * HEAD_DIM, (h + 1) * HEAD_DIM)
            for keys, queries in spans:
                grad = do_ref[0, queries, lanes]
                probs = p_ref[h, i, keys, queries]
                d_probs = dot(kv_ref[1, keys, lanes], grad, NT)
                d_scores = (probs.astype(f32) * (d_probs - inner[h][:, queries])).astype(bf16)
                d_ref[1, keys, lanes] = dot(probs, grad).astype(bf16)
                d_ref[0, keys, lanes] = dot(d_scores, q_ref[0, queries, lanes]).astype(bf16)
                back[lanes, queries] += dot(kv_ref[0, keys, lanes], d_scores, TN)

    segments(0, own_ref, down_ref, [(low, every), (high, high)])

    @pl.when(info_ref[0] == 0)
    def _():
        segments(1, par_ref, dpar_ref, [(every, high)])

    @pl.when(info_ref[0] == 1)
    def _():
        segments(1, par_ref, dpar_ref, [(low, every)])
        dpar_ref[:, high, :] = jnp.zeros((2, half, LANES), bf16)

    dq_ref[0] = (back[...].T * HEAD_DIM**-0.5).astype(bf16)


def causal_back(info, q, own, par, probs, o, do):
    _, tokens, width = q.shape
    heads = width // HEAD_DIM
    pair = LANES // HEAD_DIM
    one = pl.BlockSpec((1, tokens, LANES), lambda s, info: (0, 0, s))
    two = pl.BlockSpec((2, tokens, LANES), lambda s, info: (0, 0, s))
    kv = jax.ShapeDtypeStruct((2, tokens, width), bf16)
    return call(
        causal_back_kernel,
        info,
        (heads // pair,),
        [
            (q, one),
            (own, two),
            (par, two),
            (probs, pl.BlockSpec((pair, 2, tokens, tokens), lambda s, info: (s, 0, 0, 0))),
            (o, one),
            (do, one),
        ],
        [(jax.ShapeDtypeStruct((1, tokens, width), bf16), one), (kv, two), (kv, two)],
        [pltpu.VMEM((LANES, tokens), f32)],
        cost_estimate=cost(19),
        name="causal_back",
    )


def middle_back_kernel(
    info_ref, dq_ref, wq_ref, x2_ref, g3_ref, wo_ref, gain_ref, g2_ref, g2b_ref, do_ref, sums_ref
):
    d_normed = dot(dq_ref[0], whole_weight(wq_ref, info_ref), NT)
    back, gain_grad, bias_grad = norm_back(x2_ref[...], gain_ref[2:3], d_normed)
    g2 = g3_ref[...] + back
    g2_ref[...] = g2
    g2b = g2.astype(bf16)
    g2b_ref[...] = g2b
    sums_ref[0:1] = gain_grad
    sums_ref[1:2] = bias_grad

    def keep(at, y):
        do_ref[0, :, pl.ds(at, wo_ref[0].shape[4])] = y.astype(bf16)

    project(g2b, wo_ref, info_ref, keep)


def middle_back(info, dq, weights, x2, g3, gains):
    _, tokens, width = dq.shape
    row = full((tokens, width))
    return call(
        middle_back_kernel,
        info,
        (1,),
        [
            (dq, full(dq.shape)),
            (weights, weight_specs(weights, lambda s: 1)),
            (x2, row),
            (g3, row),
            (weights, weight_specs(weights, lambda s: 0)),
            (gains, full(gains.shape)),
        ],
        [
            (jax.ShapeDtypeStruct((tokens, width), f32), row),
            (jax.ShapeDtypeStruct((tokens, width), bf16), row),
            (jax.ShapeDtypeStruct((1, tokens, width), bf16), full((1, tokens, width))),
            (jax.ShapeDtypeStruct((2, width), f32), full((2, width))),
        ],
        cost_estimate=cost(10),
        name="middle_back",
    )


def source_back_kernel(info_ref, mine_ref, came_ref, w_ref, out_a, out_b, sum_ref, total):
    step = pl.program_id(0)
    grads = (mine_ref[0].astype(f32) + came_ref[0].astype(f32)).astype(bf16)
    sum_ref[0] = grads
    part = dot(grads, whole_weight(w_ref, info_ref), NT)

    @pl.when(step == 0)
    def _():
        total[...] = part

    @pl.when(step == pl.num_programs(0) - 1)
    def _():
        half = out_a.shape[0]
        both = total[...] + part
        put_slots((out_a, out_b), info_ref, (both[:half], both[half:]))


def source_back(info, mine, came, weights):
    parts, tokens, width = mine.shape
    part = pl.BlockSpec((1, tokens, width), lambda s, info: (s, 0, 0))
    return call(
        source_back_kernel,
        info,
        (parts,),
        [(mine, part), (came, part), (weights, weight_specs(weights, lambda s: s))],
        [
            (jax.ShapeDtypeStruct((tokens // 2, width), bf16), full((tokens // 2, width))),
            (jax.ShapeDtypeStruct((tokens // 2, width), bf16), full((tokens // 2, width))),
            (jax.ShapeDtypeStruct((parts, tokens, width), bf16), part),
        ],
        [pltpu.VMEM((tokens, width), f32)],
        cost_estimate=cost(7),
        name="source_back",
    )


def exit_kernel(
    info_ref,
    dq_ref,
    mine_ref,
    came_ref,
    wq_ref,
    wkv_ref,
    x1_ref,
    x0_ref,
    g2_ref,
    gain_ref,
    g0_ref,
    sum_ref,
    sums_ref,
    total,
):
    step = pl.program_id(0)

    @pl.when(step == 0)
    def _():
        total[...] = dot(dq_ref[0], whole_weight(wq_ref, info_ref), NT)

    @pl.when(step > 0)
    def _():
        grads = (mine_ref[0].astype(f32) + came_ref[0].astype(f32)).astype(bf16)
        sum_ref[0] = grads
        total[...] += dot(grads, whole_weight(wkv_ref, info_ref), NT)

    @pl.when(step == pl.num_programs(0) - 1)
    def _():
        back, gain_one, bias_one = norm_back(x1_ref[...], gain_ref[1:2], total[...])
        g1 = g2_ref[...] + back
        g0, gain_zero, bias_zero = norm_back(x0_ref[...], gain_ref[0:1], g1)
        g0_ref[...] = g0.T.astype(bf16)
        sums_ref[0:1] = gain_zero
        sums_ref[1:2] = bias_zero
        sums_ref[2:3] = gain_one
        sums_ref[3:4] = bias_one


def exit_back(info, dq, mine, came, first, x1, x0, g2, gains):
    _, tokens, width = dq.shape
    wq, wkv = first
    row = full((tokens, width))
    part = pl.BlockSpec((1, tokens, width), lambda s, info: (jnp.maximum(s - 1, 0), 0, 0))
    return call(
        exit_kernel,
        info,
        (3,),
        [
            (dq, full(dq.shape)),
            (mine, part),
            (came, part),
            (wq, weight_specs(wq, lambda s: 1)),
            (wkv, weight_specs(wkv, lambda s: jnp.maximum(s - 1, 0))),
            (x1, row),
            (x0, row),
            (g2, row),
            (gains, full(gains.shape)),
        ],
        [
            (jax.ShapeDtypeStruct((width, tokens), bf16), full((width, tokens))),
            (jax.ShapeDtypeStruct((2, tokens, width), bf16), part),
            (jax.ShapeDtypeStruct((4, width), f32), full((4, width))),
        ],
        [pltpu.VMEM((tokens, width), f32)],
        cost_estimate=cost(15),
        name="exit_back",
    )


def weight_grad_kernel(chips, aliased, info_ref, xo_ref, xp_ref, yo_ref, yp_ref, *refs):
    out_ref, turned = refs[-2], refs[-1]
    tokens, width = xo_ref.shape
    rows = width // (chips * CORES)
    core = info_ref[0]

    @pl.when(pl.program_id(0) == 0)
    def _():
        for i, x_ref in enumerate((xo_ref, xp_ref)):
            at = slice(i * tokens, (i + 1) * tokens)
            if rows % LANES == 0:
                for j in range(chips):
                    lanes = pl.ds(pl.multiple_of((2 * j + core) * rows, rows), rows)
                    turned[j * rows : (j + 1) * rows, at] = x_ref[:, lanes].astype(f32).T.astype(bf16)
            else:
                tall = x_ref[...].astype(f32).T.reshape(chips, CORES, rows, tokens)
                mine = jnp.where(core == 0, tall[:, 0], tall[:, 1])
                turned[:, at] = mine.reshape(chips * rows, tokens).astype(bf16)

    y_own, y_par = yo_ref[0], yp_ref[0]
    blocks, span = out_ref.shape[1], out_ref.shape[4]
    result = dot(turned[:, :tokens], y_own) + dot(turned[:, tokens:], y_par)
    for m in range(blocks):
        part = result[:, m * span : (m + 1) * span].astype(bf16)
        out_ref[:, m, 0] = part.reshape(chips, rows, span)


def weight_grad(info, x_own, x_par, y_own, y_par, shape, at, before=None):
    parts, tokens, width = y_own.shape
    chips = shape[0]
    row = full(x_own.shape)
    part = pl.BlockSpec((1, tokens, width), lambda s, info: (s, 0, 0))
    extra = [] if before is None else [before]
    return pl.pallas_call(
        functools.partial(weight_grad_kernel, chips, before is not None),
        out_shape=jax.ShapeDtypeStruct(shape, bf16),
        grid_spec=pltpu.PrefetchScalarGridSpec(
            num_scalar_prefetch=1,
            grid=(parts,),
            in_specs=[row, row, part, part] + [pl.BlockSpec(memory_space=pl.ANY) for _ in extra],
            out_specs=pl.BlockSpec(
                (chips, shape[1], 1, shape[3], shape[4]), lambda s, info: (0, 0, s + at, 0, 0)
            ),
            scratch_shapes=[pltpu.VMEM((x_own.shape[1] // 2, 2 * tokens), bf16)],
        ),
        input_output_aliases={} if before is None else {5: 0},
        compiler_params=params(),
        cost_estimate=cost(3 + 2 * parts),
        name="weight_grad",
    )(info, x_own, x_par, y_own, y_par, *extra)


def swap(value):
    return lax.ppermute(value, "core", [(0, 1), (1, 0)])


def line_moves(mp):
    rounds = []
    for turn in range(2):
        moves = []
        for c in range(CORES):
            for m in range(mp):
                target, slot = (1 if m in (1, 2) else 0), m // 2
                moves.append((c * mp + m, target * mp + 2 * c + (slot ^ turn)))
        rounds.append(moves)
    return rounds


def to_chips(value, mp):
    slot = lax.axis_index("mp") // 2
    return [
        lax.ppermute(jnp.where((slot ^ turn) == 0, value[0], value[1]), LINE, moves)
        for turn, moves in enumerate(line_moves(mp))
    ]


def from_chips(pair, mp):
    return [
        lax.ppermute(sent, LINE, [(b, a) for a, b in moves])
        for sent, moves in zip(pair, line_moves(mp))
    ]


def placed_again(came):
    slot = lax.axis_index("mp") // 2
    one, two = [c.astype(f32) for c in came]
    return jnp.stack([jnp.where(slot == 0, one, two), jnp.where(slot == 0, two, one)])


def packed(*weights):
    return jnp.concatenate([w.reshape(-1, w.shape[-1]) for w in weights], axis=0)


X_SWAP = [(0, 1), (1, 0), (2, 3), (3, 2)]
Y_SWAP = [(0, 2), (2, 0), (1, 3), (3, 1)]
def gathered(rows, unit, chips, mp):
    value = lax.all_gather(rows, ALL, axis=0, tiled=False)
    return value.reshape(chips * CORES, mp, -1, unit, rows.shape[-1])


def gathered_line(rows, unit, mp):
    value = lax.all_gather(rows, "mp", axis=0, tiled=False)
    return value.reshape(mp, -1, unit, rows.shape[-1])


class Spread:
    def __init__(self, value, cut):
        self.own, self.cut = [value], cut
        self.near, self.far, self.both = [], [], []
        self.swapped = {}

    def begin(self, *others):
        self.own = tied(self.own, *others)
        sets = [self.own[0][:, : self.cut], self.own[0][:, self.cut :]]
        self.near = [lax.ppermute(w, "chip", p) for w, p in zip(sets, (X_SWAP, Y_SWAP))]
        self.far = [lax.ppermute(w, "chip", p) for w, p in zip(sets, (Y_SWAP, X_SWAP))]

    def finish(self, *others):
        self.near = tied(self.near, *others)
        self.both = [lax.ppermute(w, "chip", p) for w, p in zip(self.near, (Y_SWAP, X_SWAP))]

    def swap(self, *names):
        for name in names:
            self.swapped[name] = [swap(w) for w in getattr(self, name)]

    def hold(self, *others):
        state = [self.own, self.near, self.far, self.both, self.swapped]
        state, others = lax.optimization_barrier((state, others))
        self.own, self.near, self.far, self.both, self.swapped = state
        return others if len(others) > 1 else others[0]

    def pieces(self):
        found = []
        for i in range(2):
            pieces = []
            for name in ("own", "near", "far", "both") if i == 0 else ("own", "far", "near", "both"):
                at, skip = (0, i * self.cut) if name == "own" else (i, 0)
                for group in (getattr(self, name), self.swapped[name]):
                    pieces.append((group[at][None], skip))
            found.append(pieces)
        return found


def tied(value, *others):
    return after(value, *others) if others else value


def scattered(grads, axis):
    return lax.psum_scatter(grads, axis, scatter_dimension=0, tiled=False)


def sent_over(grads, axis, size):
    me = lax.axis_index(axis)
    terms = []
    for k in range(size):
        if axis == "chip" and size == 4:
            to, perm = me ^ k, [(i, i ^ k) for i in range(size)]
        else:
            to, perm = (me + k) % size, [(i, (i + k) % size) for i in range(size)]
        part = lax.dynamic_index_in_dim(grads, to, axis=0, keepdims=False)
        terms.append(part if k == 0 else lax.ppermute(part, axis, perm))
    return terms


def summed(terms):
    return sum([t.astype(f32) for t in terms[1:]], start=terms[0].astype(f32))


def total_over(value, axis, size):
    terms = [
        lax.ppermute(value, axis, [(i, (i + k) % size) for i in range(size)])
        for k in range(1, size)
    ]
    return sum(terms, start=value)


def after(value, *others):
    return lax.optimization_barrier((value, others))[0]


def body(
    chips,
    mp,
    target_ids,
    tgt_lengths,
    encoder_states,
    src_lengths,
    table,
    pos_table,
    self_query_key_value_weight,
    self_output_weight,
    cross_query_weight,
    cross_key_value_weight,
    cross_output_weight,
    feedforward_input_weight,
    feedforward_output_weight,
    norm_gains,
    norm_biases,
    out_grad,
):
    dp = chips * CORES
    n = dp * mp
    seqs, block = target_ids.shape
    assert seqs * CORES == mp == 4
    tokens = seqs * block
    width = norm_gains.shape[1]
    vocab = table.shape[1]
    feats = table.shape[0]
    rows = pos_table.shape[0]
    core, m, chip = lax.axis_index("core"), lax.axis_index("mp"), lax.axis_index("chip")

    def split(weight):
        return weight.reshape(rows, -1, block).transpose(1, 0, 2)

    own_ids = jnp.broadcast_to(target_ids.reshape(1, tokens), (n, tokens))
    all_ids = lax.all_to_all(own_ids, ALL, split_axis=0, concat_axis=0, tiled=True)
    sub = feedforward_input_weight.shape[1] // block
    first = packed(pos_table, split(self_query_key_value_weight))
    second = packed(
        self_output_weight, cross_query_weight, split(cross_key_value_weight), cross_output_weight
    )
    third = packed(split(feedforward_input_weight), split(feedforward_output_weight))
    sub = feedforward_input_weight.shape[1] // block
    second = gathered(second, rows, chips, mp)
    third = gathered(third, rows, chips, mp)
    second = [(second, 0)], [(second, 2)]
    third = [(third, 0)], [(third, sub)]
    stepped = chips == 4
    if stepped:
        copies = jnp.broadcast_to(first[None], (mp,) + first.shape)
        copies = lax.all_to_all(after(copies, all_ids), "mp", split_axis=0, concat_axis=0, tiled=True)
        first = Spread(copies.reshape(mp, -1, rows, block), 2)
    else:
        first = gathered(first, rows, chips, mp)
        first = [(first, 0)], [(first, 2)]

    lengths = jnp.stack([tgt_lengths, src_lengths])
    other = swap(lengths)
    lengths = jnp.where(
        core == 0,
        jnp.concatenate([lengths, other], axis=1),
        jnp.concatenate([other, lengths], axis=1),
    )
    lengths = lax.dynamic_index_in_dim(lengths, m, axis=1, keepdims=False)
    info = jnp.stack(
        [
            core,
            lengths[0],
            lengths[1],
            core,
            3 - core,
            1 - core,
            2 + core,
            chip % 2,
            chip // 2,
            m % 2,
        ]
    ).astype(i32)

    ids = all_ids.reshape(chips, CORES, mp, seqs, block)
    ids = jnp.stack([ids[:, :, 0], ids[:, :, 3], ids[:, :, 1], ids[:, :, 2]], axis=2)
    ids = ids.reshape(chips, CORES, CORES, 2, seqs, block).transpose(0, 2, 1, 4, 3, 5)
    ids = ids.reshape(n, 1, tokens)
    height = vocab // (LANES // feats)
    row, group = ids % height, ids // height
    flat_row = row.reshape(-1)

    picked = gather_tokens(table, flat_row, group)
    if stepped:
        picked = first.hold(picked)
        first.begin(picked)
        first.finish()
        first.swap("own", "near", "far", "both")
        first = first.pieces()
    emb = lax.all_to_all(picked, ALL, split_axis=0, concat_axis=0, tiled=True)
    emb = emb.reshape(width, tokens)

    x0, x1, a, q, kv = entry(info, emb, first, norm_gains, norm_biases)
    states = to_chips(after(encoder_states, a), mp)
    kv_par = swap(kv)
    outs = attend(info, q, kv, kv_par, True)
    (o, probs), states = lax.optimization_barrier((outs, states))
    states, ckv = source_keys(info, states, second[1])
    ckv_par = swap(ckv)
    x2, c, cq = middle(info, after(o, ckv), second[0], x1, norm_gains, norm_biases)
    oc, cprobs = attend(info, cq, ckv, ckv_par, False)
    og = to_chips(after(out_grad.astype(bf16), oc), mp)
    w1, w2 = third
    oc_par, c_par = swap(oc), swap(after(c, oc))
    outs = feed(info, oc, second[1], x2, w1, w2, norm_gains, norm_biases, sub)
    (x3, f, g, slope, x4), og, oc_par, c_par = lax.optimization_barrier((outs, og, oc_par, c_par))
    f_par, g_par = swap(f), swap(g)
    a_par, o_par, states_par = [swap(after(v, x4)) for v in (a, o, states)]
    outs = feed_back(info, x4, og, slope, second[1], x3, w1, w2, norm_gains, norm_biases)
    outs, f_par, g_par, a_par, o_par, states_par = lax.optimization_barrier(
        (outs, f_par, g_par, a_par, o_par, states_par)
    )
    *hid, g4b, du, g3, g3b, doc, sums34 = outs
    g4b_par, g3b_par, du_par = swap(g4b), swap(g3b), swap(du)
    hidden_out = from_chips(tied(hid, g4b_par), mp)
    shape = (chips, mp, sub, rows, block)
    grads = weight_grad(info, g4b, g4b_par, g, g_par, shape, 0)
    part_one = scattered(grads, "chip")
    shape = (chips, mp, sub + 1, rows, block)
    grads = weight_grad(info, after(g3b, grads), g3b_par, oc, oc_par, shape, sub)
    grads = weight_grad(info, after(f, grads), f_par, du, du_par, shape, 0, grads)
    doc, hidden_out = lax.optimization_barrier((after(doc, grads), hidden_out))

    outs = attend_back(cq, ckv, ckv_par, cprobs, oc, doc)
    (dcq, dckv_own, dckv_par), part_one = lax.optimization_barrier((outs, part_one))
    part_two = scattered(after(grads, part_one), "chip")
    dckv_came, dcq_par = swap(dckv_par), swap(dcq)
    outs = middle_back(info, dcq, second[0], x2, g3, norm_gains)
    (g2, g2b, do, sums2), dckv_came, dcq_par, dckv_own = lax.optimization_barrier(
        (outs, dckv_came, dcq_par, dckv_own)
    )
    g2b_par = swap(g2b)
    outs = source_back(info, dckv_own, dckv_came, second[1])
    *enc_grad, dckv = outs
    dckv_after = swap(dckv)
    shape = (chips, mp, 4, rows, block)
    grads = weight_grad(info, c, c_par, after(dcq, dckv), dcq_par, shape, 0)
    grads = weight_grad(info, g2b, g2b_par, o, o_par, shape, 1, grads)
    grads = weight_grad(info, states, states_par, dckv, dckv_after, shape, 2, grads)
    do = after(do, grads)
    cross_grads = grads
    encoder_grad = from_chips(tied(enc_grad, grads), mp)

    outs = causal_back(info, q, kv, kv_par, probs, o, do)
    (dq, dkv_own, dkv_par), encoder_grad, part_two = lax.optimization_barrier(
        (outs, encoder_grad, part_two)
    )
    cross_part = scattered(after(cross_grads, part_two), "chip")
    dkv_came = swap(dkv_par)
    dq_par = swap(dq)
    outs = exit_back(info, dq, dkv_own, dkv_came, first, x1, x0, g2, norm_gains)
    (g0, dkv, sums01), dq_par = lax.optimization_barrier((outs, dq_par))
    sent = g0.reshape(n, feats, tokens)
    arrived = lax.all_to_all(sent, ALL, split_axis=0, concat_axis=0, tiled=True)
    sums = jnp.concatenate((sums01, sums2, sums34), axis=0)
    sums_par = swap(sums)
    shape = (chips, mp, 3, rows, block)
    dkv_after = swap(dkv)
    grads = weight_grad(info, a, a_par, dq, dq_par, shape, 0)
    grads, sums_par = lax.optimization_barrier((grads, sums_par))
    sums = total_over(sums + sums_par, "chip", chips)
    grads = weight_grad(info, a, a_par, dkv, dkv_after, shape, 1, grads)
    sums, grads, arrived, cross_part = lax.optimization_barrier((sums, grads, arrived, cross_part))
    sums_up = scattered(jnp.concatenate([part_one, part_two, cross_part], axis=1), "mp")
    self_terms = lax.all_to_all(grads, "chip", split_axis=0, concat_axis=0, tiled=True)
    sums = total_over(sums, "mp", mp)

    outs = scatter_tokens(arrived, flat_row, row, group, vocab, mp)
    (table_grad, places), self_terms, sums = lax.optimization_barrier((outs, self_terms, sums))
    hidden_out = placed_again(tied(hidden_out, places))
    encoder_grad = placed_again(tied(encoder_grad, places))
    self_part = jnp.sum(self_terms.astype(f32), axis=0).astype(bf16)
    self_grads = summed(sent_over(self_part, "mp", mp))
    sums_up = sums_up.astype(f32)
    feed_out_grads, feed_in_grads, cross_grads = (
        sums_up[:sub],
        sums_up[sub : 2 * sub + 1],
        sums_up[2 * sub + 1 :],
    )

    blocks = places.reshape(CORES, feats, 2, block).transpose(0, 2, 1, 3).reshape(4, feats, block)
    blocks = jnp.stack([blocks[0], blocks[2], blocks[3], blocks[1]])
    parts = []
    for k in range(mp):
        mine = lax.dynamic_index_in_dim(blocks, (m + k) % mp, axis=0, keepdims=False)
        parts.append(
            mine if k == 0 else lax.ppermute(mine, "mp", [(i, (i + k) % mp) for i in range(mp)])
        )
    pos_grad = []
    for source in range(mp):
        value = parts[0]
        for k in range(1, mp):
            value = jnp.where((m - source) % mp == k, parts[k], value)
        pos_grad.append(value)
    pos_grad = jnp.concatenate(pos_grad, axis=0)

    def join(parts):
        return parts.transpose(1, 0, 2)

    return (
        hidden_out,
        table_grad,
        pos_grad,
        join(self_grads),
        cross_grads[1],
        cross_grads[0],
        join(cross_grads[2:4]),
        feed_in_grads[sub],
        join(feed_in_grads[:sub]).reshape(rows, -1),
        join(feed_out_grads).reshape(rows, -1),
        sums[0::2],
        sums[1::2],
        encoder_grad,
    )


def solution(mesh):
    dp, mp = mesh.devices.shape
    chips = dp // CORES
    fine = Mesh(mesh.devices.reshape(chips, CORES, mp), ALL)
    both = ("chip", "core")
    placed = (
        P(both, "mp"),
        P(both),
        P(both, "mp", None),
        P(both),
        P(ALL, None),
        P(both, "mp"),
        P(both, None, "mp"),
        P(both, "mp"),
        P(both, "mp"),
        P(both, None, "mp"),
        P(both, "mp"),
        P(both, "mp"),
        P(both, "mp"),
        P(),
        P(),
        P(both, "mp", None),
    )
    return jax.shard_map(
        functools.partial(body, chips, mp),
        mesh=fine,
        in_specs=placed,
        out_specs=(
            P(both, "mp", None),
            P(ALL, None),
            P(both, "mp"),
            P(both, None, "mp"),
            P(both, "mp"),
            P(both, "mp"),
            P(both, None, "mp"),
            P(both, "mp"),
            P(both, "mp"),
            P(both, "mp"),
            P(),
            P(),
            P(both, "mp", None),
        ),
        check_vma=False,
    )
```

```python
import functools
import math

import jax
import jax.numpy as jnp
from jax import lax
from jax.experimental import pallas as pl
from jax.experimental.pallas import tpu as pltpu
from jax.sharding import Mesh
from jax.sharding import PartitionSpec as P

HEAD_DIM = 64
EPSILON = 1e-05
NEGATIVE = -1e30
LANES = 128
ALL = ("chip", "core", "mp")
LINE = ("core", "mp")
CORES = 2

f32 = jnp.float32
bf16 = jnp.bfloat16
i32 = jnp.int32

NT = (((1,), (1,)), ((), ()))
NN = (((1,), (0,)), ((), ()))
TN = (((0,), (0,)), ((), ()))


def dot(a, b, dims=NN):
    return lax.dot_general(a, b, dims, preferred_element_type=f32)


def params(mib=56):
    return pltpu.CompilerParams(vmem_limit_bytes=mib << 20)


def cost(microseconds):
    return pl.CostEstimate(flops=0, bytes_accessed=int(microseconds * 3.2e6), transcendentals=0)


def normed(values):
    centred = values - jnp.mean(values, axis=-1, keepdims=True)
    inverse = lax.rsqrt(jnp.mean(centred * centred, axis=-1, keepdims=True) + EPSILON)
    return centred * inverse, inverse


def norm_back(values, gain, grad):
    hat, inverse = normed(values)
    scaled = grad * gain
    first = jnp.mean(scaled, axis=-1, keepdims=True)
    second = jnp.mean(scaled * hat, axis=-1, keepdims=True)
    back = inverse * (scaled - first - hat * second)
    gain_grad = jnp.sum(grad * hat, axis=0, keepdims=True)
    bias_grad = jnp.sum(grad, axis=0, keepdims=True)
    return back, gain_grad, bias_grad


def in_order(pieces, info_ref):
    for bit, place in ((0, 0), (1, 7), (2, 8)):
        far = info_ref[place] == 1
        turned = []
        for i, piece in enumerate(pieces):
            turned.append(jnp.where(far, pieces[i ^ (1 << bit)], piece))
        pieces = turned
    return pieces


def joined(blocks, info_ref):
    flat = [b.reshape(-1, b.shape[-1]) for b in blocks]
    return flat[0] if len(flat) == 1 else jnp.concatenate(in_order(flat, info_ref), axis=0)


def columns(w_refs, m, info_ref):
    return joined([w[:, pl.ds(m, 1)] for w in w_refs], info_ref)


def whole_weight(w_refs, info_ref):
    parts = [columns(w_refs, m, info_ref) for m in range(w_refs[0].shape[1])]
    return jnp.concatenate(parts, axis=1)


def project(x, w_refs, info_ref, store):
    width = w_refs[0].shape[4]

    def step(m, carry):
        store(pl.multiple_of(m * width, width), dot(x, columns(w_refs, m, info_ref)))
        return carry

    lax.fori_loop(0, w_refs[0].shape[1], step, 0, unroll=True)


def weight_specs(weights, index):
    return [
        pl.BlockSpec(
            (w.shape[0], w.shape[1], 1, w.shape[3], w.shape[4]),
            lambda s, info, skip=skip: (0, 0, index(s) + skip, 0, 0),
        )
        for w, skip in weights
    ]


def call(kernel, info, grid, operands, outs, scratch=(), mib=56, **others):
    arrays, specs, sizes = [], [], []
    for value, spec in operands:
        group = isinstance(value, (list, tuple))
        sizes.append(len(value) if group else None)
        arrays.extend([w for w, _ in value] if group else [value])
        specs.extend(spec if group else [spec])

    def body(info_ref, *refs):
        given, rest, at = [], refs, 0
        for size in sizes:
            given.append(refs[at] if size is None else list(refs[at : at + size]))
            at += 1 if size is None else size
        kernel(info_ref, *given, *rest[at:])

    return pl.pallas_call(
        body,
        out_shape=[o for o, _ in outs],
        grid_spec=pltpu.PrefetchScalarGridSpec(
            num_scalar_prefetch=1,
            grid=grid,
            in_specs=specs,
            out_specs=[o for _, o in outs],
            scratch_shapes=list(scratch),
        ),
        compiler_params=params(mib),
        **others,
    )(info, *arrays)


def full(shape):
    return pl.BlockSpec(shape, lambda *a: (0,) * len(shape))


def gather_kernel(groups, fill, rows_ref, group_ref, *refs):
    tables, out_ref, turned, picked = refs[:groups], refs[groups], refs[-2], refs[-1]
    step = pl.program_id(0)
    feats, width = tables[0].shape
    tokens = picked.shape[0]

    @pl.when(step < fill)
    def _():
        stacked = jnp.concatenate([t[...].astype(f32) for t in tables], axis=0).astype(bf16)
        row = lax.broadcasted_iota(i32, (256, 256), 0)
        eye = jnp.where(row == lax.broadcasted_iota(i32, (256, 256), 1), 1.0, 0.0).astype(bf16)
        for k in range(width // 256):
            at = pl.multiple_of(step * width + k * 256, 256)
            turned[pl.ds(at, 256), :] = dot(eye, stacked[:, k * 256 : (k + 1) * 256], NT)

    @pl.when(step >= fill)
    def _():
        base = (step - fill) * tokens

        def some(k, carry):
            for u in range(16):
                t = k * 16 + u
                picked[pl.ds(t, 1), :] = turned[pl.ds(rows_ref[base + t], 1), :]
            return carry

        lax.fori_loop(0, tokens // 16, some, 0)
        row = lax.broadcasted_iota(i32, (LANES, LANES), 0)
        eye = jnp.where(row == lax.broadcasted_iota(i32, (LANES, LANES), 1), 1.0, 0.0)
        across = dot(eye.astype(bf16), picked[...].astype(bf16), NT)
        own = lax.broadcasted_iota(i32, (LANES, tokens), 0) // feats == group_ref[0]
        kept = jnp.where(own, across, 0.0)
        total = kept[:feats]
        for g in range(1, groups):
            total = total + kept[g * feats : (g + 1) * feats]
        out_ref[0] = total.astype(out_ref.dtype)


def gather_tokens(table, rows, group):
    feats, vocab = table.shape
    groups = LANES // feats
    height = vocab // groups
    n, _, tokens = group.shape
    width = min(2048, height)
    fill = height // width

    def table_spec(g):
        return pl.BlockSpec(
            (feats, width), lambda s, r, g=g: (0, g * fill + jnp.minimum(s, fill - 1))
        )

    return pl.pallas_call(
        functools.partial(gather_kernel, groups, fill),
        out_shape=jax.ShapeDtypeStruct((n, feats, tokens), bf16),
        grid_spec=pltpu.PrefetchScalarGridSpec(
            num_scalar_prefetch=1,
            grid=(fill + n,),
            in_specs=[pl.BlockSpec((1, 1, tokens), lambda s, r: (jnp.maximum(s - fill, 0), 0, 0))]
            + [table_spec(g) for g in range(groups)],
            out_specs=pl.BlockSpec(
                (1, feats, tokens), lambda s, r: (jnp.maximum(s - fill, 0), 0, 0)
            ),
            scratch_shapes=[pltpu.VMEM((height, LANES), f32), pltpu.VMEM((tokens, LANES), f32)],
        ),
        compiler_params=params(),
        cost_estimate=cost(45),
        name="gather_tokens",
    )(rows, group, *([table] * groups))


BATCH = 16
WIDTH = 4096
SENDERS = 8


def scatter_kernel(
    groups, per_core, rows_ref, row_ref, group_ref, grad_ref, out_ref, pos_ref, acc, update, turned, sem
):
    step = pl.program_id(0)
    senders, feats, tokens = grad_ref.shape
    height = acc.shape[0]
    width = turned.shape[2]

    @pl.when(step == 0)
    def _():
        def clear(k, carry):
            acc[pl.ds(pl.multiple_of(k * 256, 256), 256), :] = jnp.zeros((256, LANES), f32)
            return carry

        lax.fori_loop(0, height // 256, clear, 0)
        pos_ref[...] = jnp.zeros_like(pos_ref)

    row = lax.broadcasted_iota(i32, (LANES, LANES), 0)
    col = lax.broadcasted_iota(i32, (LANES, LANES), 1)
    near = row // BATCH == col // BATCH

    def sender(d, carry):
        place = step * senders + d
        grads = grad_ref[d].astype(f32)
        core = lax.rem(lax.div(place, per_core), CORES)
        pos_ref[core] += grads
        tall = jnp.concatenate([grads] * groups, axis=0)
        own = lax.broadcasted_iota(i32, (LANES, tokens), 0) // feats == group_ref[d]
        tall = jnp.where(own, tall, 0.0).astype(bf16)
        for b in range(tokens // LANES):
            at = slice(b * LANES, (b + 1) * LANES)
            along = jnp.broadcast_to(row_ref[d][:, at].astype(f32), (LANES, LANES))
            same = jnp.where((along == along.T) & near, 1.0, 0.0).astype(bf16)
            update[at, :] = dot(same, tall[:, at], NT)
        base = place * tokens

        def some(k, carry):
            where = [rows_ref[base + k * BATCH + u] for u in range(BATCH)]
            fresh = [
                acc[pl.ds(where[u], 1), :] + update[pl.ds(k * BATCH + u, 1), :]
                for u in range(BATCH)
            ]
            for u in range(BATCH):
                acc[pl.ds(where[u], 1), :] = fresh[u]
            return carry

        lax.fori_loop(0, tokens // BATCH, some, 0, unroll=True)
        return carry

    lax.fori_loop(0, senders, sender, 0)

    @pl.when(step == pl.num_programs(0) - 1)
    def _():
        def copy(i, slot, g):
            at = pl.multiple_of(g * height + i * width, width)
            return pltpu.make_async_copy(
                turned.at[slot, pl.ds(g * feats, feats)],
                out_ref.at[:, pl.ds(at, width)],
                sem.at[slot, g],
            )

        def turn(i, carry):
            slot = lax.rem(i, 2)

            @pl.when(i >= 2)
            def _():
                for g in range(groups):
                    copy(i - 2, slot, g).wait()

            at = pl.multiple_of(i * width, width)
            turned[slot] = (acc[pl.ds(at, width), :] * 32.0).T
            for g in range(groups):
                copy(i, slot, g).start()
            return carry

        count = height // width
        lax.fori_loop(0, count, turn, 0)
        for i in range(max(count - 2, 0), count):
            for g in range(groups):
                copy(i, i % 2, g).wait()


def scatter_tokens(grads, rows, row, group, vocab, per_core):
    n, feats, tokens = grads.shape
    groups = LANES // feats
    height = vocab // groups
    width = min(WIDTH, height)
    senders = math.gcd(n, SENDERS)
    token_spec = pl.BlockSpec((senders, 1, tokens), lambda s, r: (s, 0, 0))
    return pl.pallas_call(
        functools.partial(scatter_kernel, groups, per_core),
        out_shape=(
            jax.ShapeDtypeStruct((feats, vocab), f32),
            jax.ShapeDtypeStruct((CORES, feats, tokens), f32),
        ),
        grid_spec=pltpu.PrefetchScalarGridSpec(
            num_scalar_prefetch=1,
            grid=(n // senders,),
            in_specs=[
                token_spec,
                token_spec,
                pl.BlockSpec((senders, feats, tokens), lambda s, r: (s, 0, 0)),
            ],
            out_specs=(
                pl.BlockSpec(memory_space=pl.ANY),
                full((CORES, feats, tokens)),
            ),
            scratch_shapes=[
                pltpu.VMEM((height, LANES), f32),
                pltpu.VMEM((tokens, LANES), f32),
                pltpu.VMEM((2, LANES, width), f32),
                pltpu.SemaphoreType.DMA((2, groups)),
            ],
        ),
        compiler_params=params(),
        cost_estimate=cost(39),
        name="scatter_tokens",
    )(rows, row, group, grads)


def entry_kernel(
    info_ref, emb_ref, pos_a, pos_b, wq_ref, wkv_ref, gain_ref, bias_ref, x0_ref, x1_ref, a_ref, q_ref, kv_ref
):
    step = pl.program_id(0)
    half = x0_ref.shape[0] // 2

    @pl.when(step == 0)
    def _():
        for i, pos in enumerate((pos_a, pos_b)):
            at = slice(i * half, (i + 1) * half)
            places = joined([p[...] for p in pos], info_ref)
            x0 = (emb_ref[:, at].astype(f32) * 32.0 + places.astype(f32)).T
            x1 = normed(x0)[0] * gain_ref[0:1] + bias_ref[0:1]
            a = normed(x1)[0] * gain_ref[1:2] + bias_ref[1:2]
            x0_ref[at] = x0
            x1_ref[at] = x1
            a_ref[at] = a.astype(bf16)

    x = a_ref[...]
    span = wq_ref[0].shape[4]

    @pl.when(step == 0)
    def _():
        def store(at, y):
            q_ref[0, :, pl.ds(at, span)] = (y * HEAD_DIM**-0.5).astype(bf16)

        project(x, wq_ref, info_ref, store)

    @pl.when(step > 0)
    def _():
        def store(at, y):
            kv_ref[0, :, pl.ds(at, span)] = y.astype(bf16)

        project(x, wkv_ref, info_ref, store)


def entry(info, emb, first, gains, biases):
    width, tokens = emb.shape
    wq, wkv = first

    def pos_specs(i):
        return [
            pl.BlockSpec(
                (w.shape[0], 1, 1, w.shape[3], w.shape[4]),
                lambda s, info, skip=skip: (0, info[3 + i], skip, 0, 0),
            )
            for w, skip in wq
        ]

    row = full((tokens, width))
    rows = jax.ShapeDtypeStruct((tokens, width), f32)
    return call(
        entry_kernel,
        info,
        (3,),
        [
            (emb, full(emb.shape)),
            (wq, pos_specs(0)),
            (wq, pos_specs(1)),
            (wq, weight_specs(wq, lambda s: 1)),
            (wkv, weight_specs(wkv, lambda s: jnp.maximum(s - 1, 0))),
            (gains, full(gains.shape)),
            (biases, full(biases.shape)),
        ],
        [
            (rows, row),
            (rows, row),
            (jax.ShapeDtypeStruct((tokens, width), bf16), row),
            (jax.ShapeDtypeStruct((1, tokens, width), bf16), full((1, tokens, width))),
            (
                jax.ShapeDtypeStruct((2, tokens, width), bf16),
                pl.BlockSpec((1, tokens, width), lambda s, info: (jnp.maximum(s - 1, 0), 0, 0)),
            ),
        ],
        cost_estimate=cost(15),
        name="entry",
    )


def slots(pair, info_ref):
    odd = info_ref[9] == 1
    one, two = pair[0][...], pair[1][...]
    return jnp.where(odd, two, one), jnp.where(odd, one, two)


def put_slots(pair, info_ref, values):
    for odd in range(2):

        @pl.when(info_ref[9] == odd)
        def _():
            pair[odd][...] = values[0].astype(bf16)
            pair[1 - odd][...] = values[1].astype(bf16)


def source_kernel(info_ref, came_a, came_b, w_refs, x_ref, kv_ref):
    @pl.when(pl.program_id(0) == 0)
    def _():
        half = came_a.shape[0]
        x_ref[:half], x_ref[half:] = slots((came_a, came_b), info_ref)

    def store(at, y):
        kv_ref[0, :, pl.ds(at, w_refs[0].shape[4])] = y.astype(bf16)

    project(x_ref[...], w_refs, info_ref, store)


def source_keys(info, came, weights):
    half, width = came[0].shape
    tokens = 2 * half
    return call(
        source_kernel,
        info,
        (2,),
        [
            (came[0], full((half, width))),
            (came[1], full((half, width))),
            (weights, weight_specs(weights, lambda s: s)),
        ],
        [
            (jax.ShapeDtypeStruct((tokens, width), bf16), full((tokens, width))),
            (
                jax.ShapeDtypeStruct((2, tokens, width), bf16),
                pl.BlockSpec((1, tokens, width), lambda s, info: (s, 0, 0)),
            ),
        ],
        cost_estimate=cost(8),
        name="source_keys",
    )


def attend_kernel(causal, info_ref, q_ref, own_ref, par_ref, o_ref, p_ref, hide):
    tokens = q_ref.shape[1]
    half = tokens // 2
    core = info_ref[0]

    @pl.when(pl.program_id(0) == 0)
    def _():
        length = info_ref[1] if causal else info_ref[2]
        key = lax.broadcasted_iota(i32, (tokens, tokens), 0)
        query = lax.broadcasted_iota(i32, (tokens, tokens), 1)
        upper = key >= half
        own = key + jnp.where(upper, info_ref[4] - 1, info_ref[3]) * half
        par = key + jnp.where(upper, info_ref[6] - 1, info_ref[5]) * half
        at = query + jnp.where(query >= half, info_ref[4] - 1, info_ref[3]) * half
        for i, place in enumerate((own, par)):
            seen = place < length
            if causal:
                seen = seen & (place <= at)
            hide[i] = jnp.where(seen, 0.0, NEGATIVE)

    outs = []
    for h in range(LANES // HEAD_DIM):
        lanes = slice(h * HEAD_DIM, (h + 1) * HEAD_DIM)
        q = q_ref[0][:, lanes]
        s_own = dot(own_ref[0][:, lanes], q, NT) + hide[0]
        s_par = dot(par_ref[0][:, lanes], q, NT) + hide[1]
        top = jnp.maximum(
            jnp.max(s_own, axis=0, keepdims=True), jnp.max(s_par, axis=0, keepdims=True)
        )
        e_own = jnp.exp(s_own - top)
        e_par = jnp.exp(s_par - top)
        total = jnp.sum(e_own, axis=0, keepdims=True) + jnp.sum(e_par, axis=0, keepdims=True)
        scale = 1.0 / total
        p_own = (e_own * scale).astype(bf16)
        p_par = (e_par * scale).astype(bf16)
        p_ref[h, 0] = p_own
        p_ref[h, 1] = p_par
        outs.append(dot(own_ref[1][:, lanes], p_own, TN) + dot(par_ref[1][:, lanes], p_par, TN))
    o_ref[0] = jnp.concatenate(outs, axis=0).T.astype(bf16)


def attend(info, q, own, par, causal):
    _, tokens, width = q.shape
    heads = width // HEAD_DIM
    pair = LANES // HEAD_DIM
    one = pl.BlockSpec((1, tokens, LANES), lambda s, info: (0, 0, s))
    two = pl.BlockSpec((2, tokens, LANES), lambda s, info: (0, 0, s))
    return pl.pallas_call(
        functools.partial(attend_kernel, causal),
        out_shape=(
            jax.ShapeDtypeStruct((1, tokens, width), bf16),
            jax.ShapeDtypeStruct((heads, 2, tokens, tokens), bf16),
        ),
        grid_spec=pltpu.PrefetchScalarGridSpec(
            num_scalar_prefetch=1,
            grid=(heads // pair,),
            in_specs=[one, two, two],
            out_specs=(
                one,
                pl.BlockSpec((pair, 2, tokens, tokens), lambda s, info: (s, 0, 0, 0)),
            ),
            scratch_shapes=[pltpu.VMEM((2, tokens, tokens), f32)],
        ),
        compiler_params=params(),
        cost_estimate=cost(22),
        name="attend",
    )(info, q, own, par)


def middle_kernel(info_ref, o_ref, w_ref, x_ref, wq_ref, gain_ref, bias_ref, x2_ref, c_ref, q_ref):
    x2 = x_ref[...] + dot(o_ref[0], whole_weight(w_ref, info_ref), NT)
    x2_ref[...] = x2
    c = (normed(x2)[0] * gain_ref[2:3] + bias_ref[2:3]).astype(bf16)
    c_ref[...] = c

    def store(at, y):
        q_ref[0, :, pl.ds(at, wq_ref[0].shape[4])] = (y * HEAD_DIM**-0.5).astype(bf16)

    project(c, wq_ref, info_ref, store)


def middle(info, o, weights, x1, gains, biases):
    _, tokens, width = o.shape
    row = full((tokens, width))
    return call(
        middle_kernel,
        info,
        (1,),
        [
            (o, full(o.shape)),
            (weights, weight_specs(weights, lambda s: 0)),
            (x1, row),
            (weights, weight_specs(weights, lambda s: 1)),
            (gains, full(gains.shape)),
            (biases, full(biases.shape)),
        ],
        [
            (jax.ShapeDtypeStruct((tokens, width), f32), row),
            (jax.ShapeDtypeStruct((tokens, width), bf16), row),
            (jax.ShapeDtypeStruct((1, tokens, width), bf16), full((1, tokens, width))),
        ],
        cost_estimate=cost(9),
        name="middle",
    )


def feed_kernel(
    info_ref,
    o_ref,
    wo_ref,
    x_ref,
    w1_ref,
    w2_ref,
    gain_ref,
    bias_ref,
    x3_ref,
    f_ref,
    g_ref,
    slope_ref,
    x4_ref,
):
    step = pl.program_id(0)

    @pl.when(step == 0)
    def _():
        x3 = x_ref[...] + dot(o_ref[0], whole_weight(wo_ref, info_ref), NT)
        x3_ref[...] = x3
        f_ref[...] = (normed(x3)[0] * gain_ref[3:4] + bias_ref[3:4]).astype(bf16)
        x4_ref[...] = x3

    def store(at, u):
        bell = 0.5 + 0.5 * lax.erf(u * 0.7071067811865476)
        lanes = pl.ds(at, w1_ref[0].shape[4])
        g_ref[0, :, lanes] = (u * bell).astype(bf16)
        slope = bell + u * (0.3989422804014327 * jnp.exp(-0.5 * u * u))
        slope_ref[0, :, lanes] = slope.astype(bf16)

    project(f_ref[...], w1_ref, info_ref, store)
    x4_ref[...] += dot(g_ref[0], whole_weight(w2_ref, info_ref), NT)


def feed(info, o, wo, x2, w1, w2, gains, biases, slabs):
    _, tokens, width = o.shape
    blocks = slabs
    row = full((tokens, width))
    part = pl.BlockSpec((1, tokens, width), lambda s, info: (s, 0, 0))
    wide = jax.ShapeDtypeStruct((tokens, width), f32)
    slim = jax.ShapeDtypeStruct((tokens, width), bf16)
    many = jax.ShapeDtypeStruct((blocks, tokens, width), bf16)
    return call(
        feed_kernel,
        info,
        (blocks,),
        [
            (o, full(o.shape)),
            (wo, weight_specs(wo, lambda s: 2)),
            (x2, row),
            (w1, weight_specs(w1, lambda s: s)),
            (w2, weight_specs(w2, lambda s: s)),
            (gains, full(gains.shape)),
            (biases, full(biases.shape)),
        ],
        [(wide, row), (slim, row), (many, part), (many, part), (wide, row)],
        mib=60,
        cost_estimate=cost(28),
        name="feed",
    )


def feed_back_kernel(
    info_ref,
    x4_ref,
    og_a,
    og_b,
    slope_ref,
    w1_ref,
    w2_ref,
    x3_ref,
    wo_ref,
    gain_ref,
    bias_ref,
    hid_a,
    hid_b,
    g4b_ref,
    du_ref,
    g3_ref,
    g3b_ref,
    do_ref,
    sums_ref,
    total,
):
    step = pl.program_id(0)

    @pl.when(step == 0)
    def _():
        x4 = x4_ref[...]
        half = og_a.shape[0]
        hidden = normed(x4)[0] * gain_ref[4:5] + bias_ref[4:5]
        put_slots((hid_a, hid_b), info_ref, (hidden[:half], hidden[half:]))
        out_grad = jnp.concatenate(slots((og_a, og_b), info_ref), axis=0).astype(f32)
        g4, gain_grad, bias_grad = norm_back(x4, gain_ref[4:5], out_grad)
        g3_ref[...] = g4
        g4b_ref[...] = g4.astype(bf16)
        sums_ref[2:3] = gain_grad
        sums_ref[3:4] = bias_grad

    def store(at, y):
        lanes = pl.ds(at, w2_ref[0].shape[4])
        du_ref[0, :, lanes] = (y * slope_ref[0, :, lanes].astype(f32)).astype(bf16)

    project(g4b_ref[...], w2_ref, info_ref, store)
    part = dot(du_ref[0], whole_weight(w1_ref, info_ref), NT)

    @pl.when(step == 0)
    def _():
        total[...] = part

    @pl.when(step > 0)
    def _():
        total[...] += part

    @pl.when(step == pl.num_programs(0) - 1)
    def _():
        back, gain_grad, bias_grad = norm_back(x3_ref[...], gain_ref[3:4], total[...])
        g3 = g3_ref[...] + back
        g3_ref[...] = g3
        g3b = g3.astype(bf16)
        g3b_ref[...] = g3b
        sums_ref[0:1] = gain_grad
        sums_ref[1:2] = bias_grad

        def keep(at, y):
            do_ref[0, :, pl.ds(at, wo_ref[0].shape[4])] = y.astype(bf16)

        project(g3b, wo_ref, info_ref, keep)


def feed_back(info, x4, og, slope, wo, x3, w1, w2, gains, biases):
    blocks, tokens, width = slope.shape
    row = full((tokens, width))
    part_row = full((tokens // 2, width))
    part_shape = jax.ShapeDtypeStruct((tokens // 2, width), bf16)
    part = pl.BlockSpec((1, tokens, width), lambda s, info: (s, 0, 0))
    wide = jax.ShapeDtypeStruct((tokens, width), f32)
    slim = jax.ShapeDtypeStruct((tokens, width), bf16)
    return call(
        feed_back_kernel,
        info,
        (blocks,),
        [
            (x4, row),
            (og[0], part_row),
            (og[1], part_row),
            (slope, part),
            (w1, weight_specs(w1, lambda s: s)),
            (w2, weight_specs(w2, lambda s: s)),
            (x3, row),
            (wo, weight_specs(wo, lambda s: 2)),
            (gains, full(gains.shape)),
            (biases, full(biases.shape)),
        ],
        [
            (part_shape, part_row),
            (part_shape, part_row),
            (slim, row),
            (jax.ShapeDtypeStruct((blocks, tokens, width), bf16), part),
            (wide, row),
            (slim, row),
            (jax.ShapeDtypeStruct((1, tokens, width), bf16), full((1, tokens, width))),
            (jax.ShapeDtypeStruct((4, width), f32), full((4, width))),
        ],
        [pltpu.VMEM((tokens, width), f32)],
        60,
        cost_estimate=cost(28),
        name="feed_back",
    )


def attend_back_kernel(
    q_ref, own_ref, par_ref, p_ref, o_ref, do_ref, dq_ref, down_ref, dpar_ref
):
    flat = do_ref[0].astype(f32).T * o_ref[0].astype(f32).T
    outs = []
    for h in range(LANES // HEAD_DIM):
        lanes = slice(h * HEAD_DIM, (h + 1) * HEAD_DIM)
        q = q_ref[0][:, lanes]
        grad = do_ref[0][:, lanes]
        inner = jnp.sum(flat[lanes], axis=0, keepdims=True)
        back = None
        for i, (kv_ref, d_ref) in enumerate(((own_ref, down_ref), (par_ref, dpar_ref))):
            keys = kv_ref[0][:, lanes]
            probs = p_ref[h, i]
            d_probs = dot(kv_ref[1][:, lanes], grad, NT)
            d_scores = (probs.astype(f32) * (d_probs - inner)).astype(bf16)
            d_ref[1, :, lanes] = dot(probs, grad).astype(bf16)
            d_ref[0, :, lanes] = dot(d_scores, q).astype(bf16)
            some = dot(keys, d_scores, TN)
            back = some if back is None else back + some
        outs.append(back)
    dq_ref[0] = (jnp.concatenate(outs, axis=0).T * HEAD_DIM**-0.5).astype(bf16)


def attend_back(q, own, par, probs, o, do):
    _, tokens, width = q.shape
    heads = width // HEAD_DIM
    pair = LANES // HEAD_DIM
    one = pl.BlockSpec((1, tokens, LANES), lambda s: (0, 0, s))
    two = pl.BlockSpec((2, tokens, LANES), lambda s: (0, 0, s))
    kv = jax.ShapeDtypeStruct((2, tokens, width), bf16)
    return pl.pallas_call(
        attend_back_kernel,
        out_shape=(jax.ShapeDtypeStruct((1, tokens, width), bf16), kv, kv),
        grid=(heads // pair,),
        in_specs=[
            one,
            two,
            two,
            pl.BlockSpec((pair, 2, tokens, tokens), lambda s: (s, 0, 0, 0)),
            one,
            one,
        ],
        out_specs=(one, two, two),
        compiler_params=params(),
        cost_estimate=cost(21),
        name="attend_back",
    )(q, own, par, probs, o, do)


def causal_back_kernel(
    info_ref, q_ref, own_ref, par_ref, p_ref, o_ref, do_ref, dq_ref, down_ref, dpar_ref, back
):
    tokens = q_ref.shape[1]
    half = tokens // 2
    low, high, every = slice(0, half), slice(half, tokens), slice(0, tokens)
    flat = do_ref[0].astype(f32).T * o_ref[0].astype(f32).T
    inner = [
        jnp.sum(flat[h * HEAD_DIM : (h + 1) * HEAD_DIM], axis=0, keepdims=True)
        for h in range(LANES // HEAD_DIM)
    ]
    back[...] = jnp.zeros_like(back)

    def segments(i, kv_ref, d_ref, spans):
        for h in range(LANES // HEAD_DIM):
            lanes = slice(h * HEAD_DIM, (h + 1) * HEAD_DIM)
            for keys, queries in spans:
                grad = do_ref[0, queries, lanes]
                probs = p_ref[h, i, keys, queries]
                d_probs = dot(kv_ref[1, keys, lanes], grad, NT)
                d_scores = (probs.astype(f32) * (d_probs - inner[h][:, queries])).astype(bf16)
                d_ref[1, keys, lanes] = dot(probs, grad).astype(bf16)
                d_ref[0, keys, lanes] = dot(d_scores, q_ref[0, queries, lanes]).astype(bf16)
                back[lanes, queries] += dot(kv_ref[0, keys, lanes], d_scores, TN)

    segments(0, own_ref, down_ref, [(low, every), (high, high)])

    @pl.when(info_ref[0] == 0)
    def _():
        segments(1, par_ref, dpar_ref, [(every, high)])

    @pl.when(info_ref[0] == 1)
    def _():
        segments(1, par_ref, dpar_ref, [(low, every)])
        dpar_ref[:, high, :] = jnp.zeros((2, half, LANES), bf16)

    dq_ref[0] = (back[...].T * HEAD_DIM**-0.5).astype(bf16)


def causal_back(info, q, own, par, probs, o, do):
    _, tokens, width = q.shape
    heads = width // HEAD_DIM
    pair = LANES // HEAD_DIM
    one = pl.BlockSpec((1, tokens, LANES), lambda s, info: (0, 0, s))
    two = pl.BlockSpec((2, tokens, LANES), lambda s, info: (0, 0, s))
    kv = jax.ShapeDtypeStruct((2, tokens, width), bf16)
    return call(
        causal_back_kernel,
        info,
        (heads // pair,),
        [
            (q, one),
            (own, two),
            (par, two),
            (probs, pl.BlockSpec((pair, 2, tokens, tokens), lambda s, info: (s, 0, 0, 0))),
            (o, one),
            (do, one),
        ],
        [(jax.ShapeDtypeStruct((1, tokens, width), bf16), one), (kv, two), (kv, two)],
        [pltpu.VMEM((LANES, tokens), f32)],
        cost_estimate=cost(19),
        name="causal_back",
    )


def middle_back_kernel(
    info_ref, dq_ref, wq_ref, x2_ref, g3_ref, wo_ref, gain_ref, g2_ref, g2b_ref, do_ref, sums_ref
):
    d_normed = dot(dq_ref[0], whole_weight(wq_ref, info_ref), NT)
    back, gain_grad, bias_grad = norm_back(x2_ref[...], gain_ref[2:3], d_normed)
    g2 = g3_ref[...] + back
    g2_ref[...] = g2
    g2b = g2.astype(bf16)
    g2b_ref[...] = g2b
    sums_ref[0:1] = gain_grad
    sums_ref[1:2] = bias_grad

    def keep(at, y):
        do_ref[0, :, pl.ds(at, wo_ref[0].shape[4])] = y.astype(bf16)

    project(g2b, wo_ref, info_ref, keep)


def middle_back(info, dq, weights, x2, g3, gains):
    _, tokens, width = dq.shape
    row = full((tokens, width))
    return call(
        middle_back_kernel,
        info,
        (1,),
        [
            (dq, full(dq.shape)),
            (weights, weight_specs(weights, lambda s: 1)),
            (x2, row),
            (g3, row),
            (weights, weight_specs(weights, lambda s: 0)),
            (gains, full(gains.shape)),
        ],
        [
            (jax.ShapeDtypeStruct((tokens, width), f32), row),
            (jax.ShapeDtypeStruct((tokens, width), bf16), row),
            (jax.ShapeDtypeStruct((1, tokens, width), bf16), full((1, tokens, width))),
            (jax.ShapeDtypeStruct((2, width), f32), full((2, width))),
        ],
        cost_estimate=cost(10),
        name="middle_back",
    )


def source_back_kernel(info_ref, mine_ref, came_ref, w_ref, out_a, out_b, sum_ref, total):
    step = pl.program_id(0)
    grads = (mine_ref[0].astype(f32) + came_ref[0].astype(f32)).astype(bf16)
    sum_ref[0] = grads
    part = dot(grads, whole_weight(w_ref, info_ref), NT)

    @pl.when(step == 0)
    def _():
        total[...] = part

    @pl.when(step == pl.num_programs(0) - 1)
    def _():
        half = out_a.shape[0]
        both = total[...] + part
        put_slots((out_a, out_b), info_ref, (both[:half], both[half:]))


def source_back(info, mine, came, weights):
    parts, tokens, width = mine.shape
    part = pl.BlockSpec((1, tokens, width), lambda s, info: (s, 0, 0))
    return call(
        source_back_kernel,
        info,
        (parts,),
        [(mine, part), (came, part), (weights, weight_specs(weights, lambda s: s))],
        [
            (jax.ShapeDtypeStruct((tokens // 2, width), bf16), full((tokens // 2, width))),
            (jax.ShapeDtypeStruct((tokens // 2, width), bf16), full((tokens // 2, width))),
            (jax.ShapeDtypeStruct((parts, tokens, width), bf16), part),
        ],
        [pltpu.VMEM((tokens, width), f32)],
        cost_estimate=cost(7),
        name="source_back",
    )


def exit_kernel(
    info_ref,
    dq_ref,
    mine_ref,
    came_ref,
    wq_ref,
    wkv_ref,
    x1_ref,
    x0_ref,
    g2_ref,
    gain_ref,
    g0_ref,
    sum_ref,
    sums_ref,
    total,
):
    step = pl.program_id(0)

    @pl.when(step == 0)
    def _():
        total[...] = dot(dq_ref[0], whole_weight(wq_ref, info_ref), NT)

    @pl.when(step > 0)
    def _():
        grads = (mine_ref[0].astype(f32) + came_ref[0].astype(f32)).astype(bf16)
        sum_ref[0] = grads
        total[...] += dot(grads, whole_weight(wkv_ref, info_ref), NT)

    @pl.when(step == pl.num_programs(0) - 1)
    def _():
        back, gain_one, bias_one = norm_back(x1_ref[...], gain_ref[1:2], total[...])
        g1 = g2_ref[...] + back
        g0, gain_zero, bias_zero = norm_back(x0_ref[...], gain_ref[0:1], g1)
        g0_ref[...] = g0.T.astype(bf16)
        sums_ref[0:1] = gain_zero
        sums_ref[1:2] = bias_zero
        sums_ref[2:3] = gain_one
        sums_ref[3:4] = bias_one


def exit_back(info, dq, mine, came, first, x1, x0, g2, gains):
    _, tokens, width = dq.shape
    wq, wkv = first
    row = full((tokens, width))
    part = pl.BlockSpec((1, tokens, width), lambda s, info: (jnp.maximum(s - 1, 0), 0, 0))
    return call(
        exit_kernel,
        info,
        (3,),
        [
            (dq, full(dq.shape)),
            (mine, part),
            (came, part),
            (wq, weight_specs(wq, lambda s: 1)),
            (wkv, weight_specs(wkv, lambda s: jnp.maximum(s - 1, 0))),
            (x1, row),
            (x0, row),
            (g2, row),
            (gains, full(gains.shape)),
        ],
        [
            (jax.ShapeDtypeStruct((width, tokens), bf16), full((width, tokens))),
            (jax.ShapeDtypeStruct((2, tokens, width), bf16), part),
            (jax.ShapeDtypeStruct((4, width), f32), full((4, width))),
        ],
        [pltpu.VMEM((tokens, width), f32)],
        cost_estimate=cost(15),
        name="exit_back",
    )


def weight_grad_kernel(chips, aliased, info_ref, xo_ref, xp_ref, yo_ref, yp_ref, *refs):
    out_ref, turned = refs[-2], refs[-1]
    tokens, width = xo_ref.shape
    rows = width // (chips * CORES)
    core = info_ref[0]

    @pl.when(pl.program_id(0) == 0)
    def _():
        for i, x_ref in enumerate((xo_ref, xp_ref)):
            at = slice(i * tokens, (i + 1) * tokens)
            if rows % LANES == 0:
                for j in range(chips):
                    lanes = pl.ds(pl.multiple_of((2 * j + core) * rows, rows), rows)
                    turned[j * rows : (j + 1) * rows, at] = x_ref[:, lanes].astype(f32).T.astype(bf16)
            else:
                tall = x_ref[...].astype(f32).T.reshape(chips, CORES, rows, tokens)
                mine = jnp.where(core == 0, tall[:, 0], tall[:, 1])
                turned[:, at] = mine.reshape(chips * rows, tokens).astype(bf16)

    y_own, y_par = yo_ref[0], yp_ref[0]
    blocks, span = out_ref.shape[1], out_ref.shape[4]
    result = dot(turned[:, :tokens], y_own) + dot(turned[:, tokens:], y_par)
    for m in range(blocks):
        part = result[:, m * span : (m + 1) * span].astype(bf16)
        out_ref[:, m, 0] = part.reshape(chips, rows, span)


def weight_grad(info, x_own, x_par, y_own, y_par, shape, at, before=None):
    parts, tokens, width = y_own.shape
    chips = shape[0]
    row = full(x_own.shape)
    part = pl.BlockSpec((1, tokens, width), lambda s, info: (s, 0, 0))
    extra = [] if before is None else [before]
    return pl.pallas_call(
        functools.partial(weight_grad_kernel, chips, before is not None),
        out_shape=jax.ShapeDtypeStruct(shape, bf16),
        grid_spec=pltpu.PrefetchScalarGridSpec(
            num_scalar_prefetch=1,
            grid=(parts,),
            in_specs=[row, row, part, part] + [pl.BlockSpec(memory_space=pl.ANY) for _ in extra],
            out_specs=pl.BlockSpec(
                (chips, shape[1], 1, shape[3], shape[4]), lambda s, info: (0, 0, s + at, 0, 0)
            ),
            scratch_shapes=[pltpu.VMEM((x_own.shape[1] // 2, 2 * tokens), bf16)],
        ),
        input_output_aliases={} if before is None else {5: 0},
        compiler_params=params(),
        cost_estimate=cost(3 + 2 * parts),
        name="weight_grad",
    )(info, x_own, x_par, y_own, y_par, *extra)


def swap(value):
    return lax.ppermute(value, "core", [(0, 1), (1, 0)])


def line_moves(mp):
    rounds = []
    for turn in range(2):
        moves = []
        for c in range(CORES):
            for m in range(mp):
                target, slot = (1 if m in (1, 2) else 0), m // 2
                moves.append((c * mp + m, target * mp + 2 * c + (slot ^ turn)))
        rounds.append(moves)
    return rounds


def to_chips(value, mp):
    slot = lax.axis_index("mp") // 2
    return [
        lax.ppermute(jnp.where((slot ^ turn) == 0, value[0], value[1]), LINE, moves)
        for turn, moves in enumerate(line_moves(mp))
    ]


def from_chips(pair, mp):
    return [
        lax.ppermute(sent, LINE, [(b, a) for a, b in moves])
        for sent, moves in zip(pair, line_moves(mp))
    ]


def placed_again(came):
    slot = lax.axis_index("mp") // 2
    one, two = [c.astype(f32) for c in came]
    return jnp.stack([jnp.where(slot == 0, one, two), jnp.where(slot == 0, two, one)])


def packed(*weights):
    return jnp.concatenate([w.reshape(-1, w.shape[-1]) for w in weights], axis=0)


X_SWAP = [(0, 1), (1, 0), (2, 3), (3, 2)]
Y_SWAP = [(0, 2), (2, 0), (1, 3), (3, 1)]
def gathered(rows, unit, chips, mp):
    value = lax.all_gather(rows, ALL, axis=0, tiled=False)
    return value.reshape(chips * CORES, mp, -1, unit, rows.shape[-1])


def gathered_line(rows, unit, mp):
    value = lax.all_gather(rows, "mp", axis=0, tiled=False)
    return value.reshape(mp, -1, unit, rows.shape[-1])


class Spread:
    def __init__(self, value, cut):
        self.own, self.cut = [value], cut
        self.near, self.far, self.both = [], [], []
        self.swapped = {}

    def begin(self, *others):
        self.own = tied(self.own, *others)
        sets = [self.own[0][:, : self.cut], self.own[0][:, self.cut :]]
        self.near = [lax.ppermute(w, "chip", p) for w, p in zip(sets, (X_SWAP, Y_SWAP))]
        self.far = [lax.ppermute(w, "chip", p) for w, p in zip(sets, (Y_SWAP, X_SWAP))]

    def finish(self, *others):
        self.near = tied(self.near, *others)
        self.both = [lax.ppermute(w, "chip", p) for w, p in zip(self.near, (Y_SWAP, X_SWAP))]

    def swap(self, *names):
        for name in names:
            self.swapped[name] = [swap(w) for w in getattr(self, name)]

    def hold(self, *others):
        state = [self.own, self.near, self.far, self.both, self.swapped]
        state, others = lax.optimization_barrier((state, others))
        self.own, self.near, self.far, self.both, self.swapped = state
        return others if len(others) > 1 else others[0]

    def pieces(self):
        found = []
        for i in range(2):
            pieces = []
            for name in ("own", "near", "far", "both") if i == 0 else ("own", "far", "near", "both"):
                at, skip = (0, i * self.cut) if name == "own" else (i, 0)
                for group in (getattr(self, name), self.swapped[name]):
                    pieces.append((group[at][None], skip))
            found.append(pieces)
        return found


def tied(value, *others):
    return after(value, *others) if others else value


def scattered(grads, axis):
    return lax.psum_scatter(grads, axis, scatter_dimension=0, tiled=False)


def sent_over(grads, axis, size):
    me = lax.axis_index(axis)
    terms = []
    for k in range(size):
        if axis == "chip" and size == 4:
            to, perm = me ^ k, [(i, i ^ k) for i in range(size)]
        else:
            to, perm = (me + k) % size, [(i, (i + k) % size) for i in range(size)]
        part = lax.dynamic_index_in_dim(grads, to, axis=0, keepdims=False)
        terms.append(part if k == 0 else lax.ppermute(part, axis, perm))
    return terms


def summed(terms):
    return sum([t.astype(f32) for t in terms[1:]], start=terms[0].astype(f32))


def total_over(value, axis, size):
    terms = [
        lax.ppermute(value, axis, [(i, (i + k) % size) for i in range(size)])
        for k in range(1, size)
    ]
    return sum(terms, start=value)


def after(value, *others):
    return lax.optimization_barrier((value, others))[0]


def body(
    chips,
    mp,
    target_ids,
    tgt_lengths,
    encoder_states,
    src_lengths,
    table,
    pos_table,
    self_query_key_value_weight,
    self_output_weight,
    cross_query_weight,
    cross_key_value_weight,
    cross_output_weight,
    feedforward_input_weight,
    feedforward_output_weight,
    norm_gains,
    norm_biases,
    out_grad,
):
    dp = chips * CORES
    n = dp * mp
    seqs, block = target_ids.shape
    assert seqs * CORES == mp == 4
    tokens = seqs * block
    width = norm_gains.shape[1]
    vocab = table.shape[1]
    feats = table.shape[0]
    rows = pos_table.shape[0]
    core, m, chip = lax.axis_index("core"), lax.axis_index("mp"), lax.axis_index("chip")

    def split(weight):
        return weight.reshape(rows, -1, block).transpose(1, 0, 2)

    own_ids = jnp.broadcast_to(target_ids.reshape(1, tokens), (n, tokens))
    all_ids = lax.all_to_all(own_ids, ALL, split_axis=0, concat_axis=0, tiled=True)
    sub = feedforward_input_weight.shape[1] // block
    first = packed(pos_table, split(self_query_key_value_weight))
    second = packed(
        self_output_weight, cross_query_weight, split(cross_key_value_weight), cross_output_weight
    )
    third = packed(split(feedforward_input_weight), split(feedforward_output_weight))
    sub = feedforward_input_weight.shape[1] // block
    second = gathered(second, rows, chips, mp)
    third = gathered(third, rows, chips, mp)
    second = [(second, 0)], [(second, 2)]
    third = [(third, 0)], [(third, sub)]
    stepped = chips == 4
    if stepped:
        copies = jnp.broadcast_to(first[None], (mp,) + first.shape)
        copies = lax.all_to_all(after(copies, all_ids), "mp", split_axis=0, concat_axis=0, tiled=True)
        first = Spread(copies.reshape(mp, -1, rows, block), 2)
    else:
        first = gathered(first, rows, chips, mp)
        first = [(first, 0)], [(first, 2)]

    lengths = jnp.stack([tgt_lengths, src_lengths])
    other = swap(lengths)
    lengths = jnp.where(
        core == 0,
        jnp.concatenate([lengths, other], axis=1),
        jnp.concatenate([other, lengths], axis=1),
    )
    lengths = lax.dynamic_index_in_dim(lengths, m, axis=1, keepdims=False)
    info = jnp.stack(
        [
            core,
            lengths[0],
            lengths[1],
            core,
            3 - core,
            1 - core,
            2 + core,
            chip % 2,
            chip // 2,
            m % 2,
        ]
    ).astype(i32)

    ids = all_ids.reshape(chips, CORES, mp, seqs, block)
    ids = jnp.stack([ids[:, :, 0], ids[:, :, 3], ids[:, :, 1], ids[:, :, 2]], axis=2)
    ids = ids.reshape(chips, CORES, CORES, 2, seqs, block).transpose(0, 2, 1, 4, 3, 5)
    ids = ids.reshape(n, 1, tokens)
    height = vocab // (LANES // feats)
    row, group = ids % height, ids // height
    flat_row = row.reshape(-1)

    picked = gather_tokens(table, flat_row, group)
    if stepped:
        picked = first.hold(picked)
        first.begin(picked)
        first.finish()
        first.swap("own", "near", "far", "both")
        first = first.pieces()
    emb = lax.all_to_all(picked, ALL, split_axis=0, concat_axis=0, tiled=True)
    emb = emb.reshape(width, tokens)

    x0, x1, a, q, kv = entry(info, emb, first, norm_gains, norm_biases)
    states = to_chips(after(encoder_states, a), mp)
    kv_par = swap(kv)
    outs = attend(info, q, kv, kv_par, True)
    (o, probs), states = lax.optimization_barrier((outs, states))
    states, ckv = source_keys(info, states, second[1])
    ckv_par = swap(ckv)
    x2, c, cq = middle(info, after(o, ckv), second[0], x1, norm_gains, norm_biases)
    oc, cprobs = attend(info, cq, ckv, ckv_par, False)
    og = to_chips(after(out_grad.astype(bf16), oc), mp)
    w1, w2 = third
    oc_par, c_par = swap(oc), swap(after(c, oc))
    outs = feed(info, oc, second[1], x2, w1, w2, norm_gains, norm_biases, sub)
    (x3, f, g, slope, x4), og, oc_par, c_par = lax.optimization_barrier((outs, og, oc_par, c_par))
    f_par, g_par = swap(f), swap(g)
    a_par, o_par, states_par = [swap(after(v, x4)) for v in (a, o, states)]
    outs = feed_back(info, x4, og, slope, second[1], x3, w1, w2, norm_gains, norm_biases)
    outs, f_par, g_par, a_par, o_par, states_par = lax.optimization_barrier(
        (outs, f_par, g_par, a_par, o_par, states_par)
    )
    *hid, g4b, du, g3, g3b, doc, sums34 = outs
    g4b_par, g3b_par, du_par = swap(g4b), swap(g3b), swap(du)
    hidden_out = from_chips(tied(hid, g4b_par), mp)
    shape = (chips, mp, sub, rows, block)
    grads = weight_grad(info, g4b, g4b_par, g, g_par, shape, 0)
    part_one = scattered(grads, "chip")
    shape = (chips, mp, sub + 1, rows, block)
    grads = weight_grad(info, after(g3b, grads), g3b_par, oc, oc_par, shape, sub)
    grads = weight_grad(info, after(f, grads), f_par, du, du_par, shape, 0, grads)
    doc, hidden_out = lax.optimization_barrier((after(doc, grads), hidden_out))

    outs = attend_back(cq, ckv, ckv_par, cprobs, oc, doc)
    (dcq, dckv_own, dckv_par), part_one = lax.optimization_barrier((outs, part_one))
    part_two = scattered(after(grads, part_one), "chip")
    dckv_came, dcq_par = swap(dckv_par), swap(dcq)
    outs = middle_back(info, dcq, second[0], x2, g3, norm_gains)
    (g2, g2b, do, sums2), dckv_came, dcq_par, dckv_own = lax.optimization_barrier(
        (outs, dckv_came, dcq_par, dckv_own)
    )
    g2b_par = swap(g2b)
    outs = source_back(info, dckv_own, dckv_came, second[1])
    *enc_grad, dckv = outs
    dckv_after = swap(dckv)
    shape = (chips, mp, 4, rows, block)
    grads = weight_grad(info, c, c_par, after(dcq, dckv), dcq_par, shape, 0)
    grads = weight_grad(info, g2b, g2b_par, o, o_par, shape, 1, grads)
    grads = weight_grad(info, states, states_par, dckv, dckv_after, shape, 2, grads)
    do = after(do, grads)
    cross_grads = grads
    encoder_grad = from_chips(tied(enc_grad, grads), mp)

    outs = causal_back(info, q, kv, kv_par, probs, o, do)
    (dq, dkv_own, dkv_par), encoder_grad, part_two = lax.optimization_barrier(
        (outs, encoder_grad, part_two)
    )
    cross_part = scattered(after(cross_grads, part_two), "chip")
    dkv_came = swap(dkv_par)
    dq_par = swap(dq)
    outs = exit_back(info, dq, dkv_own, dkv_came, first, x1, x0, g2, norm_gains)
    (g0, dkv, sums01), dq_par = lax.optimization_barrier((outs, dq_par))
    sent = g0.reshape(n, feats, tokens)
    arrived = lax.all_to_all(sent, ALL, split_axis=0, concat_axis=0, tiled=True)
    sums = jnp.concatenate((sums01, sums2, sums34), axis=0)
    sums_par = swap(sums)
    shape = (chips, mp, 3, rows, block)
    dkv_after = swap(dkv)
    grads = weight_grad(info, a, a_par, dq, dq_par, shape, 0)
    grads, sums_par = lax.optimization_barrier((grads, sums_par))
    sums = total_over(sums + sums_par, "chip", chips)
    grads = weight_grad(info, a, a_par, dkv, dkv_after, shape, 1, grads)
    sums, grads, arrived, cross_part = lax.optimization_barrier((sums, grads, arrived, cross_part))
    sums_up = scattered(jnp.concatenate([part_one, part_two, cross_part], axis=1), "mp")
    self_terms = lax.all_to_all(grads, "chip", split_axis=0, concat_axis=0, tiled=True)
    sums = total_over(sums, "mp", mp)

    outs = scatter_tokens(arrived, flat_row, row, group, vocab, mp)
    (table_grad, places), self_terms, sums = lax.optimization_barrier((outs, self_terms, sums))
    hidden_out = placed_again(tied(hidden_out, places))
    encoder_grad = placed_again(tied(encoder_grad, places))
    self_part = jnp.sum(self_terms.astype(f32), axis=0).astype(bf16)
    self_grads = summed(sent_over(self_part, "mp", mp))
    sums_up = sums_up.astype(f32)
    feed_out_grads, feed_in_grads, cross_grads = (
        sums_up[:sub],
        sums_up[sub : 2 * sub + 1],
        sums_up[2 * sub + 1 :],
    )

    blocks = places.reshape(CORES, feats, 2, block).transpose(0, 2, 1, 3).reshape(4, feats, block)
    blocks = jnp.stack([blocks[0], blocks[2], blocks[3], blocks[1]])
    parts = []
    for k in range(mp):
        mine = lax.dynamic_index_in_dim(blocks, (m + k) % mp, axis=0, keepdims=False)
        parts.append(
            mine if k == 0 else lax.ppermute(mine, "mp", [(i, (i + k) % mp) for i in range(mp)])
        )
    pos_grad = []
    for source in range(mp):
        value = parts[0]
        for k in range(1, mp):
            value = jnp.where((m - source) % mp == k, parts[k], value)
        pos_grad.append(value)
    pos_grad = jnp.concatenate(pos_grad, axis=0)

    def join(parts):
        return parts.transpose(1, 0, 2)

    return (
        hidden_out,
        table_grad,
        pos_grad,
        join(self_grads),
        cross_grads[1],
        cross_grads[0],
        join(cross_grads[2:4]),
        feed_in_grads[sub],
        join(feed_in_grads[:sub]).reshape(rows, -1),
        join(feed_out_grads).reshape(rows, -1),
        sums[0::2],
        sums[1::2],
        encoder_grad,
    )


def solution(mesh):
    dp, mp = mesh.devices.shape
    chips = dp // CORES
    fine = Mesh(mesh.devices.reshape(chips, CORES, mp), ALL)
    both = ("chip", "core")
    placed = (
        P(both, "mp"),
        P(both),
        P(both, "mp", None),
        P(both),
        P(ALL, None),
        P(both, "mp"),
        P(both, None, "mp"),
        P(both, "mp"),
        P(both, "mp"),
        P(both, None, "mp"),
        P(both, "mp"),
        P(both, "mp"),
        P(both, "mp"),
        P(),
        P(),
        P(both, "mp", None),
    )
    return jax.shard_map(
        functools.partial(body, chips, mp),
        mesh=fine,
        in_specs=placed,
        out_specs=(
            P(both, "mp", None),
            P(ALL, None),
            P(both, "mp"),
            P(both, None, "mp"),
            P(both, "mp"),
            P(both, "mp"),
            P(both, None, "mp"),
            P(both, "mp"),
            P(both, "mp"),
            P(both, "mp"),
            P(),
            P(),
            P(both, "mp", None),
        ),
        check_vma=False,
    )
```

```python
import functools
import math

import jax
import jax.numpy as jnp
from jax import lax
from jax.experimental import pallas as pl
from jax.experimental.pallas import tpu as pltpu
from jax.sharding import Mesh
from jax.sharding import PartitionSpec as P

HEAD_DIM = 64
EPSILON = 1e-05
NEGATIVE = -1e30
LANES = 128
ALL = ("chip", "core", "mp")
LINE = ("core", "mp")
CORES = 2

f32 = jnp.float32
bf16 = jnp.bfloat16
i32 = jnp.int32

NT = (((1,), (1,)), ((), ()))
NN = (((1,), (0,)), ((), ()))
TN = (((0,), (0,)), ((), ()))


def dot(a, b, dims=NN):
    return lax.dot_general(a, b, dims, preferred_element_type=f32)


def params(mib=56):
    return pltpu.CompilerParams(vmem_limit_bytes=mib << 20)


def cost(microseconds):
    return pl.CostEstimate(flops=0, bytes_accessed=int(microseconds * 3.2e6), transcendentals=0)


def normed(values):
    centred = values - jnp.mean(values, axis=-1, keepdims=True)
    inverse = lax.rsqrt(jnp.mean(centred * centred, axis=-1, keepdims=True) + EPSILON)
    return centred * inverse, inverse


def norm_back(values, gain, grad):
    hat, inverse = normed(values)
    scaled = grad * gain
    first = jnp.mean(scaled, axis=-1, keepdims=True)
    second = jnp.mean(scaled * hat, axis=-1, keepdims=True)
    back = inverse * (scaled - first - hat * second)
    gain_grad = jnp.sum(grad * hat, axis=0, keepdims=True)
    bias_grad = jnp.sum(grad, axis=0, keepdims=True)
    return back, gain_grad, bias_grad


def in_order(pieces, info_ref):
    for bit, place in ((0, 0), (1, 7), (2, 8)):
        far = info_ref[place] == 1
        turned = []
        for i, piece in enumerate(pieces):
            turned.append(jnp.where(far, pieces[i ^ (1 << bit)], piece))
        pieces = turned
    return pieces


def joined(blocks, info_ref):
    flat = [b.reshape(-1, b.shape[-1]) for b in blocks]
    return flat[0] if len(flat) == 1 else jnp.concatenate(in_order(flat, info_ref), axis=0)


def columns(w_refs, m, info_ref):
    return joined([w[:, pl.ds(m, 1)] for w in w_refs], info_ref)


def whole_weight(w_refs, info_ref):
    parts = [columns(w_refs, m, info_ref) for m in range(w_refs[0].shape[1])]
    return jnp.concatenate(parts, axis=1)


def project(x, w_refs, info_ref, store):
    width = w_refs[0].shape[4]

    def step(m, carry):
        store(pl.multiple_of(m * width, width), dot(x, columns(w_refs, m, info_ref)))
        return carry

    lax.fori_loop(0, w_refs[0].shape[1], step, 0, unroll=True)


def weight_specs(weights, index):
    return [
        pl.BlockSpec(
            (w.shape[0], w.shape[1], 1, w.shape[3], w.shape[4]),
            lambda s, info, skip=skip: (0, 0, index(s) + skip, 0, 0),
        )
        for w, skip in weights
    ]


def call(kernel, info, grid, operands, outs, scratch=(), mib=56, **others):
    arrays, specs, sizes = [], [], []
    for value, spec in operands:
        group = isinstance(value, (list, tuple))
        sizes.append(len(value) if group else None)
        arrays.extend([w for w, _ in value] if group else [value])
        specs.extend(spec if group else [spec])

    def body(info_ref, *refs):
        given, rest, at = [], refs, 0
        for size in sizes:
            given.append(refs[at] if size is None else list(refs[at : at + size]))
            at += 1 if size is None else size
        kernel(info_ref, *given, *rest[at:])

    return pl.pallas_call(
        body,
        out_shape=[o for o, _ in outs],
        grid_spec=pltpu.PrefetchScalarGridSpec(
            num_scalar_prefetch=1,
            grid=grid,
            in_specs=specs,
            out_specs=[o for _, o in outs],
            scratch_shapes=list(scratch),
        ),
        compiler_params=params(mib),
        **others,
    )(info, *arrays)


def full(shape):
    return pl.BlockSpec(shape, lambda *a: (0,) * len(shape))


def gather_kernel(groups, fill, rows_ref, group_ref, *refs):
    tables, out_ref, turned, picked = refs[:groups], refs[groups], refs[-2], refs[-1]
    step = pl.program_id(0)
    feats, width = tables[0].shape
    tokens = picked.shape[0]

    @pl.when(step < fill)
    def _():
        stacked = jnp.concatenate([t[...].astype(f32) for t in tables], axis=0).astype(bf16)
        row = lax.broadcasted_iota(i32, (256, 256), 0)
        eye = jnp.where(row == lax.broadcasted_iota(i32, (256, 256), 1), 1.0, 0.0).astype(bf16)
        for k in range(width // 256):
            at = pl.multiple_of(step * width + k * 256, 256)
            turned[pl.ds(at, 256), :] = dot(eye, stacked[:, k * 256 : (k + 1) * 256], NT)

    @pl.when(step >= fill)
    def _():
        base = (step - fill) * tokens

        def some(k, carry):
            for u in range(16):
                t = k * 16 + u
                picked[pl.ds(t, 1), :] = turned[pl.ds(rows_ref[base + t], 1), :]
            return carry

        lax.fori_loop(0, tokens // 16, some, 0)
        row = lax.broadcasted_iota(i32, (LANES, LANES), 0)
        eye = jnp.where(row == lax.broadcasted_iota(i32, (LANES, LANES), 1), 1.0, 0.0)
        across = dot(eye.astype(bf16), picked[...].astype(bf16), NT)
        own = lax.broadcasted_iota(i32, (LANES, tokens), 0) // feats == group_ref[0]
        kept = jnp.where(own, across, 0.0)
        total = kept[:feats]
        for g in range(1, groups):
            total = total + kept[g * feats : (g + 1) * feats]
        out_ref[0] = total.astype(out_ref.dtype)


def gather_tokens(table, rows, group):
    feats, vocab = table.shape
    groups = LANES // feats
    height = vocab // groups
    n, _, tokens = group.shape
    width = min(2048, height)
    fill = height // width

    def table_spec(g):
        return pl.BlockSpec(
            (feats, width), lambda s, r, g=g: (0, g * fill + jnp.minimum(s, fill - 1))
        )

    return pl.pallas_call(
        functools.partial(gather_kernel, groups, fill),
        out_shape=jax.ShapeDtypeStruct((n, feats, tokens), bf16),
        grid_spec=pltpu.PrefetchScalarGridSpec(
            num_scalar_prefetch=1,
            grid=(fill + n,),
            in_specs=[pl.BlockSpec((1, 1, tokens), lambda s, r: (jnp.maximum(s - fill, 0), 0, 0))]
            + [table_spec(g) for g in range(groups)],
            out_specs=pl.BlockSpec(
                (1, feats, tokens), lambda s, r: (jnp.maximum(s - fill, 0), 0, 0)
            ),
            scratch_shapes=[pltpu.VMEM((height, LANES), f32), pltpu.VMEM((tokens, LANES), f32)],
        ),
        compiler_params=params(),
        cost_estimate=cost(45),
        name="gather_tokens",
    )(rows, group, *([table] * groups))


BATCH = 16
WIDTH = 4096
SENDERS = 8


def scatter_kernel(
    groups, per_core, rows_ref, row_ref, group_ref, grad_ref, out_ref, pos_ref, acc, update, turned, sem
):
    step = pl.program_id(0)
    senders, feats, tokens = grad_ref.shape
    height = acc.shape[0]
    width = turned.shape[2]

    @pl.when(step == 0)
    def _():
        def clear(k, carry):
            acc[pl.ds(pl.multiple_of(k * 256, 256), 256), :] = jnp.zeros((256, LANES), f32)
            return carry

        lax.fori_loop(0, height // 256, clear, 0)
        pos_ref[...] = jnp.zeros_like(pos_ref)

    row = lax.broadcasted_iota(i32, (LANES, LANES), 0)
    col = lax.broadcasted_iota(i32, (LANES, LANES), 1)
    near = row // BATCH == col // BATCH

    def sender(d, carry):
        place = step * senders + d
        grads = grad_ref[d].astype(f32)
        core = lax.rem(lax.div(place, per_core), CORES)
        pos_ref[core] += grads
        tall = jnp.concatenate([grads] * groups, axis=0)
        own = lax.broadcasted_iota(i32, (LANES, tokens), 0) // feats == group_ref[d]
        tall = jnp.where(own, tall, 0.0).astype(bf16)
        for b in range(tokens // LANES):
            at = slice(b * LANES, (b + 1) * LANES)
            along = jnp.broadcast_to(row_ref[d][:, at].astype(f32), (LANES, LANES))
            same = jnp.where((along == along.T) & near, 1.0, 0.0).astype(bf16)
            update[at, :] = dot(same, tall[:, at], NT)
        base = place * tokens

        def some(k, carry):
            where = [rows_ref[base + k * BATCH + u] for u in range(BATCH)]
            fresh = [
                acc[pl.ds(where[u], 1), :] + update[pl.ds(k * BATCH + u, 1), :]
                for u in range(BATCH)
            ]
            for u in range(BATCH):
                acc[pl.ds(where[u], 1), :] = fresh[u]
            return carry

        lax.fori_loop(0, tokens // BATCH, some, 0, unroll=True)
        return carry

    lax.fori_loop(0, senders, sender, 0)

    @pl.when(step == pl.num_programs(0) - 1)
    def _():
        def copy(i, slot, g):
            at = pl.multiple_of(g * height + i * width, width)
            return pltpu.make_async_copy(
                turned.at[slot, pl.ds(g * feats, feats)],
                out_ref.at[:, pl.ds(at, width)],
                sem.at[slot, g],
            )

        def turn(i, carry):
            slot = lax.rem(i, 2)

            @pl.when(i >= 2)
            def _():
                for g in range(groups):
                    copy(i - 2, slot, g).wait()

            at = pl.multiple_of(i * width, width)
            turned[slot] = (acc[pl.ds(at, width), :] * 32.0).T
            for g in range(groups):
                copy(i, slot, g).start()
            return carry

        count = height // width
        lax.fori_loop(0, count, turn, 0)
        for i in range(max(count - 2, 0), count):
            for g in range(groups):
                copy(i, i % 2, g).wait()


def scatter_tokens(grads, rows, row, group, vocab, per_core):
    n, feats, tokens = grads.shape
    groups = LANES // feats
    height = vocab // groups
    width = min(WIDTH, height)
    senders = math.gcd(n, SENDERS)
    token_spec = pl.BlockSpec((senders, 1, tokens), lambda s, r: (s, 0, 0))
    return pl.pallas_call(
        functools.partial(scatter_kernel, groups, per_core),
        out_shape=(
            jax.ShapeDtypeStruct((feats, vocab), f32),
            jax.ShapeDtypeStruct((CORES, feats, tokens), f32),
        ),
        grid_spec=pltpu.PrefetchScalarGridSpec(
            num_scalar_prefetch=1,
            grid=(n // senders,),
            in_specs=[
                token_spec,
                token_spec,
                pl.BlockSpec((senders, feats, tokens), lambda s, r: (s, 0, 0)),
            ],
            out_specs=(
                pl.BlockSpec(memory_space=pl.ANY),
                full((CORES, feats, tokens)),
            ),
            scratch_shapes=[
                pltpu.VMEM((height, LANES), f32),
                pltpu.VMEM((tokens, LANES), f32),
                pltpu.VMEM((2, LANES, width), f32),
                pltpu.SemaphoreType.DMA((2, groups)),
            ],
        ),
        compiler_params=params(),
        cost_estimate=cost(39),
        name="scatter_tokens",
    )(rows, row, group, grads)


def entry_kernel(
    info_ref, emb_ref, pos_a, pos_b, wq_ref, wkv_ref, gain_ref, bias_ref, x0_ref, x1_ref, a_ref, q_ref, kv_ref
):
    step = pl.program_id(0)
    half = x0_ref.shape[0] // 2

    @pl.when(step == 0)
    def _():
        for i, pos in enumerate((pos_a, pos_b)):
            at = slice(i * half, (i + 1) * half)
            places = joined([p[...] for p in pos], info_ref)
            x0 = (emb_ref[:, at].astype(f32) * 32.0 + places.astype(f32)).T
            x1 = normed(x0)[0] * gain_ref[0:1] + bias_ref[0:1]
            a = normed(x1)[0] * gain_ref[1:2] + bias_ref[1:2]
            x0_ref[at] = x0
            x1_ref[at] = x1
            a_ref[at] = a.astype(bf16)

    x = a_ref[...]
    span = wq_ref[0].shape[4]

    @pl.when(step == 0)
    def _():
        def store(at, y):
            q_ref[0, :, pl.ds(at, span)] = (y * HEAD_DIM**-0.5).astype(bf16)

        project(x, wq_ref, info_ref, store)

    @pl.when(step > 0)
    def _():
        def store(at, y):
            kv_ref[0, :, pl.ds(at, span)] = y.astype(bf16)

        project(x, wkv_ref, info_ref, store)


def entry(info, emb, first, gains, biases):
    width, tokens = emb.shape
    wq, wkv = first

    def pos_specs(i):
        return [
            pl.BlockSpec(
                (w.shape[0], 1, 1, w.shape[3], w.shape[4]),
                lambda s, info, skip=skip: (0, info[3 + i], skip, 0, 0),
            )
            for w, skip in wq
        ]

    row = full((tokens, width))
    rows = jax.ShapeDtypeStruct((tokens, width), f32)
    return call(
        entry_kernel,
        info,
        (3,),
        [
            (emb, full(emb.shape)),
            (wq, pos_specs(0)),
            (wq, pos_specs(1)),
            (wq, weight_specs(wq, lambda s: 1)),
            (wkv, weight_specs(wkv, lambda s: jnp.maximum(s - 1, 0))),
            (gains, full(gains.shape)),
            (biases, full(biases.shape)),
        ],
        [
            (rows, row),
            (rows, row),
            (jax.ShapeDtypeStruct((tokens, width), bf16), row),
            (jax.ShapeDtypeStruct((1, tokens, width), bf16), full((1, tokens, width))),
            (
                jax.ShapeDtypeStruct((2, tokens, width), bf16),
                pl.BlockSpec((1, tokens, width), lambda s, info: (jnp.maximum(s - 1, 0), 0, 0)),
            ),
        ],
        cost_estimate=cost(15),
        name="entry",
    )


def slots(pair, info_ref):
    odd = info_ref[9] == 1
    one, two = pair[0][...], pair[1][...]
    return jnp.where(odd, two, one), jnp.where(odd, one, two)


def put_slots(pair, info_ref, values):
    for odd in range(2):

        @pl.when(info_ref[9] == odd)
        def _():
            pair[odd][...] = values[0].astype(bf16)
            pair[1 - odd][...] = values[1].astype(bf16)


def source_kernel(info_ref, came_a, came_b, w_refs, x_ref, kv_ref):
    @pl.when(pl.program_id(0) == 0)
    def _():
        half = came_a.shape[0]
        x_ref[:half], x_ref[half:] = slots((came_a, came_b), info_ref)

    def store(at, y):
        kv_ref[0, :, pl.ds(at, w_refs[0].shape[4])] = y.astype(bf16)

    project(x_ref[...], w_refs, info_ref, store)


def source_keys(info, came, weights):
    half, width = came[0].shape
    tokens = 2 * half
    return call(
        source_kernel,
        info,
        (2,),
        [
            (came[0], full((half, width))),
            (came[1], full((half, width))),
            (weights, weight_specs(weights, lambda s: s)),
        ],
        [
            (jax.ShapeDtypeStruct((tokens, width), bf16), full((tokens, width))),
            (
                jax.ShapeDtypeStruct((2, tokens, width), bf16),
                pl.BlockSpec((1, tokens, width), lambda s, info: (s, 0, 0)),
            ),
        ],
        cost_estimate=cost(8),
        name="source_keys",
    )


def attend_kernel(causal, info_ref, q_ref, own_ref, par_ref, o_ref, p_ref, hide):
    tokens = q_ref.shape[1]
    half = tokens // 2
    core = info_ref[0]

    @pl.when(pl.program_id(0) == 0)
    def _():
        length = info_ref[1] if causal else info_ref[2]
        key = lax.broadcasted_iota(i32, (tokens, tokens), 0)
        query = lax.broadcasted_iota(i32, (tokens, tokens), 1)
        upper = key >= half
        own = key + jnp.where(upper, info_ref[4] - 1, info_ref[3]) * half
        par = key + jnp.where(upper, info_ref[6] - 1, info_ref[5]) * half
        at = query + jnp.where(query >= half, info_ref[4] - 1, info_ref[3]) * half
        for i, place in enumerate((own, par)):
            seen = place < length
            if causal:
                seen = seen & (place <= at)
            hide[i] = jnp.where(seen, 0.0, NEGATIVE)

    outs = []
    for h in range(LANES // HEAD_DIM):
        lanes = slice(h * HEAD_DIM, (h + 1) * HEAD_DIM)
        q = q_ref[0][:, lanes]
        s_own = dot(own_ref[0][:, lanes], q, NT) + hide[0]
        s_par = dot(par_ref[0][:, lanes], q, NT) + hide[1]
        top = jnp.maximum(
            jnp.max(s_own, axis=0, keepdims=True), jnp.max(s_par, axis=0, keepdims=True)
        )
        e_own = jnp.exp(s_own - top)
        e_par = jnp.exp(s_par - top)
        total = jnp.sum(e_own, axis=0, keepdims=True) + jnp.sum(e_par, axis=0, keepdims=True)
        scale = 1.0 / total
        p_own = (e_own * scale).astype(bf16)
        p_par = (e_par * scale).astype(bf16)
        p_ref[h, 0] = p_own
        p_ref[h, 1] = p_par
        outs.append(dot(own_ref[1][:, lanes], p_own, TN) + dot(par_ref[1][:, lanes], p_par, TN))
    o_ref[0] = jnp.concatenate(outs, axis=0).T.astype(bf16)


def attend(info, q, own, par, causal):
    _, tokens, width = q.shape
    heads = width // HEAD_DIM
    pair = LANES // HEAD_DIM
    one = pl.BlockSpec((1, tokens, LANES), lambda s, info: (0, 0, s))
    two = pl.BlockSpec((2, tokens, LANES), lambda s, info: (0, 0, s))
    return pl.pallas_call(
        functools.partial(attend_kernel, causal),
        out_shape=(
            jax.ShapeDtypeStruct((1, tokens, width), bf16),
            jax.ShapeDtypeStruct((heads, 2, tokens, tokens), bf16),
        ),
        grid_spec=pltpu.PrefetchScalarGridSpec(
            num_scalar_prefetch=1,
            grid=(heads // pair,),
            in_specs=[one, two, two],
            out_specs=(
                one,
                pl.BlockSpec((pair, 2, tokens, tokens), lambda s, info: (s, 0, 0, 0)),
            ),
            scratch_shapes=[pltpu.VMEM((2, tokens, tokens), f32)],
        ),
        compiler_params=params(),
        cost_estimate=cost(22),
        name="attend",
    )(info, q, own, par)


def middle_kernel(info_ref, o_ref, w_ref, x_ref, wq_ref, gain_ref, bias_ref, x2_ref, c_ref, q_ref):
    x2 = x_ref[...] + dot(o_ref[0], whole_weight(w_ref, info_ref), NT)
    x2_ref[...] = x2
    c = (normed(x2)[0] * gain_ref[2:3] + bias_ref[2:3]).astype(bf16)
    c_ref[...] = c

    def store(at, y):
        q_ref[0, :, pl.ds(at, wq_ref[0].shape[4])] = (y * HEAD_DIM**-0.5).astype(bf16)

    project(c, wq_ref, info_ref, store)


def middle(info, o, weights, x1, gains, biases):
    _, tokens, width = o.shape
    row = full((tokens, width))
    return call(
        middle_kernel,
        info,
        (1,),
        [
            (o, full(o.shape)),
            (weights, weight_specs(weights, lambda s: 0)),
            (x1, row),
            (weights, weight_specs(weights, lambda s: 1)),
            (gains, full(gains.shape)),
            (biases, full(biases.shape)),
        ],
        [
            (jax.ShapeDtypeStruct((tokens, width), f32), row),
            (jax.ShapeDtypeStruct((tokens, width), bf16), row),
            (jax.ShapeDtypeStruct((1, tokens, width), bf16), full((1, tokens, width))),
        ],
        cost_estimate=cost(9),
        name="middle",
    )


def feed_kernel(
    info_ref,
    o_ref,
    wo_ref,
    x_ref,
    w1_ref,
    w2_ref,
    gain_ref,
    bias_ref,
    x3_ref,
    f_ref,
    g_ref,
    slope_ref,
    x4_ref,
):
    step = pl.program_id(0)

    @pl.when(step == 0)
    def _():
        x3 = x_ref[...] + dot(o_ref[0], whole_weight(wo_ref, info_ref), NT)
        x3_ref[...] = x3
        f_ref[...] = (normed(x3)[0] * gain_ref[3:4] + bias_ref[3:4]).astype(bf16)
        x4_ref[...] = x3

    def store(at, u):
        bell = 0.5 + 0.5 * lax.erf(u * 0.7071067811865476)
        lanes = pl.ds(at, w1_ref[0].shape[4])
        g_ref[0, :, lanes] = (u * bell).astype(bf16)
        slope = bell + u * (0.3989422804014327 * jnp.exp(-0.5 * u * u))
        slope_ref[0, :, lanes] = slope.astype(bf16)

    project(f_ref[...], w1_ref, info_ref, store)
    x4_ref[...] += dot(g_ref[0], whole_weight(w2_ref, info_ref), NT)


def feed(info, o, wo, x2, w1, w2, gains, biases, slabs):
    _, tokens, width = o.shape
    blocks = slabs
    row = full((tokens, width))
    part = pl.BlockSpec((1, tokens, width), lambda s, info: (s, 0, 0))
    wide = jax.ShapeDtypeStruct((tokens, width), f32)
    slim = jax.ShapeDtypeStruct((tokens, width), bf16)
    many = jax.ShapeDtypeStruct((blocks, tokens, width), bf16)
    return call(
        feed_kernel,
        info,
        (blocks,),
        [
            (o, full(o.shape)),
            (wo, weight_specs(wo, lambda s: 2)),
            (x2, row),
            (w1, weight_specs(w1, lambda s: s)),
            (w2, weight_specs(w2, lambda s: s)),
            (gains, full(gains.shape)),
            (biases, full(biases.shape)),
        ],
        [(wide, row), (slim, row), (many, part), (many, part), (wide, row)],
        mib=60,
        cost_estimate=cost(28),
        name="feed",
    )


def feed_back_kernel(
    info_ref,
    x4_ref,
    og_a,
    og_b,
    slope_ref,
    w1_ref,
    w2_ref,
    x3_ref,
    wo_ref,
    gain_ref,
    bias_ref,
    hid_a,
    hid_b,
    g4b_ref,
    du_ref,
    g3_ref,
    g3b_ref,
    do_ref,
    sums_ref,
    total,
):
    step = pl.program_id(0)

    @pl.when(step == 0)
    def _():
        x4 = x4_ref[...]
        half = og_a.shape[0]
        hidden = normed(x4)[0] * gain_ref[4:5] + bias_ref[4:5]
        put_slots((hid_a, hid_b), info_ref, (hidden[:half], hidden[half:]))
        out_grad = jnp.concatenate(slots((og_a, og_b), info_ref), axis=0).astype(f32)
        g4, gain_grad, bias_grad = norm_back(x4, gain_ref[4:5], out_grad)
        g3_ref[...] = g4
        g4b_ref[...] = g4.astype(bf16)
        sums_ref[2:3] = gain_grad
        sums_ref[3:4] = bias_grad

    def store(at, y):
        lanes = pl.ds(at, w2_ref[0].shape[4])
        du_ref[0, :, lanes] = (y * slope_ref[0, :, lanes].astype(f32)).astype(bf16)

    project(g4b_ref[...], w2_ref, info_ref, store)
    part = dot(du_ref[0], whole_weight(w1_ref, info_ref), NT)

    @pl.when(step == 0)
    def _():
        total[...] = part

    @pl.when(step > 0)
    def _():
        total[...] += part

    @pl.when(step == pl.num_programs(0) - 1)
    def _():
        back, gain_grad, bias_grad = norm_back(x3_ref[...], gain_ref[3:4], total[...])
        g3 = g3_ref[...] + back
        g3_ref[...] = g3
        g3b = g3.astype(bf16)
        g3b_ref[...] = g3b
        sums_ref[0:1] = gain_grad
        sums_ref[1:2] = bias_grad

        def keep(at, y):
            do_ref[0, :, pl.ds(at, wo_ref[0].shape[4])] = y.astype(bf16)

        project(g3b, wo_ref, info_ref, keep)


def feed_back(info, x4, og, slope, wo, x3, w1, w2, gains, biases):
    blocks, tokens, width = slope.shape
    row = full((tokens, width))
    part_row = full((tokens // 2, width))
    part_shape = jax.ShapeDtypeStruct((tokens // 2, width), bf16)
    part = pl.BlockSpec((1, tokens, width), lambda s, info: (s, 0, 0))
    wide = jax.ShapeDtypeStruct((tokens, width), f32)
    slim = jax.ShapeDtypeStruct((tokens, width), bf16)
    return call(
        feed_back_kernel,
        info,
        (blocks,),
        [
            (x4, row),
            (og[0], part_row),
            (og[1], part_row),
            (slope, part),
            (w1, weight_specs(w1, lambda s: s)),
            (w2, weight_specs(w2, lambda s: s)),
            (x3, row),
            (wo, weight_specs(wo, lambda s: 2)),
            (gains, full(gains.shape)),
            (biases, full(biases.shape)),
        ],
        [
            (part_shape, part_row),
            (part_shape, part_row),
            (slim, row),
            (jax.ShapeDtypeStruct((blocks, tokens, width), bf16), part),
            (wide, row),
            (slim, row),
            (jax.ShapeDtypeStruct((1, tokens, width), bf16), full((1, tokens, width))),
            (jax.ShapeDtypeStruct((4, width), f32), full((4, width))),
        ],
        [pltpu.VMEM((tokens, width), f32)],
        60,
        cost_estimate=cost(28),
        name="feed_back",
    )


def attend_back_kernel(
    q_ref, own_ref, par_ref, p_ref, o_ref, do_ref, dq_ref, down_ref, dpar_ref
):
    flat = do_ref[0].astype(f32).T * o_ref[0].astype(f32).T
    outs = []
    for h in range(LANES // HEAD_DIM):
        lanes = slice(h * HEAD_DIM, (h + 1) * HEAD_DIM)
        q = q_ref[0][:, lanes]
        grad = do_ref[0][:, lanes]
        inner = jnp.sum(flat[lanes], axis=0, keepdims=True)
        back = None
        for i, (kv_ref, d_ref) in enumerate(((own_ref, down_ref), (par_ref, dpar_ref))):
            keys = kv_ref[0][:, lanes]
            probs = p_ref[h, i]
            d_probs = dot(kv_ref[1][:, lanes], grad, NT)
            d_scores = (probs.astype(f32) * (d_probs - inner)).astype(bf16)
            d_ref[1, :, lanes] = dot(probs, grad).astype(bf16)
            d_ref[0, :, lanes] = dot(d_scores, q).astype(bf16)
            some = dot(keys, d_scores, TN)
            back = some if back is None else back + some
        outs.append(back)
    dq_ref[0] = (jnp.concatenate(outs, axis=0).T * HEAD_DIM**-0.5).astype(bf16)


def attend_back(q, own, par, probs, o, do):
    _, tokens, width = q.shape
    heads = width // HEAD_DIM
    pair = LANES // HEAD_DIM
    one = pl.BlockSpec((1, tokens, LANES), lambda s: (0, 0, s))
    two = pl.BlockSpec((2, tokens, LANES), lambda s: (0, 0, s))
    kv = jax.ShapeDtypeStruct((2, tokens, width), bf16)
    return pl.pallas_call(
        attend_back_kernel,
        out_shape=(jax.ShapeDtypeStruct((1, tokens, width), bf16), kv, kv),
        grid=(heads // pair,),
        in_specs=[
            one,
            two,
            two,
            pl.BlockSpec((pair, 2, tokens, tokens), lambda s: (s, 0, 0, 0)),
            one,
            one,
        ],
        out_specs=(one, two, two),
        compiler_params=params(),
        cost_estimate=cost(21),
        name="attend_back",
    )(q, own, par, probs, o, do)


def causal_back_kernel(
    info_ref, q_ref, own_ref, par_ref, p_ref, o_ref, do_ref, dq_ref, down_ref, dpar_ref, back
):
    tokens = q_ref.shape[1]
    half = tokens // 2
    low, high, every = slice(0, half), slice(half, tokens), slice(0, tokens)
    flat = do_ref[0].astype(f32).T * o_ref[0].astype(f32).T
    inner = [
        jnp.sum(flat[h * HEAD_DIM : (h + 1) * HEAD_DIM], axis=0, keepdims=True)
        for h in range(LANES // HEAD_DIM)
    ]
    back[...] = jnp.zeros_like(back)

    def segments(i, kv_ref, d_ref, spans):
        for h in range(LANES // HEAD_DIM):
            lanes = slice(h * HEAD_DIM, (h + 1) * HEAD_DIM)
            for keys, queries in spans:
                grad = do_ref[0, queries, lanes]
                probs = p_ref[h, i, keys, queries]
                d_probs = dot(kv_ref[1, keys, lanes], grad, NT)
                d_scores = (probs.astype(f32) * (d_probs - inner[h][:, queries])).astype(bf16)
                d_ref[1, keys, lanes] = dot(probs, grad).astype(bf16)
                d_ref[0, keys, lanes] = dot(d_scores, q_ref[0, queries, lanes]).astype(bf16)
                back[lanes, queries] += dot(kv_ref[0, keys, lanes], d_scores, TN)

    segments(0, own_ref, down_ref, [(low, every), (high, high)])

    @pl.when(info_ref[0] == 0)
    def _():
        segments(1, par_ref, dpar_ref, [(every, high)])

    @pl.when(info_ref[0] == 1)
    def _():
        segments(1, par_ref, dpar_ref, [(low, every)])
        dpar_ref[:, high, :] = jnp.zeros((2, half, LANES), bf16)

    dq_ref[0] = (back[...].T * HEAD_DIM**-0.5).astype(bf16)


def causal_back(info, q, own, par, probs, o, do):
    _, tokens, width = q.shape
    heads = width // HEAD_DIM
    pair = LANES // HEAD_DIM
    one = pl.BlockSpec((1, tokens, LANES), lambda s, info: (0, 0, s))
    two = pl.BlockSpec((2, tokens, LANES), lambda s, info: (0, 0, s))
    kv = jax.ShapeDtypeStruct((2, tokens, width), bf16)
    return call(
        causal_back_kernel,
        info,
        (heads // pair,),
        [
            (q, one),
            (own, two),
            (par, two),
            (probs, pl.BlockSpec((pair, 2, tokens, tokens), lambda s, info: (s, 0, 0, 0))),
            (o, one),
            (do, one),
        ],
        [(jax.ShapeDtypeStruct((1, tokens, width), bf16), one), (kv, two), (kv, two)],
        [pltpu.VMEM((LANES, tokens), f32)],
        cost_estimate=cost(19),
        name="causal_back",
    )


def middle_back_kernel(
    info_ref, dq_ref, wq_ref, x2_ref, g3_ref, wo_ref, gain_ref, g2_ref, g2b_ref, do_ref, sums_ref
):
    d_normed = dot(dq_ref[0], whole_weight(wq_ref, info_ref), NT)
    back, gain_grad, bias_grad = norm_back(x2_ref[...], gain_ref[2:3], d_normed)
    g2 = g3_ref[...] + back
    g2_ref[...] = g2
    g2b = g2.astype(bf16)
    g2b_ref[...] = g2b
    sums_ref[0:1] = gain_grad
    sums_ref[1:2] = bias_grad

    def keep(at, y):
        do_ref[0, :, pl.ds(at, wo_ref[0].shape[4])] = y.astype(bf16)

    project(g2b, wo_ref, info_ref, keep)


def middle_back(info, dq, weights, x2, g3, gains):
    _, tokens, width = dq.shape
    row = full((tokens, width))
    return call(
        middle_back_kernel,
        info,
        (1,),
        [
            (dq, full(dq.shape)),
            (weights, weight_specs(weights, lambda s: 1)),
            (x2, row),
            (g3, row),
            (weights, weight_specs(weights, lambda s: 0)),
            (gains, full(gains.shape)),
        ],
        [
            (jax.ShapeDtypeStruct((tokens, width), f32), row),
            (jax.ShapeDtypeStruct((tokens, width), bf16), row),
            (jax.ShapeDtypeStruct((1, tokens, width), bf16), full((1, tokens, width))),
            (jax.ShapeDtypeStruct((2, width), f32), full((2, width))),
        ],
        cost_estimate=cost(10),
        name="middle_back",
    )


def source_back_kernel(info_ref, mine_ref, came_ref, w_ref, out_a, out_b, sum_ref, total):
    step = pl.program_id(0)
    grads = (mine_ref[0].astype(f32) + came_ref[0].astype(f32)).astype(bf16)
    sum_ref[0] = grads
    part = dot(grads, whole_weight(w_ref, info_ref), NT)

    @pl.when(step == 0)
    def _():
        total[...] = part

    @pl.when(step == pl.num_programs(0) - 1)
    def _():
        half = out_a.shape[0]
        both = total[...] + part
        put_slots((out_a, out_b), info_ref, (both[:half], both[half:]))


def source_back(info, mine, came, weights):
    parts, tokens, width = mine.shape
    part = pl.BlockSpec((1, tokens, width), lambda s, info: (s, 0, 0))
    return call(
        source_back_kernel,
        info,
        (parts,),
        [(mine, part), (came, part), (weights, weight_specs(weights, lambda s: s))],
        [
            (jax.ShapeDtypeStruct((tokens // 2, width), bf16), full((tokens // 2, width))),
            (jax.ShapeDtypeStruct((tokens // 2, width), bf16), full((tokens // 2, width))),
            (jax.ShapeDtypeStruct((parts, tokens, width), bf16), part),
        ],
        [pltpu.VMEM((tokens, width), f32)],
        cost_estimate=cost(7),
        name="source_back",
    )


def exit_kernel(
    info_ref,
    dq_ref,
    mine_ref,
    came_ref,
    wq_ref,
    wkv_ref,
    x1_ref,
    x0_ref,
    g2_ref,
    gain_ref,
    g0_ref,
    sum_ref,
    sums_ref,
    total,
):
    step = pl.program_id(0)

    @pl.when(step == 0)
    def _():
        total[...] = dot(dq_ref[0], whole_weight(wq_ref, info_ref), NT)

    @pl.when(step > 0)
    def _():
        grads = (mine_ref[0].astype(f32) + came_ref[0].astype(f32)).astype(bf16)
        sum_ref[0] = grads
        total[...] += dot(grads, whole_weight(wkv_ref, info_ref), NT)

    @pl.when(step == pl.num_programs(0) - 1)
    def _():
        back, gain_one, bias_one = norm_back(x1_ref[...], gain_ref[1:2], total[...])
        g1 = g2_ref[...] + back
        g0, gain_zero, bias_zero = norm_back(x0_ref[...], gain_ref[0:1], g1)
        g0_ref[...] = g0.T.astype(bf16)
        sums_ref[0:1] = gain_zero
        sums_ref[1:2] = bias_zero
        sums_ref[2:3] = gain_one
        sums_ref[3:4] = bias_one


def exit_back(info, dq, mine, came, first, x1, x0, g2, gains):
    _, tokens, width = dq.shape
    wq, wkv = first
    row = full((tokens, width))
    part = pl.BlockSpec((1, tokens, width), lambda s, info: (jnp.maximum(s - 1, 0), 0, 0))
    return call(
        exit_kernel,
        info,
        (3,),
        [
            (dq, full(dq.shape)),
            (mine, part),
            (came, part),
            (wq, weight_specs(wq, lambda s: 1)),
            (wkv, weight_specs(wkv, lambda s: jnp.maximum(s - 1, 0))),
            (x1, row),
            (x0, row),
            (g2, row),
            (gains, full(gains.shape)),
        ],
        [
            (jax.ShapeDtypeStruct((width, tokens), bf16), full((width, tokens))),
            (jax.ShapeDtypeStruct((2, tokens, width), bf16), part),
            (jax.ShapeDtypeStruct((4, width), f32), full((4, width))),
        ],
        [pltpu.VMEM((tokens, width), f32)],
        cost_estimate=cost(15),
        name="exit_back",
    )


def weight_grad_kernel(chips, aliased, info_ref, xo_ref, xp_ref, yo_ref, yp_ref, *refs):
    out_ref, turned = refs[-2], refs[-1]
    tokens, width = xo_ref.shape
    rows = width // (chips * CORES)
    core = info_ref[0]

    @pl.when(pl.program_id(0) == 0)
    def _():
        for i, x_ref in enumerate((xo_ref, xp_ref)):
            at = slice(i * tokens, (i + 1) * tokens)
            if rows % LANES == 0:
                for j in range(chips):
                    lanes = pl.ds(pl.multiple_of((2 * j + core) * rows, rows), rows)
                    turned[j * rows : (j + 1) * rows, at] = x_ref[:, lanes].astype(f32).T.astype(bf16)
            else:
                tall = x_ref[...].astype(f32).T.reshape(chips, CORES, rows, tokens)
                mine = jnp.where(core == 0, tall[:, 0], tall[:, 1])
                turned[:, at] = mine.reshape(chips * rows, tokens).astype(bf16)

    y_own, y_par = yo_ref[0], yp_ref[0]
    blocks, span = out_ref.shape[1], out_ref.shape[4]
    result = dot(turned[:, :tokens], y_own) + dot(turned[:, tokens:], y_par)
    for m in range(blocks):
        part = result[:, m * span : (m + 1) * span].astype(bf16)
        out_ref[:, m, 0] = part.reshape(chips, rows, span)


def weight_grad(info, x_own, x_par, y_own, y_par, shape, at, before=None):
    parts, tokens, width = y_own.shape
    chips = shape[0]
    row = full(x_own.shape)
    part = pl.BlockSpec((1, tokens, width), lambda s, info: (s, 0, 0))
    extra = [] if before is None else [before]
    return pl.pallas_call(
        functools.partial(weight_grad_kernel, chips, before is not None),
        out_shape=jax.ShapeDtypeStruct(shape, bf16),
        grid_spec=pltpu.PrefetchScalarGridSpec(
            num_scalar_prefetch=1,
            grid=(parts,),
            in_specs=[row, row, part, part] + [pl.BlockSpec(memory_space=pl.ANY) for _ in extra],
            out_specs=pl.BlockSpec(
                (chips, shape[1], 1, shape[3], shape[4]), lambda s, info: (0, 0, s + at, 0, 0)
            ),
            scratch_shapes=[pltpu.VMEM((x_own.shape[1] // 2, 2 * tokens), bf16)],
        ),
        input_output_aliases={} if before is None else {5: 0},
        compiler_params=params(30),
        cost_estimate=cost(3 + 2 * parts),
        name="weight_grad",
    )(info, x_own, x_par, y_own, y_par, *extra)


def swap(value):
    return lax.ppermute(value, "core", [(0, 1), (1, 0)])


def line_moves(mp):
    rounds = []
    for turn in range(2):
        moves = []
        for c in range(CORES):
            for m in range(mp):
                target, slot = (1 if m in (1, 2) else 0), m // 2
                moves.append((c * mp + m, target * mp + 2 * c + (slot ^ turn)))
        rounds.append(moves)
    return rounds


def to_chips(value, mp):
    slot = lax.axis_index("mp") // 2
    return [
        lax.ppermute(jnp.where((slot ^ turn) == 0, value[0], value[1]), LINE, moves)
        for turn, moves in enumerate(line_moves(mp))
    ]


def from_chips(pair, mp):
    return [
        lax.ppermute(sent, LINE, [(b, a) for a, b in moves])
        for sent, moves in zip(pair, line_moves(mp))
    ]


def placed_again(came):
    slot = lax.axis_index("mp") // 2
    one, two = [c.astype(f32) for c in came]
    return jnp.stack([jnp.where(slot == 0, one, two), jnp.where(slot == 0, two, one)])


def packed(*weights):
    return jnp.concatenate([w.reshape(-1, w.shape[-1]) for w in weights], axis=0)


X_SWAP = [(0, 1), (1, 0), (2, 3), (3, 2)]
Y_SWAP = [(0, 2), (2, 0), (1, 3), (3, 1)]
def gathered(rows, unit, chips, mp):
    value = lax.all_gather(rows, ALL, axis=0, tiled=False)
    return value.reshape(chips * CORES, mp, -1, unit, rows.shape[-1])


def gathered_line(rows, unit, mp):
    value = lax.all_gather(rows, "mp", axis=0, tiled=False)
    return value.reshape(mp, -1, unit, rows.shape[-1])


class Spread:
    def __init__(self, value, cut):
        self.own, self.cut = [value], cut
        self.near, self.far, self.both = [], [], []
        self.swapped = {}

    def begin(self, *others):
        self.own = tied(self.own, *others)
        sets = [self.own[0][:, : self.cut], self.own[0][:, self.cut :]]
        self.near = [lax.ppermute(w, "chip", p) for w, p in zip(sets, (X_SWAP, Y_SWAP))]
        self.far = [lax.ppermute(w, "chip", p) for w, p in zip(sets, (Y_SWAP, X_SWAP))]

    def finish(self, *others):
        self.near = tied(self.near, *others)
        self.both = [lax.ppermute(w, "chip", p) for w, p in zip(self.near, (Y_SWAP, X_SWAP))]

    def swap(self, *names):
        for name in names:
            self.swapped[name] = [swap(w) for w in getattr(self, name)]

    def hold(self, *others):
        state = [self.own, self.near, self.far, self.both, self.swapped]
        state, others = lax.optimization_barrier((state, others))
        self.own, self.near, self.far, self.both, self.swapped = state
        return others if len(others) > 1 else others[0]

    def pieces(self):
        found = []
        for i in range(2):
            pieces = []
            for name in ("own", "near", "far", "both") if i == 0 else ("own", "far", "near", "both"):
                at, skip = (0, i * self.cut) if name == "own" else (i, 0)
                for group in (getattr(self, name), self.swapped[name]):
                    pieces.append((group[at][None], skip))
            found.append(pieces)
        return found


def tied(value, *others):
    return after(value, *others) if others else value


def scattered(grads, axis):
    return lax.psum_scatter(grads, axis, scatter_dimension=0, tiled=False)


def sent_over(grads, axis, size):
    me = lax.axis_index(axis)
    terms = []
    for k in range(size):
        if axis == "chip" and size == 4:
            to, perm = me ^ k, [(i, i ^ k) for i in range(size)]
        else:
            to, perm = (me + k) % size, [(i, (i + k) % size) for i in range(size)]
        part = lax.dynamic_index_in_dim(grads, to, axis=0, keepdims=False)
        terms.append(part if k == 0 else lax.ppermute(part, axis, perm))
    return terms


def summed(terms):
    return sum([t.astype(f32) for t in terms[1:]], start=terms[0].astype(f32))


def total_over(value, axis, size):
    terms = [
        lax.ppermute(value, axis, [(i, (i + k) % size) for i in range(size)])
        for k in range(1, size)
    ]
    return sum(terms, start=value)


def after(value, *others):
    return lax.optimization_barrier((value, others))[0]


def body(
    chips,
    mp,
    target_ids,
    tgt_lengths,
    encoder_states,
    src_lengths,
    table,
    pos_table,
    self_query_key_value_weight,
    self_output_weight,
    cross_query_weight,
    cross_key_value_weight,
    cross_output_weight,
    feedforward_input_weight,
    feedforward_output_weight,
    norm_gains,
    norm_biases,
    out_grad,
):
    dp = chips * CORES
    n = dp * mp
    seqs, block = target_ids.shape
    assert seqs * CORES == mp == 4
    tokens = seqs * block
    width = norm_gains.shape[1]
    vocab = table.shape[1]
    feats = table.shape[0]
    rows = pos_table.shape[0]
    core, m, chip = lax.axis_index("core"), lax.axis_index("mp"), lax.axis_index("chip")

    def split(weight):
        return weight.reshape(rows, -1, block).transpose(1, 0, 2)

    own_ids = jnp.broadcast_to(target_ids.reshape(1, tokens), (n, tokens))
    all_ids = lax.all_to_all(own_ids, ALL, split_axis=0, concat_axis=0, tiled=True)
    sub = feedforward_input_weight.shape[1] // block
    first = packed(pos_table, split(self_query_key_value_weight))
    second = packed(
        self_output_weight, cross_query_weight, split(cross_key_value_weight), cross_output_weight
    )
    third = packed(split(feedforward_input_weight), split(feedforward_output_weight))
    sub = feedforward_input_weight.shape[1] // block
    second = gathered(second, rows, chips, mp)
    third = gathered(third, rows, chips, mp)
    second = [(second, 0)], [(second, 2)]
    third = [(third, 0)], [(third, sub)]
    stepped = chips == 4
    if stepped:
        copies = jnp.broadcast_to(first[None], (mp,) + first.shape)
        copies = lax.all_to_all(after(copies, all_ids), "mp", split_axis=0, concat_axis=0, tiled=True)
        first = Spread(copies.reshape(mp, -1, rows, block), 2)
    else:
        first = gathered(first, rows, chips, mp)
        first = [(first, 0)], [(first, 2)]

    lengths = jnp.stack([tgt_lengths, src_lengths])
    other = swap(lengths)
    lengths = jnp.where(
        core == 0,
        jnp.concatenate([lengths, other], axis=1),
        jnp.concatenate([other, lengths], axis=1),
    )
    lengths = lax.dynamic_index_in_dim(lengths, m, axis=1, keepdims=False)
    info = jnp.stack(
        [
            core,
            lengths[0],
            lengths[1],
            core,
            3 - core,
            1 - core,
            2 + core,
            chip % 2,
            chip // 2,
            m % 2,
        ]
    ).astype(i32)

    ids = all_ids.reshape(chips, CORES, mp, seqs, block)
    ids = jnp.stack([ids[:, :, 0], ids[:, :, 3], ids[:, :, 1], ids[:, :, 2]], axis=2)
    ids = ids.reshape(chips, CORES, CORES, 2, seqs, block).transpose(0, 2, 1, 4, 3, 5)
    ids = ids.reshape(n, 1, tokens)
    height = vocab // (LANES // feats)
    row, group = ids % height, ids // height
    flat_row = row.reshape(-1)

    picked = gather_tokens(table, flat_row, group)
    if stepped:
        picked = first.hold(picked)
        first.begin(picked)
        first.finish()
        first.swap("own", "near", "far", "both")
        first = first.pieces()
    emb = lax.all_to_all(picked, ALL, split_axis=0, concat_axis=0, tiled=True)
    emb = emb.reshape(width, tokens)

    x0, x1, a, q, kv = entry(info, emb, first, norm_gains, norm_biases)
    states = to_chips(after(encoder_states, a), mp)
    kv_par = swap(kv)
    outs = attend(info, q, kv, kv_par, True)
    (o, probs), states = lax.optimization_barrier((outs, states))
    states, ckv = source_keys(info, states, second[1])
    ckv_par = swap(ckv)
    x2, c, cq = middle(info, after(o, ckv), second[0], x1, norm_gains, norm_biases)
    oc, cprobs = attend(info, cq, ckv, ckv_par, False)
    og = to_chips(after(out_grad.astype(bf16), oc), mp)
    w1, w2 = third
    oc_par, c_par = swap(oc), swap(after(c, oc))
    outs = feed(info, oc, second[1], x2, w1, w2, norm_gains, norm_biases, sub)
    (x3, f, g, slope, x4), og, oc_par, c_par = lax.optimization_barrier((outs, og, oc_par, c_par))
    f_par, g_par = swap(f), swap(g)
    a_par, o_par, states_par = [swap(after(v, x4)) for v in (a, o, states)]
    outs = feed_back(info, x4, og, slope, second[1], x3, w1, w2, norm_gains, norm_biases)
    outs, f_par, g_par, a_par, o_par, states_par = lax.optimization_barrier(
        (outs, f_par, g_par, a_par, o_par, states_par)
    )
    *hid, g4b, du, g3, g3b, doc, sums34 = outs
    g4b_par, g3b_par, du_par = swap(g4b), swap(g3b), swap(du)
    hidden_out = from_chips(tied(hid, g4b_par), mp)
    shape = (chips, mp, sub, rows, block)
    grads = weight_grad(info, g4b, g4b_par, g, g_par, shape, 0)
    part_one = scattered(grads, "chip")
    shape = (chips, mp, sub + 1, rows, block)
    grads = weight_grad(info, after(g3b, grads), g3b_par, oc, oc_par, shape, sub)
    grads = weight_grad(info, after(f, grads), f_par, du, du_par, shape, 0, grads)
    doc, hidden_out = lax.optimization_barrier((after(doc, grads), hidden_out))

    outs = attend_back(cq, ckv, ckv_par, cprobs, oc, doc)
    (dcq, dckv_own, dckv_par), part_one = lax.optimization_barrier((outs, part_one))
    part_two = scattered(after(grads, part_one), "chip")
    dckv_came, dcq_par = swap(dckv_par), swap(dcq)
    outs = middle_back(info, dcq, second[0], x2, g3, norm_gains)
    (g2, g2b, do, sums2), dckv_came, dcq_par, dckv_own = lax.optimization_barrier(
        (outs, dckv_came, dcq_par, dckv_own)
    )
    g2b_par = swap(g2b)
    outs = source_back(info, dckv_own, dckv_came, second[1])
    *enc_grad, dckv = outs
    dckv_after = swap(dckv)
    shape = (chips, mp, 3, rows, block)
    grads = weight_grad(info, c, c_par, after(dcq, dckv), dcq_par, shape, 0)
    self_shape = (chips, mp, 4, rows, block)
    held = weight_grad(info, after(g2b, grads), g2b_par, o, o_par, self_shape, 3)
    grads = weight_grad(info, after(states, held), states_par, dckv, dckv_after, shape, 1, grads)
    do = after(do, grads)
    cross_grads = grads
    encoder_grad = from_chips(tied(enc_grad, grads), mp)

    outs = causal_back(info, q, kv, kv_par, probs, o, do)
    (dq, dkv_own, dkv_par), encoder_grad, part_two = lax.optimization_barrier(
        (outs, encoder_grad, part_two)
    )
    cross_part = scattered(after(cross_grads, part_two), "chip")
    dkv_came = swap(dkv_par)
    dq_par = swap(dq)
    outs = exit_back(info, dq, dkv_own, dkv_came, first, x1, x0, g2, norm_gains)
    (g0, dkv, sums01), dq_par = lax.optimization_barrier((outs, dq_par))
    sent = g0.reshape(n, feats, tokens)
    arrived = lax.all_to_all(sent, ALL, split_axis=0, concat_axis=0, tiled=True)
    sums = jnp.concatenate((sums01, sums2, sums34), axis=0)
    sums_par = swap(sums)
    dkv_after = swap(dkv)
    grads = weight_grad(info, a, a_par, dq, dq_par, self_shape, 0, held)
    grads, sums_par = lax.optimization_barrier((grads, sums_par))
    sums = total_over(sums + sums_par, "chip", chips)
    grads = weight_grad(info, a, a_par, dkv, dkv_after, self_shape, 1, grads)
    sums, grads, arrived, cross_part = lax.optimization_barrier((sums, grads, arrived, cross_part))
    sums_up = scattered(jnp.concatenate([part_one, part_two, cross_part], axis=1), "mp")
    self_terms = lax.all_to_all(grads, "chip", split_axis=0, concat_axis=0, tiled=True)
    sums = total_over(sums, "mp", mp)

    outs = scatter_tokens(arrived, flat_row, row, group, vocab, mp)
    (table_grad, places), self_terms, sums = lax.optimization_barrier((outs, self_terms, sums))
    hidden_out = placed_again(tied(hidden_out, places))
    encoder_grad = placed_again(tied(encoder_grad, places))
    self_part = jnp.sum(self_terms.astype(f32), axis=0).astype(bf16)
    self_grads = summed(sent_over(self_part, "mp", mp))
    sums_up = sums_up.astype(f32)
    feed_out_grads, feed_in_grads, cross_grads = (
        sums_up[:sub],
        sums_up[sub : 2 * sub + 1],
        sums_up[2 * sub + 1 :],
    )

    blocks = places.reshape(CORES, feats, 2, block).transpose(0, 2, 1, 3).reshape(4, feats, block)
    blocks = jnp.stack([blocks[0], blocks[2], blocks[3], blocks[1]])
    parts = []
    for k in range(mp):
        mine = lax.dynamic_index_in_dim(blocks, (m + k) % mp, axis=0, keepdims=False)
        parts.append(
            mine if k == 0 else lax.ppermute(mine, "mp", [(i, (i + k) % mp) for i in range(mp)])
        )
    pos_grad = []
    for source in range(mp):
        value = parts[0]
        for k in range(1, mp):
            value = jnp.where((m - source) % mp == k, parts[k], value)
        pos_grad.append(value)
    pos_grad = jnp.concatenate(pos_grad, axis=0)

    def join(parts):
        return parts.transpose(1, 0, 2)

    return (
        hidden_out,
        table_grad,
        pos_grad,
        join(self_grads[:3]),
        self_grads[3],
        cross_grads[0],
        join(cross_grads[1:3]),
        feed_in_grads[sub],
        join(feed_in_grads[:sub]).reshape(rows, -1),
        join(feed_out_grads).reshape(rows, -1),
        sums[0::2],
        sums[1::2],
        encoder_grad,
    )


def solution(mesh):
    dp, mp = mesh.devices.shape
    chips = dp // CORES
    fine = Mesh(mesh.devices.reshape(chips, CORES, mp), ALL)
    both = ("chip", "core")
    placed = (
        P(both, "mp"),
        P(both),
        P(both, "mp", None),
        P(both),
        P(ALL, None),
        P(both, "mp"),
        P(both, None, "mp"),
        P(both, "mp"),
        P(both, "mp"),
        P(both, None, "mp"),
        P(both, "mp"),
        P(both, "mp"),
        P(both, "mp"),
        P(),
        P(),
        P(both, "mp", None),
    )
    return jax.shard_map(
        functools.partial(body, chips, mp),
        mesh=fine,
        in_specs=placed,
        out_specs=(
            P(both, "mp", None),
            P(ALL, None),
            P(both, "mp"),
            P(both, None, "mp"),
            P(both, "mp"),
            P(both, "mp"),
            P(both, None, "mp"),
            P(both, "mp"),
            P(both, "mp"),
            P(both, "mp"),
            P(),
            P(),
            P(both, "mp", None),
        ),
        check_vma=False,
    )
```

```python
import functools
import math

import jax
import jax.numpy as jnp
from jax import lax
from jax.experimental import pallas as pl
from jax.experimental.pallas import tpu as pltpu
from jax.sharding import Mesh
from jax.sharding import PartitionSpec as P

HEAD_DIM = 64
EPSILON = 1e-05
NEGATIVE = -1e30
LANES = 128
ALL = ("chip", "core", "mp")
LINE = ("core", "mp")
CORES = 2

f32 = jnp.float32
bf16 = jnp.bfloat16
i32 = jnp.int32

NT = (((1,), (1,)), ((), ()))
NN = (((1,), (0,)), ((), ()))
TN = (((0,), (0,)), ((), ()))


def dot(a, b, dims=NN):
    return lax.dot_general(a, b, dims, preferred_element_type=f32)


def params(mib=56):
    return pltpu.CompilerParams(vmem_limit_bytes=mib << 20)


def cost(microseconds):
    return pl.CostEstimate(flops=0, bytes_accessed=int(microseconds * 3.2e6), transcendentals=0)


def normed(values):
    centred = values - jnp.mean(values, axis=-1, keepdims=True)
    inverse = lax.rsqrt(jnp.mean(centred * centred, axis=-1, keepdims=True) + EPSILON)
    return centred * inverse, inverse


def norm_back(values, gain, grad):
    hat, inverse = normed(values)
    scaled = grad * gain
    first = jnp.mean(scaled, axis=-1, keepdims=True)
    second = jnp.mean(scaled * hat, axis=-1, keepdims=True)
    back = inverse * (scaled - first - hat * second)
    gain_grad = jnp.sum(grad * hat, axis=0, keepdims=True)
    bias_grad = jnp.sum(grad, axis=0, keepdims=True)
    return back, gain_grad, bias_grad


def in_order(pieces, info_ref):
    for bit, place in ((0, 0), (1, 7), (2, 8)):
        far = info_ref[place] == 1
        turned = []
        for i, piece in enumerate(pieces):
            turned.append(jnp.where(far, pieces[i ^ (1 << bit)], piece))
        pieces = turned
    return pieces


def joined(blocks, info_ref):
    flat = [b.reshape(-1, b.shape[-1]) for b in blocks]
    return flat[0] if len(flat) == 1 else jnp.concatenate(in_order(flat, info_ref), axis=0)


def columns(w_refs, m, info_ref):
    return joined([w[:, pl.ds(m, 1)] for w in w_refs], info_ref)


def whole_weight(w_refs, info_ref):
    parts = [columns(w_refs, m, info_ref) for m in range(w_refs[0].shape[1])]
    return jnp.concatenate(parts, axis=1)


def project(x, w_refs, info_ref, store):
    width = w_refs[0].shape[4]

    def step(m, carry):
        store(pl.multiple_of(m * width, width), dot(x, columns(w_refs, m, info_ref)))
        return carry

    lax.fori_loop(0, w_refs[0].shape[1], step, 0, unroll=True)


def weight_specs(weights, index):
    return [
        pl.BlockSpec(
            (w.shape[0], w.shape[1], 1, w.shape[3], w.shape[4]),
            lambda s, info, skip=skip: (0, 0, index(s) + skip, 0, 0),
        )
        for w, skip in weights
    ]


def call(kernel, info, grid, operands, outs, scratch=(), mib=56, **others):
    arrays, specs, sizes = [], [], []
    for value, spec in operands:
        group = isinstance(value, (list, tuple))
        sizes.append(len(value) if group else None)
        arrays.extend([w for w, _ in value] if group else [value])
        specs.extend(spec if group else [spec])

    def body(info_ref, *refs):
        given, rest, at = [], refs, 0
        for size in sizes:
            given.append(refs[at] if size is None else list(refs[at : at + size]))
            at += 1 if size is None else size
        kernel(info_ref, *given, *rest[at:])

    return pl.pallas_call(
        body,
        out_shape=[o for o, _ in outs],
        grid_spec=pltpu.PrefetchScalarGridSpec(
            num_scalar_prefetch=1,
            grid=grid,
            in_specs=specs,
            out_specs=[o for _, o in outs],
            scratch_shapes=list(scratch),
        ),
        compiler_params=params(mib),
        **others,
    )(info, *arrays)


def full(shape):
    return pl.BlockSpec(shape, lambda *a: (0,) * len(shape))


def gather_kernel(groups, fill, rows_ref, group_ref, *refs):
    tables, out_ref, turned, picked = refs[:groups], refs[groups], refs[-2], refs[-1]
    step = pl.program_id(0)
    feats, width = tables[0].shape
    tokens = picked.shape[0]

    @pl.when(step < fill)
    def _():
        stacked = jnp.concatenate([t[...].astype(f32) for t in tables], axis=0).astype(bf16)
        row = lax.broadcasted_iota(i32, (256, 256), 0)
        eye = jnp.where(row == lax.broadcasted_iota(i32, (256, 256), 1), 1.0, 0.0).astype(bf16)
        for k in range(width // 256):
            at = pl.multiple_of(step * width + k * 256, 256)
            turned[pl.ds(at, 256), :] = dot(eye, stacked[:, k * 256 : (k + 1) * 256], NT)

    @pl.when(step >= fill)
    def _():
        base = (step - fill) * tokens

        def some(k, carry):
            for u in range(16):
                t = k * 16 + u
                picked[pl.ds(t, 1), :] = turned[pl.ds(rows_ref[base + t], 1), :]
            return carry

        lax.fori_loop(0, tokens // 16, some, 0)
        row = lax.broadcasted_iota(i32, (LANES, LANES), 0)
        eye = jnp.where(row == lax.broadcasted_iota(i32, (LANES, LANES), 1), 1.0, 0.0)
        across = dot(eye.astype(bf16), picked[...].astype(bf16), NT)
        own = lax.broadcasted_iota(i32, (LANES, tokens), 0) // feats == group_ref[0]
        kept = jnp.where(own, across, 0.0)
        total = kept[:feats]
        for g in range(1, groups):
            total = total + kept[g * feats : (g + 1) * feats]
        out_ref[0] = total.astype(out_ref.dtype)


def gather_tokens(table, rows, group):
    feats, vocab = table.shape
    groups = LANES // feats
    height = vocab // groups
    n, _, tokens = group.shape
    width = min(2048, height)
    fill = height // width

    def table_spec(g):
        return pl.BlockSpec(
            (feats, width), lambda s, r, g=g: (0, g * fill + jnp.minimum(s, fill - 1))
        )

    return pl.pallas_call(
        functools.partial(gather_kernel, groups, fill),
        out_shape=jax.ShapeDtypeStruct((n, feats, tokens), bf16),
        grid_spec=pltpu.PrefetchScalarGridSpec(
            num_scalar_prefetch=1,
            grid=(fill + n,),
            in_specs=[pl.BlockSpec((1, 1, tokens), lambda s, r: (jnp.maximum(s - fill, 0), 0, 0))]
            + [table_spec(g) for g in range(groups)],
            out_specs=pl.BlockSpec(
                (1, feats, tokens), lambda s, r: (jnp.maximum(s - fill, 0), 0, 0)
            ),
            scratch_shapes=[pltpu.VMEM((height, LANES), f32), pltpu.VMEM((tokens, LANES), f32)],
        ),
        compiler_params=params(),
        cost_estimate=cost(45),
        name="gather_tokens",
    )(rows, group, *([table] * groups))


BATCH = 16
WIDTH = 8192
SENDERS = 8


def scatter_kernel(
    groups, per_core, rows_ref, row_ref, group_ref, grad_ref, out_ref, pos_ref, acc, update, turned, sem
):
    step = pl.program_id(0)
    senders, feats, tokens = grad_ref.shape
    height = acc.shape[0]
    width = turned.shape[2]

    @pl.when(step == 0)
    def _():
        def clear(k, carry):
            acc[pl.ds(pl.multiple_of(k * 256, 256), 256), :] = jnp.zeros((256, LANES), f32)
            return carry

        lax.fori_loop(0, height // 256, clear, 0)
        pos_ref[...] = jnp.zeros_like(pos_ref)

    row = lax.broadcasted_iota(i32, (LANES, LANES), 0)
    col = lax.broadcasted_iota(i32, (LANES, LANES), 1)
    near = row // BATCH == col // BATCH

    def sender(d, carry):
        place = step * senders + d
        grads = grad_ref[d].astype(f32)
        core = lax.rem(lax.div(place, per_core), CORES)
        pos_ref[core] += grads
        tall = jnp.concatenate([grads] * groups, axis=0)
        own = lax.broadcasted_iota(i32, (LANES, tokens), 0) // feats == group_ref[d]
        tall = jnp.where(own, tall, 0.0).astype(bf16)
        for b in range(tokens // LANES):
            at = slice(b * LANES, (b + 1) * LANES)
            along = jnp.broadcast_to(row_ref[d][:, at].astype(f32), (LANES, LANES))
            same = jnp.where((along == along.T) & near, 1.0, 0.0).astype(bf16)
            update[at, :] = dot(same, tall[:, at], NT)
        base = place * tokens

        def some(k, carry):
            where = [rows_ref[base + k * BATCH + u] for u in range(BATCH)]
            fresh = [
                acc[pl.ds(where[u], 1), :] + update[pl.ds(k * BATCH + u, 1), :]
                for u in range(BATCH)
            ]
            for u in range(BATCH):
                acc[pl.ds(where[u], 1), :] = fresh[u]
            return carry

        lax.fori_loop(0, tokens // BATCH, some, 0, unroll=True)
        return carry

    lax.fori_loop(0, senders, sender, 0)

    @pl.when(step == pl.num_programs(0) - 1)
    def _():
        def copy(i, slot, g):
            at = pl.multiple_of(g * height + i * width, width)
            return pltpu.make_async_copy(
                turned.at[slot, pl.ds(g * feats, feats)],
                out_ref.at[:, pl.ds(at, width)],
                sem.at[slot, g],
            )

        def turn(i, carry):
            slot = lax.rem(i, 2)

            @pl.when(i >= 2)
            def _():
                for g in range(groups):
                    copy(i - 2, slot, g).wait()

            at = pl.multiple_of(i * width, width)
            turned[slot] = (acc[pl.ds(at, width), :] * 32.0).T
            for g in range(groups):
                copy(i, slot, g).start()
            return carry

        count = height // width
        lax.fori_loop(0, count, turn, 0)
        for i in range(max(count - 2, 0), count):
            for g in range(groups):
                copy(i, i % 2, g).wait()


def scatter_tokens(grads, rows, row, group, vocab, per_core):
    n, feats, tokens = grads.shape
    groups = LANES // feats
    height = vocab // groups
    width = min(WIDTH, height)
    senders = math.gcd(n, SENDERS)
    token_spec = pl.BlockSpec((senders, 1, tokens), lambda s, r: (s, 0, 0))
    return pl.pallas_call(
        functools.partial(scatter_kernel, groups, per_core),
        out_shape=(
            jax.ShapeDtypeStruct((feats, vocab), f32),
            jax.ShapeDtypeStruct((CORES, feats, tokens), f32),
        ),
        grid_spec=pltpu.PrefetchScalarGridSpec(
            num_scalar_prefetch=1,
            grid=(n // senders,),
            in_specs=[
                token_spec,
                token_spec,
                pl.BlockSpec((senders, feats, tokens), lambda s, r: (s, 0, 0)),
            ],
            out_specs=(
                pl.BlockSpec(memory_space=pl.ANY),
                full((CORES, feats, tokens)),
            ),
            scratch_shapes=[
                pltpu.VMEM((height, LANES), f32),
                pltpu.VMEM((tokens, LANES), f32),
                pltpu.VMEM((2, LANES, width), f32),
                pltpu.SemaphoreType.DMA((2, groups)),
            ],
        ),
        compiler_params=params(),
        cost_estimate=cost(39),
        name="scatter_tokens",
    )(rows, row, group, grads)


def entry_kernel(
    info_ref, emb_ref, pos_a, pos_b, wq_ref, wkv_ref, gain_ref, bias_ref, x0_ref, x1_ref, a_ref, q_ref, kv_ref
):
    step = pl.program_id(0)
    half = x0_ref.shape[0] // 2

    @pl.when(step == 0)
    def _():
        for i, pos in enumerate((pos_a, pos_b)):
            at = slice(i * half, (i + 1) * half)
            places = joined([p[...] for p in pos], info_ref)
            x0 = (emb_ref[:, at].astype(f32) * 32.0 + places.astype(f32)).T
            x1 = normed(x0)[0] * gain_ref[0:1] + bias_ref[0:1]
            a = normed(x1)[0] * gain_ref[1:2] + bias_ref[1:2]
            x0_ref[at] = x0
            x1_ref[at] = x1
            a_ref[at] = a.astype(bf16)

    x = a_ref[...]
    span = wq_ref[0].shape[4]

    @pl.when(step == 0)
    def _():
        def store(at, y):
            q_ref[0, :, pl.ds(at, span)] = (y * HEAD_DIM**-0.5).astype(bf16)

        project(x, wq_ref, info_ref, store)

    @pl.when(step > 0)
    def _():
        def store(at, y):
            kv_ref[0, :, pl.ds(at, span)] = y.astype(bf16)

        project(x, wkv_ref, info_ref, store)


def entry(info, emb, first, gains, biases):
    width, tokens = emb.shape
    wq, wkv = first

    def pos_specs(i):
        return [
            pl.BlockSpec(
                (w.shape[0], 1, 1, w.shape[3], w.shape[4]),
                lambda s, info, skip=skip: (0, info[3 + i], skip, 0, 0),
            )
            for w, skip in wq
        ]

    row = full((tokens, width))
    rows = jax.ShapeDtypeStruct((tokens, width), f32)
    return call(
        entry_kernel,
        info,
        (3,),
        [
            (emb, full(emb.shape)),
            (wq, pos_specs(0)),
            (wq, pos_specs(1)),
            (wq, weight_specs(wq, lambda s: 1)),
            (wkv, weight_specs(wkv, lambda s: jnp.maximum(s - 1, 0))),
            (gains, full(gains.shape)),
            (biases, full(biases.shape)),
        ],
        [
            (rows, row),
            (rows, row),
            (jax.ShapeDtypeStruct((tokens, width), bf16), row),
            (jax.ShapeDtypeStruct((1, tokens, width), bf16), full((1, tokens, width))),
            (
                jax.ShapeDtypeStruct((2, tokens, width), bf16),
                pl.BlockSpec((1, tokens, width), lambda s, info: (jnp.maximum(s - 1, 0), 0, 0)),
            ),
        ],
        cost_estimate=cost(15),
        name="entry",
    )


def slots(pair, info_ref):
    odd = info_ref[9] == 1
    one, two = pair[0][...], pair[1][...]
    return jnp.where(odd, two, one), jnp.where(odd, one, two)


def put_slots(pair, info_ref, values):
    for odd in range(2):

        @pl.when(info_ref[9] == odd)
        def _():
            pair[odd][...] = values[0].astype(bf16)
            pair[1 - odd][...] = values[1].astype(bf16)


def source_kernel(info_ref, came_a, came_b, w_refs, x_ref, kv_ref):
    @pl.when(pl.program_id(0) == 0)
    def _():
        half = came_a.shape[0]
        x_ref[:half], x_ref[half:] = slots((came_a, came_b), info_ref)

    def store(at, y):
        kv_ref[0, :, pl.ds(at, w_refs[0].shape[4])] = y.astype(bf16)

    project(x_ref[...], w_refs, info_ref, store)


def source_keys(info, came, weights):
    half, width = came[0].shape
    tokens = 2 * half
    return call(
        source_kernel,
        info,
        (2,),
        [
            (came[0], full((half, width))),
            (came[1], full((half, width))),
            (weights, weight_specs(weights, lambda s: s)),
        ],
        [
            (jax.ShapeDtypeStruct((tokens, width), bf16), full((tokens, width))),
            (
                jax.ShapeDtypeStruct((2, tokens, width), bf16),
                pl.BlockSpec((1, tokens, width), lambda s, info: (s, 0, 0)),
            ),
        ],
        cost_estimate=cost(8),
        name="source_keys",
    )


def attend_kernel(causal, info_ref, q_ref, own_ref, par_ref, o_ref, p_ref, hide):
    tokens = q_ref.shape[1]
    half = tokens // 2
    core = info_ref[0]

    @pl.when(pl.program_id(0) == 0)
    def _():
        length = info_ref[1] if causal else info_ref[2]
        key = lax.broadcasted_iota(i32, (tokens, tokens), 0)
        query = lax.broadcasted_iota(i32, (tokens, tokens), 1)
        upper = key >= half
        own = key + jnp.where(upper, info_ref[4] - 1, info_ref[3]) * half
        par = key + jnp.where(upper, info_ref[6] - 1, info_ref[5]) * half
        at = query + jnp.where(query >= half, info_ref[4] - 1, info_ref[3]) * half
        for i, place in enumerate((own, par)):
            seen = place < length
            if causal:
                seen = seen & (place <= at)
            hide[i] = jnp.where(seen, 0.0, NEGATIVE)

    outs = []
    for h in range(LANES // HEAD_DIM):
        lanes = slice(h * HEAD_DIM, (h + 1) * HEAD_DIM)
        q = q_ref[0][:, lanes]
        s_own = dot(own_ref[0][:, lanes], q, NT) + hide[0]
        s_par = dot(par_ref[0][:, lanes], q, NT) + hide[1]
        top = jnp.maximum(
            jnp.max(s_own, axis=0, keepdims=True), jnp.max(s_par, axis=0, keepdims=True)
        )
        e_own = jnp.exp(s_own - top)
        e_par = jnp.exp(s_par - top)
        total = jnp.sum(e_own, axis=0, keepdims=True) + jnp.sum(e_par, axis=0, keepdims=True)
        scale = 1.0 / total
        p_own = (e_own * scale).astype(bf16)
        p_par = (e_par * scale).astype(bf16)
        p_ref[h, 0] = p_own
        p_ref[h, 1] = p_par
        outs.append(dot(own_ref[1][:, lanes], p_own, TN) + dot(par_ref[1][:, lanes], p_par, TN))
    o_ref[0] = jnp.concatenate(outs, axis=0).T.astype(bf16)


def attend(info, q, own, par, causal):
    _, tokens, width = q.shape
    heads = width // HEAD_DIM
    pair = LANES // HEAD_DIM
    one = pl.BlockSpec((1, tokens, LANES), lambda s, info: (0, 0, s))
    two = pl.BlockSpec((2, tokens, LANES), lambda s, info: (0, 0, s))
    return pl.pallas_call(
        functools.partial(attend_kernel, causal),
        out_shape=(
            jax.ShapeDtypeStruct((1, tokens, width), bf16),
            jax.ShapeDtypeStruct((heads, 2, tokens, tokens), bf16),
        ),
        grid_spec=pltpu.PrefetchScalarGridSpec(
            num_scalar_prefetch=1,
            grid=(heads // pair,),
            in_specs=[one, two, two],
            out_specs=(
                one,
                pl.BlockSpec((pair, 2, tokens, tokens), lambda s, info: (s, 0, 0, 0)),
            ),
            scratch_shapes=[pltpu.VMEM((2, tokens, tokens), f32)],
        ),
        compiler_params=params(),
        cost_estimate=cost(22),
        name="attend",
    )(info, q, own, par)


def middle_kernel(info_ref, o_ref, w_ref, x_ref, wq_ref, gain_ref, bias_ref, x2_ref, c_ref, q_ref):
    x2 = x_ref[...] + dot(o_ref[0], whole_weight(w_ref, info_ref), NT)
    x2_ref[...] = x2
    c = (normed(x2)[0] * gain_ref[2:3] + bias_ref[2:3]).astype(bf16)
    c_ref[...] = c

    def store(at, y):
        q_ref[0, :, pl.ds(at, wq_ref[0].shape[4])] = (y * HEAD_DIM**-0.5).astype(bf16)

    project(c, wq_ref, info_ref, store)


def middle(info, o, weights, x1, gains, biases):
    _, tokens, width = o.shape
    row = full((tokens, width))
    return call(
        middle_kernel,
        info,
        (1,),
        [
            (o, full(o.shape)),
            (weights, weight_specs(weights, lambda s: 0)),
            (x1, row),
            (weights, weight_specs(weights, lambda s: 1)),
            (gains, full(gains.shape)),
            (biases, full(biases.shape)),
        ],
        [
            (jax.ShapeDtypeStruct((tokens, width), f32), row),
            (jax.ShapeDtypeStruct((tokens, width), bf16), row),
            (jax.ShapeDtypeStruct((1, tokens, width), bf16), full((1, tokens, width))),
        ],
        cost_estimate=cost(9),
        name="middle",
    )


def feed_kernel(
    info_ref,
    o_ref,
    wo_ref,
    x_ref,
    w1_ref,
    w2_ref,
    gain_ref,
    bias_ref,
    x3_ref,
    f_ref,
    g_ref,
    slope_ref,
    x4_ref,
):
    step = pl.program_id(0)

    @pl.when(step == 0)
    def _():
        x3 = x_ref[...] + dot(o_ref[0], whole_weight(wo_ref, info_ref), NT)
        x3_ref[...] = x3
        f_ref[...] = (normed(x3)[0] * gain_ref[3:4] + bias_ref[3:4]).astype(bf16)
        x4_ref[...] = x3

    def store(at, u):
        bell = 0.5 + 0.5 * lax.erf(u * 0.7071067811865476)
        lanes = pl.ds(at, w1_ref[0].shape[4])
        g_ref[0, :, lanes] = (u * bell).astype(bf16)
        slope = bell + u * (0.3989422804014327 * jnp.exp(-0.5 * u * u))
        slope_ref[0, :, lanes] = slope.astype(bf16)

    project(f_ref[...], w1_ref, info_ref, store)
    x4_ref[...] += dot(g_ref[0], whole_weight(w2_ref, info_ref), NT)


def feed(info, o, wo, x2, w1, w2, gains, biases, slabs):
    _, tokens, width = o.shape
    blocks = slabs
    row = full((tokens, width))
    part = pl.BlockSpec((1, tokens, width), lambda s, info: (s, 0, 0))
    wide = jax.ShapeDtypeStruct((tokens, width), f32)
    slim = jax.ShapeDtypeStruct((tokens, width), bf16)
    many = jax.ShapeDtypeStruct((blocks, tokens, width), bf16)
    return call(
        feed_kernel,
        info,
        (blocks,),
        [
            (o, full(o.shape)),
            (wo, weight_specs(wo, lambda s: 2)),
            (x2, row),
            (w1, weight_specs(w1, lambda s: s)),
            (w2, weight_specs(w2, lambda s: s)),
            (gains, full(gains.shape)),
            (biases, full(biases.shape)),
        ],
        [(wide, row), (slim, row), (many, part), (many, part), (wide, row)],
        mib=60,
        cost_estimate=cost(28),
        name="feed",
    )


def feed_back_kernel(
    info_ref,
    x4_ref,
    og_a,
    og_b,
    slope_ref,
    w1_ref,
    w2_ref,
    x3_ref,
    wo_ref,
    gain_ref,
    bias_ref,
    hid_a,
    hid_b,
    g4b_ref,
    du_ref,
    g3_ref,
    g3b_ref,
    do_ref,
    sums_ref,
    total,
):
    step = pl.program_id(0)

    @pl.when(step == 0)
    def _():
        x4 = x4_ref[...]
        half = og_a.shape[0]
        hidden = normed(x4)[0] * gain_ref[4:5] + bias_ref[4:5]
        put_slots((hid_a, hid_b), info_ref, (hidden[:half], hidden[half:]))
        out_grad = jnp.concatenate(slots((og_a, og_b), info_ref), axis=0).astype(f32)
        g4, gain_grad, bias_grad = norm_back(x4, gain_ref[4:5], out_grad)
        g3_ref[...] = g4
        g4b_ref[...] = g4.astype(bf16)
        sums_ref[2:3] = gain_grad
        sums_ref[3:4] = bias_grad

    def store(at, y):
        lanes = pl.ds(at, w2_ref[0].shape[4])
        du_ref[0, :, lanes] = (y * slope_ref[0, :, lanes].astype(f32)).astype(bf16)

    project(g4b_ref[...], w2_ref, info_ref, store)
    part = dot(du_ref[0], whole_weight(w1_ref, info_ref), NT)

    @pl.when(step == 0)
    def _():
        total[...] = part

    @pl.when(step > 0)
    def _():
        total[...] += part

    @pl.when(step == pl.num_programs(0) - 1)
    def _():
        back, gain_grad, bias_grad = norm_back(x3_ref[...], gain_ref[3:4], total[...])
        g3 = g3_ref[...] + back
        g3_ref[...] = g3
        g3b = g3.astype(bf16)
        g3b_ref[...] = g3b
        sums_ref[0:1] = gain_grad
        sums_ref[1:2] = bias_grad

        def keep(at, y):
            do_ref[0, :, pl.ds(at, wo_ref[0].shape[4])] = y.astype(bf16)

        project(g3b, wo_ref, info_ref, keep)


def feed_back(info, x4, og, slope, wo, x3, w1, w2, gains, biases):
    blocks, tokens, width = slope.shape
    row = full((tokens, width))
    part_row = full((tokens // 2, width))
    part_shape = jax.ShapeDtypeStruct((tokens // 2, width), bf16)
    part = pl.BlockSpec((1, tokens, width), lambda s, info: (s, 0, 0))
    wide = jax.ShapeDtypeStruct((tokens, width), f32)
    slim = jax.ShapeDtypeStruct((tokens, width), bf16)
    return call(
        feed_back_kernel,
        info,
        (blocks,),
        [
            (x4, row),
            (og[0], part_row),
            (og[1], part_row),
            (slope, part),
            (w1, weight_specs(w1, lambda s: s)),
            (w2, weight_specs(w2, lambda s: s)),
            (x3, row),
            (wo, weight_specs(wo, lambda s: 2)),
            (gains, full(gains.shape)),
            (biases, full(biases.shape)),
        ],
        [
            (part_shape, part_row),
            (part_shape, part_row),
            (slim, row),
            (jax.ShapeDtypeStruct((blocks, tokens, width), bf16), part),
            (wide, row),
            (slim, row),
            (jax.ShapeDtypeStruct((1, tokens, width), bf16), full((1, tokens, width))),
            (jax.ShapeDtypeStruct((4, width), f32), full((4, width))),
        ],
        [pltpu.VMEM((tokens, width), f32)],
        60,
        cost_estimate=cost(28),
        name="feed_back",
    )


def attend_back_kernel(
    q_ref, own_ref, par_ref, p_ref, o_ref, do_ref, dq_ref, down_ref, dpar_ref
):
    flat = do_ref[0].astype(f32).T * o_ref[0].astype(f32).T
    outs = []
    for h in range(LANES // HEAD_DIM):
        lanes = slice(h * HEAD_DIM, (h + 1) * HEAD_DIM)
        q = q_ref[0][:, lanes]
        grad = do_ref[0][:, lanes]
        inner = jnp.sum(flat[lanes], axis=0, keepdims=True)
        back = None
        for i, (kv_ref, d_ref) in enumerate(((own_ref, down_ref), (par_ref, dpar_ref))):
            keys = kv_ref[0][:, lanes]
            probs = p_ref[h, i]
            d_probs = dot(kv_ref[1][:, lanes], grad, NT)
            d_scores = (probs.astype(f32) * (d_probs - inner)).astype(bf16)
            d_ref[1, :, lanes] = dot(probs, grad).astype(bf16)
            d_ref[0, :, lanes] = dot(d_scores, q).astype(bf16)
            some = dot(keys, d_scores, TN)
            back = some if back is None else back + some
        outs.append(back)
    dq_ref[0] = (jnp.concatenate(outs, axis=0).T * HEAD_DIM**-0.5).astype(bf16)


def attend_back(q, own, par, probs, o, do):
    _, tokens, width = q.shape
    heads = width // HEAD_DIM
    pair = LANES // HEAD_DIM
    one = pl.BlockSpec((1, tokens, LANES), lambda s: (0, 0, s))
    two = pl.BlockSpec((2, tokens, LANES), lambda s: (0, 0, s))
    kv = jax.ShapeDtypeStruct((2, tokens, width), bf16)
    return pl.pallas_call(
        attend_back_kernel,
        out_shape=(jax.ShapeDtypeStruct((1, tokens, width), bf16), kv, kv),
        grid=(heads // pair,),
        in_specs=[
            one,
            two,
            two,
            pl.BlockSpec((pair, 2, tokens, tokens), lambda s: (s, 0, 0, 0)),
            one,
            one,
        ],
        out_specs=(one, two, two),
        compiler_params=params(),
        cost_estimate=cost(21),
        name="attend_back",
    )(q, own, par, probs, o, do)


def causal_back_kernel(
    info_ref, q_ref, own_ref, par_ref, p_ref, o_ref, do_ref, dq_ref, down_ref, dpar_ref, back
):
    tokens = q_ref.shape[1]
    half = tokens // 2
    low, high, every = slice(0, half), slice(half, tokens), slice(0, tokens)
    flat = do_ref[0].astype(f32).T * o_ref[0].astype(f32).T
    inner = [
        jnp.sum(flat[h * HEAD_DIM : (h + 1) * HEAD_DIM], axis=0, keepdims=True)
        for h in range(LANES // HEAD_DIM)
    ]
    back[...] = jnp.zeros_like(back)

    def segments(i, kv_ref, d_ref, spans):
        for h in range(LANES // HEAD_DIM):
            lanes = slice(h * HEAD_DIM, (h + 1) * HEAD_DIM)
            for keys, queries in spans:
                grad = do_ref[0, queries, lanes]
                probs = p_ref[h, i, keys, queries]
                d_probs = dot(kv_ref[1, keys, lanes], grad, NT)
                d_scores = (probs.astype(f32) * (d_probs - inner[h][:, queries])).astype(bf16)
                d_ref[1, keys, lanes] = dot(probs, grad).astype(bf16)
                d_ref[0, keys, lanes] = dot(d_scores, q_ref[0, queries, lanes]).astype(bf16)
                back[lanes, queries] += dot(kv_ref[0, keys, lanes], d_scores, TN)

    segments(0, own_ref, down_ref, [(low, every), (high, high)])

    @pl.when(info_ref[0] == 0)
    def _():
        segments(1, par_ref, dpar_ref, [(every, high)])

    @pl.when(info_ref[0] == 1)
    def _():
        segments(1, par_ref, dpar_ref, [(low, every)])
        dpar_ref[:, high, :] = jnp.zeros((2, half, LANES), bf16)

    dq_ref[0] = (back[...].T * HEAD_DIM**-0.5).astype(bf16)


def causal_back(info, q, own, par, probs, o, do):
    _, tokens, width = q.shape
    heads = width // HEAD_DIM
    pair = LANES // HEAD_DIM
    one = pl.BlockSpec((1, tokens, LANES), lambda s, info: (0, 0, s))
    two = pl.BlockSpec((2, tokens, LANES), lambda s, info: (0, 0, s))
    kv = jax.ShapeDtypeStruct((2, tokens, width), bf16)
    return call(
        causal_back_kernel,
        info,
        (heads // pair,),
        [
            (q, one),
            (own, two),
            (par, two),
            (probs, pl.BlockSpec((pair, 2, tokens, tokens), lambda s, info: (s, 0, 0, 0))),
            (o, one),
            (do, one),
        ],
        [(jax.ShapeDtypeStruct((1, tokens, width), bf16), one), (kv, two), (kv, two)],
        [pltpu.VMEM((LANES, tokens), f32)],
        cost_estimate=cost(19),
        name="causal_back",
    )


def middle_back_kernel(
    info_ref, dq_ref, wq_ref, x2_ref, g3_ref, wo_ref, gain_ref, g2_ref, g2b_ref, do_ref, sums_ref
):
    d_normed = dot(dq_ref[0], whole_weight(wq_ref, info_ref), NT)
    back, gain_grad, bias_grad = norm_back(x2_ref[...], gain_ref[2:3], d_normed)
    g2 = g3_ref[...] + back
    g2_ref[...] = g2
    g2b = g2.astype(bf16)
    g2b_ref[...] = g2b
    sums_ref[0:1] = gain_grad
    sums_ref[1:2] = bias_grad

    def keep(at, y):
        do_ref[0, :, pl.ds(at, wo_ref[0].shape[4])] = y.astype(bf16)

    project(g2b, wo_ref, info_ref, keep)


def middle_back(info, dq, weights, x2, g3, gains):
    _, tokens, width = dq.shape
    row = full((tokens, width))
    return call(
        middle_back_kernel,
        info,
        (1,),
        [
            (dq, full(dq.shape)),
            (weights, weight_specs(weights, lambda s: 1)),
            (x2, row),
            (g3, row),
            (weights, weight_specs(weights, lambda s: 0)),
            (gains, full(gains.shape)),
        ],
        [
            (jax.ShapeDtypeStruct((tokens, width), f32), row),
            (jax.ShapeDtypeStruct((tokens, width), bf16), row),
            (jax.ShapeDtypeStruct((1, tokens, width), bf16), full((1, tokens, width))),
            (jax.ShapeDtypeStruct((2, width), f32), full((2, width))),
        ],
        cost_estimate=cost(10),
        name="middle_back",
    )


def source_back_kernel(info_ref, mine_ref, came_ref, w_ref, out_a, out_b, sum_ref, total):
    step = pl.program_id(0)
    grads = (mine_ref[0].astype(f32) + came_ref[0].astype(f32)).astype(bf16)
    sum_ref[0] = grads
    part = dot(grads, whole_weight(w_ref, info_ref), NT)

    @pl.when(step == 0)
    def _():
        total[...] = part

    @pl.when(step == pl.num_programs(0) - 1)
    def _():
        half = out_a.shape[0]
        both = total[...] + part
        put_slots((out_a, out_b), info_ref, (both[:half], both[half:]))


def source_back(info, mine, came, weights):
    parts, tokens, width = mine.shape
    part = pl.BlockSpec((1, tokens, width), lambda s, info: (s, 0, 0))
    return call(
        source_back_kernel,
        info,
        (parts,),
        [(mine, part), (came, part), (weights, weight_specs(weights, lambda s: s))],
        [
            (jax.ShapeDtypeStruct((tokens // 2, width), bf16), full((tokens // 2, width))),
            (jax.ShapeDtypeStruct((tokens // 2, width), bf16), full((tokens // 2, width))),
            (jax.ShapeDtypeStruct((parts, tokens, width), bf16), part),
        ],
        [pltpu.VMEM((tokens, width), f32)],
        cost_estimate=cost(7),
        name="source_back",
    )


def exit_kernel(
    info_ref,
    dq_ref,
    mine_ref,
    came_ref,
    wq_ref,
    wkv_ref,
    x1_ref,
    x0_ref,
    g2_ref,
    gain_ref,
    g0_ref,
    sum_ref,
    sums_ref,
    total,
):
    step = pl.program_id(0)

    @pl.when(step == 0)
    def _():
        total[...] = dot(dq_ref[0], whole_weight(wq_ref, info_ref), NT)

    @pl.when(step > 0)
    def _():
        grads = (mine_ref[0].astype(f32) + came_ref[0].astype(f32)).astype(bf16)
        sum_ref[0] = grads
        total[...] += dot(grads, whole_weight(wkv_ref, info_ref), NT)

    @pl.when(step == pl.num_programs(0) - 1)
    def _():
        back, gain_one, bias_one = norm_back(x1_ref[...], gain_ref[1:2], total[...])
        g1 = g2_ref[...] + back
        g0, gain_zero, bias_zero = norm_back(x0_ref[...], gain_ref[0:1], g1)
        g0_ref[...] = g0.T.astype(bf16)
        sums_ref[0:1] = gain_zero
        sums_ref[1:2] = bias_zero
        sums_ref[2:3] = gain_one
        sums_ref[3:4] = bias_one


def exit_back(info, dq, mine, came, first, x1, x0, g2, gains):
    _, tokens, width = dq.shape
    wq, wkv = first
    row = full((tokens, width))
    part = pl.BlockSpec((1, tokens, width), lambda s, info: (jnp.maximum(s - 1, 0), 0, 0))
    return call(
        exit_kernel,
        info,
        (3,),
        [
            (dq, full(dq.shape)),
            (mine, part),
            (came, part),
            (wq, weight_specs(wq, lambda s: 1)),
            (wkv, weight_specs(wkv, lambda s: jnp.maximum(s - 1, 0))),
            (x1, row),
            (x0, row),
            (g2, row),
            (gains, full(gains.shape)),
        ],
        [
            (jax.ShapeDtypeStruct((width, tokens), bf16), full((width, tokens))),
            (jax.ShapeDtypeStruct((2, tokens, width), bf16), part),
            (jax.ShapeDtypeStruct((4, width), f32), full((4, width))),
        ],
        [pltpu.VMEM((tokens, width), f32)],
        cost_estimate=cost(15),
        name="exit_back",
    )


def weight_grad_kernel(chips, aliased, info_ref, xo_ref, xp_ref, yo_ref, yp_ref, *refs):
    out_ref, turned = refs[-2], refs[-1]
    tokens, width = xo_ref.shape
    rows = width // (chips * CORES)
    core = info_ref[0]

    @pl.when(pl.program_id(0) == 0)
    def _():
        for i, x_ref in enumerate((xo_ref, xp_ref)):
            at = slice(i * tokens, (i + 1) * tokens)
            if rows % LANES == 0:
                for j in range(chips):
                    lanes = pl.ds(pl.multiple_of((2 * j + core) * rows, rows), rows)
                    turned[j * rows : (j + 1) * rows, at] = x_ref[:, lanes].astype(f32).T.astype(bf16)
            else:
                tall = x_ref[...].astype(f32).T.reshape(chips, CORES, rows, tokens)
                mine = jnp.where(core == 0, tall[:, 0], tall[:, 1])
                turned[:, at] = mine.reshape(chips * rows, tokens).astype(bf16)

    y_own, y_par = yo_ref[0], yp_ref[0]
    blocks, span = out_ref.shape[1], out_ref.shape[4]
    result = dot(turned[:, :tokens], y_own) + dot(turned[:, tokens:], y_par)
    for m in range(blocks):
        part = result[:, m * span : (m + 1) * span].astype(bf16)
        out_ref[:, m, 0] = part.reshape(chips, rows, span)


def weight_grad(info, x_own, x_par, y_own, y_par, shape, at, before=None):
    parts, tokens, width = y_own.shape
    chips = shape[0]
    row = full(x_own.shape)
    part = pl.BlockSpec((1, tokens, width), lambda s, info: (s, 0, 0))
    extra = [] if before is None else [before]
    return pl.pallas_call(
        functools.partial(weight_grad_kernel, chips, before is not None),
        out_shape=jax.ShapeDtypeStruct(shape, bf16),
        grid_spec=pltpu.PrefetchScalarGridSpec(
            num_scalar_prefetch=1,
            grid=(parts,),
            in_specs=[row, row, part, part] + [pl.BlockSpec(memory_space=pl.ANY) for _ in extra],
            out_specs=pl.BlockSpec(
                (chips, shape[1], 1, shape[3], shape[4]), lambda s, info: (0, 0, s + at, 0, 0)
            ),
            scratch_shapes=[pltpu.VMEM((x_own.shape[1] // 2, 2 * tokens), bf16)],
        ),
        input_output_aliases={} if before is None else {5: 0},
        compiler_params=params(30),
        cost_estimate=cost(3 + 2 * parts),
        name="weight_grad",
    )(info, x_own, x_par, y_own, y_par, *extra)


def swap(value):
    return lax.ppermute(value, "core", [(0, 1), (1, 0)])


def line_moves(mp):
    rounds = []
    for turn in range(2):
        moves = []
        for c in range(CORES):
            for m in range(mp):
                target, slot = (1 if m in (1, 2) else 0), m // 2
                moves.append((c * mp + m, target * mp + 2 * c + (slot ^ turn)))
        rounds.append(moves)
    return rounds


def to_chips(value, mp):
    slot = lax.axis_index("mp") // 2
    return [
        lax.ppermute(jnp.where((slot ^ turn) == 0, value[0], value[1]), LINE, moves)
        for turn, moves in enumerate(line_moves(mp))
    ]


def from_chips(pair, mp):
    return [
        lax.ppermute(sent, LINE, [(b, a) for a, b in moves])
        for sent, moves in zip(pair, line_moves(mp))
    ]


def placed_again(came):
    slot = lax.axis_index("mp") // 2
    one, two = [c.astype(f32) for c in came]
    return jnp.stack([jnp.where(slot == 0, one, two), jnp.where(slot == 0, two, one)])


def packed(*weights):
    return jnp.concatenate([w.reshape(-1, w.shape[-1]) for w in weights], axis=0)


X_SWAP = [(0, 1), (1, 0), (2, 3), (3, 2)]
Y_SWAP = [(0, 2), (2, 0), (1, 3), (3, 1)]
def gathered(rows, unit, chips, mp):
    value = lax.all_gather(rows, ALL, axis=0, tiled=False)
    return value.reshape(chips * CORES, mp, -1, unit, rows.shape[-1])


def gathered_line(rows, unit, mp):
    value = lax.all_gather(rows, "mp", axis=0, tiled=False)
    return value.reshape(mp, -1, unit, rows.shape[-1])


class Spread:
    def __init__(self, value, cut):
        self.own, self.cut = [value], cut
        self.near, self.far, self.both = [], [], []
        self.swapped = {}

    def begin(self, *others):
        self.own = tied(self.own, *others)
        sets = [self.own[0][:, : self.cut], self.own[0][:, self.cut :]]
        self.near = [lax.ppermute(w, "chip", p) for w, p in zip(sets, (X_SWAP, Y_SWAP))]
        self.far = [lax.ppermute(w, "chip", p) for w, p in zip(sets, (Y_SWAP, X_SWAP))]

    def finish(self, *others):
        self.near = tied(self.near, *others)
        self.both = [lax.ppermute(w, "chip", p) for w, p in zip(self.near, (Y_SWAP, X_SWAP))]

    def swap(self, *names):
        for name in names:
            self.swapped[name] = [swap(w) for w in getattr(self, name)]

    def hold(self, *others):
        state = [self.own, self.near, self.far, self.both, self.swapped]
        state, others = lax.optimization_barrier((state, others))
        self.own, self.near, self.far, self.both, self.swapped = state
        return others if len(others) > 1 else others[0]

    def pieces(self):
        found = []
        for i in range(2):
            pieces = []
            for name in ("own", "near", "far", "both") if i == 0 else ("own", "far", "near", "both"):
                at, skip = (0, i * self.cut) if name == "own" else (i, 0)
                for group in (getattr(self, name), self.swapped[name]):
                    pieces.append((group[at][None], skip))
            found.append(pieces)
        return found


def tied(value, *others):
    return after(value, *others) if others else value


def scattered(grads, axis):
    return lax.psum_scatter(grads, axis, scatter_dimension=0, tiled=False)


def sent_over(grads, axis, size):
    me = lax.axis_index(axis)
    terms = []
    for k in range(size):
        if axis == "chip" and size == 4:
            to, perm = me ^ k, [(i, i ^ k) for i in range(size)]
        else:
            to, perm = (me + k) % size, [(i, (i + k) % size) for i in range(size)]
        part = lax.dynamic_index_in_dim(grads, to, axis=0, keepdims=False)
        terms.append(part if k == 0 else lax.ppermute(part, axis, perm))
    return terms


def summed(terms):
    return sum([t.astype(f32) for t in terms[1:]], start=terms[0].astype(f32))


def total_over(value, axis, size):
    terms = [
        lax.ppermute(value, axis, [(i, (i + k) % size) for i in range(size)])
        for k in range(1, size)
    ]
    return sum(terms, start=value)


def after(value, *others):
    return lax.optimization_barrier((value, others))[0]


def body(
    chips,
    mp,
    target_ids,
    tgt_lengths,
    encoder_states,
    src_lengths,
    table,
    pos_table,
    self_query_key_value_weight,
    self_output_weight,
    cross_query_weight,
    cross_key_value_weight,
    cross_output_weight,
    feedforward_input_weight,
    feedforward_output_weight,
    norm_gains,
    norm_biases,
    out_grad,
):
    dp = chips * CORES
    n = dp * mp
    seqs, block = target_ids.shape
    assert seqs * CORES == mp == 4
    tokens = seqs * block
    width = norm_gains.shape[1]
    vocab = table.shape[1]
    feats = table.shape[0]
    rows = pos_table.shape[0]
    core, m, chip = lax.axis_index("core"), lax.axis_index("mp"), lax.axis_index("chip")

    def split(weight):
        return weight.reshape(rows, -1, block).transpose(1, 0, 2)

    own_ids = jnp.broadcast_to(target_ids.reshape(1, tokens), (n, tokens))
    all_ids = lax.all_to_all(own_ids, ALL, split_axis=0, concat_axis=0, tiled=True)
    sub = feedforward_input_weight.shape[1] // block
    first = packed(pos_table, split(self_query_key_value_weight))
    second = packed(
        self_output_weight, cross_query_weight, split(cross_key_value_weight), cross_output_weight
    )
    third = packed(split(feedforward_input_weight), split(feedforward_output_weight))
    sub = feedforward_input_weight.shape[1] // block
    second = gathered(second, rows, chips, mp)
    third = gathered(third, rows, chips, mp)
    second = [(second, 0)], [(second, 2)]
    third = [(third, 0)], [(third, sub)]
    stepped = chips == 4
    if stepped:
        copies = jnp.broadcast_to(first[None], (mp,) + first.shape)
        copies = lax.all_to_all(after(copies, all_ids), "mp", split_axis=0, concat_axis=0, tiled=True)
        first = Spread(copies.reshape(mp, -1, rows, block), 2)
    else:
        first = gathered(first, rows, chips, mp)
        first = [(first, 0)], [(first, 2)]

    lengths = jnp.stack([tgt_lengths, src_lengths])
    other = swap(lengths)
    lengths = jnp.where(
        core == 0,
        jnp.concatenate([lengths, other], axis=1),
        jnp.concatenate([other, lengths], axis=1),
    )
    lengths = lax.dynamic_index_in_dim(lengths, m, axis=1, keepdims=False)
    info = jnp.stack(
        [
            core,
            lengths[0],
            lengths[1],
            core,
            3 - core,
            1 - core,
            2 + core,
            chip % 2,
            chip // 2,
            m % 2,
        ]
    ).astype(i32)

    ids = all_ids.reshape(chips, CORES, mp, seqs, block)
    ids = jnp.stack([ids[:, :, 0], ids[:, :, 3], ids[:, :, 1], ids[:, :, 2]], axis=2)
    ids = ids.reshape(chips, CORES, CORES, 2, seqs, block).transpose(0, 2, 1, 4, 3, 5)
    ids = ids.reshape(n, 1, tokens)
    height = vocab // (LANES // feats)
    row, group = ids % height, ids // height
    flat_row = row.reshape(-1)

    picked = gather_tokens(table, flat_row, group)
    if stepped:
        picked = first.hold(picked)
        first.begin(picked)
        first.finish()
        first.swap("own", "near", "far", "both")
        first = first.pieces()
    emb = lax.all_to_all(picked, ALL, split_axis=0, concat_axis=0, tiled=True)
    emb = emb.reshape(width, tokens)

    x0, x1, a, q, kv = entry(info, emb, first, norm_gains, norm_biases)
    states = to_chips(after(encoder_states, a), mp)
    kv_par = swap(kv)
    outs = attend(info, q, kv, kv_par, True)
    (o, probs), states = lax.optimization_barrier((outs, states))
    states, ckv = source_keys(info, states, second[1])
    ckv_par = swap(ckv)
    x2, c, cq = middle(info, after(o, ckv), second[0], x1, norm_gains, norm_biases)
    oc, cprobs = attend(info, cq, ckv, ckv_par, False)
    og = to_chips(after(out_grad.astype(bf16), oc), mp)
    w1, w2 = third
    oc_par, c_par = swap(oc), swap(after(c, oc))
    outs = feed(info, oc, second[1], x2, w1, w2, norm_gains, norm_biases, sub)
    (x3, f, g, slope, x4), og, oc_par, c_par = lax.optimization_barrier((outs, og, oc_par, c_par))
    f_par, g_par = swap(f), swap(g)
    a_par, o_par, states_par = [swap(after(v, x4)) for v in (a, o, states)]
    outs = feed_back(info, x4, og, slope, second[1], x3, w1, w2, norm_gains, norm_biases)
    outs, f_par, g_par, a_par, o_par, states_par = lax.optimization_barrier(
        (outs, f_par, g_par, a_par, o_par, states_par)
    )
    *hid, g4b, du, g3, g3b, doc, sums34 = outs
    g4b_par, g3b_par, du_par = swap(g4b), swap(g3b), swap(du)
    hidden_out = from_chips(tied(hid, g4b_par), mp)
    shape = (chips, mp, sub, rows, block)
    grads = weight_grad(info, g4b, g4b_par, g, g_par, shape, 0)
    part_one = scattered(grads, "chip")
    shape = (chips, mp, sub + 1, rows, block)
    grads = weight_grad(info, after(g3b, grads), g3b_par, oc, oc_par, shape, sub)
    grads = weight_grad(info, after(f, grads), f_par, du, du_par, shape, 0, grads)
    doc, hidden_out = lax.optimization_barrier((after(doc, grads), hidden_out))

    outs = attend_back(cq, ckv, ckv_par, cprobs, oc, doc)
    (dcq, dckv_own, dckv_par), part_one = lax.optimization_barrier((outs, part_one))
    part_two = scattered(after(grads, part_one), "chip")
    dckv_came, dcq_par = swap(dckv_par), swap(dcq)
    outs = middle_back(info, dcq, second[0], x2, g3, norm_gains)
    (g2, g2b, do, sums2), dckv_came, dcq_par, dckv_own = lax.optimization_barrier(
        (outs, dckv_came, dcq_par, dckv_own)
    )
    g2b_par = swap(g2b)
    outs = source_back(info, dckv_own, dckv_came, second[1])
    *enc_grad, dckv = outs
    dckv_after = swap(dckv)
    shape = (chips, mp, 3, rows, block)
    grads = weight_grad(info, c, c_par, after(dcq, dckv), dcq_par, shape, 0)
    self_shape = (chips, mp, 4, rows, block)
    held = weight_grad(info, after(g2b, grads), g2b_par, o, o_par, self_shape, 3)
    grads = weight_grad(info, after(states, held), states_par, dckv, dckv_after, shape, 1, grads)
    do = after(do, grads)
    cross_grads = grads
    encoder_grad = from_chips(tied(enc_grad, grads), mp)

    outs = causal_back(info, q, kv, kv_par, probs, o, do)
    (dq, dkv_own, dkv_par), encoder_grad, part_two = lax.optimization_barrier(
        (outs, encoder_grad, part_two)
    )
    cross_part = scattered(after(cross_grads, part_two), "chip")
    dkv_came = swap(dkv_par)
    dq_par = swap(dq)
    outs = exit_back(info, dq, dkv_own, dkv_came, first, x1, x0, g2, norm_gains)
    (g0, dkv, sums01), dq_par = lax.optimization_barrier((outs, dq_par))
    sent = g0.reshape(n, feats, tokens)
    arrived = lax.all_to_all(sent, ALL, split_axis=0, concat_axis=0, tiled=True)
    sums = jnp.concatenate((sums01, sums2, sums34), axis=0)
    sums_par = swap(sums)
    dkv_after = swap(dkv)
    grads = weight_grad(info, a, a_par, dq, dq_par, self_shape, 0, held)
    grads, sums_par = lax.optimization_barrier((grads, sums_par))
    sums = total_over(sums + sums_par, "chip", chips)
    grads = weight_grad(info, a, a_par, dkv, dkv_after, self_shape, 1, grads)
    sums, grads, arrived, cross_part = lax.optimization_barrier((sums, grads, arrived, cross_part))
    sums_up = scattered(jnp.concatenate([part_one, part_two, cross_part], axis=1), "mp")
    self_terms = lax.all_to_all(grads, "chip", split_axis=0, concat_axis=0, tiled=True)
    sums = total_over(sums, "mp", mp)

    outs = scatter_tokens(arrived, flat_row, row, group, vocab, mp)
    (table_grad, places), self_terms, sums = lax.optimization_barrier((outs, self_terms, sums))
    hidden_out = placed_again(tied(hidden_out, places))
    encoder_grad = placed_again(tied(encoder_grad, places))
    self_part = jnp.sum(self_terms.astype(f32), axis=0).astype(bf16)
    self_grads = summed(sent_over(self_part, "mp", mp))
    sums_up = sums_up.astype(f32)
    feed_out_grads, feed_in_grads, cross_grads = (
        sums_up[:sub],
        sums_up[sub : 2 * sub + 1],
        sums_up[2 * sub + 1 :],
    )

    blocks = places.reshape(CORES, feats, 2, block).transpose(0, 2, 1, 3).reshape(4, feats, block)
    blocks = jnp.stack([blocks[0], blocks[2], blocks[3], blocks[1]])
    parts = []
    for k in range(mp):
        mine = lax.dynamic_index_in_dim(blocks, (m + k) % mp, axis=0, keepdims=False)
        parts.append(
            mine if k == 0 else lax.ppermute(mine, "mp", [(i, (i + k) % mp) for i in range(mp)])
        )
    pos_grad = []
    for source in range(mp):
        value = parts[0]
        for k in range(1, mp):
            value = jnp.where((m - source) % mp == k, parts[k], value)
        pos_grad.append(value)
    pos_grad = jnp.concatenate(pos_grad, axis=0)

    def join(parts):
        return parts.transpose(1, 0, 2)

    return (
        hidden_out,
        table_grad,
        pos_grad,
        join(self_grads[:3]),
        self_grads[3],
        cross_grads[0],
        join(cross_grads[1:3]),
        feed_in_grads[sub],
        join(feed_in_grads[:sub]).reshape(rows, -1),
        join(feed_out_grads).reshape(rows, -1),
        sums[0::2],
        sums[1::2],
        encoder_grad,
    )


def solution(mesh):
    dp, mp = mesh.devices.shape
    chips = dp // CORES
    fine = Mesh(mesh.devices.reshape(chips, CORES, mp), ALL)
    both = ("chip", "core")
    placed = (
        P(both, "mp"),
        P(both),
        P(both, "mp", None),
        P(both),
        P(ALL, None),
        P(both, "mp"),
        P(both, None, "mp"),
        P(both, "mp"),
        P(both, "mp"),
        P(both, None, "mp"),
        P(both, "mp"),
        P(both, "mp"),
        P(both, "mp"),
        P(),
        P(),
        P(both, "mp", None),
    )
    return jax.shard_map(
        functools.partial(body, chips, mp),
        mesh=fine,
        in_specs=placed,
        out_specs=(
            P(both, "mp", None),
            P(ALL, None),
            P(both, "mp"),
            P(both, None, "mp"),
            P(both, "mp"),
            P(both, "mp"),
            P(both, None, "mp"),
            P(both, "mp"),
            P(both, "mp"),
            P(both, "mp"),
            P(),
            P(),
            P(both, "mp", None),
        ),
        check_vma=False,
    )
```
